32 devices in a mesh: groups: 2 (over y), gx: 4 (over z), gy: 2 (over x), gz: 2 (over core).
Axes of the slice: x: 2, y: 2, z: 4, core: 2. Of those that a mesh axis runs over, the one named last changes fastest.
Arguments:
- earlier_warmth_field: float32 [16, 512, 512], P(('groups', 'gz'), 'gy', 'gx'), parts along dimension 0, may hold values from -6 to 6
- caloric_storage: float32 [16, 512, 512], P(('groups', 'gz'), 'gy', 'gx'), parts along dimension 0, may hold values from 0.5 to 4
- thermal_diffusivity_coefficient: float32 [16, 512, 512], P(('groups', 'gz'), 'gy', 'gx'), parts along dimension 0, may hold values from 0.3 to 3
- dissipation_catalog: float32 [16, 64, 128], P('groups'), parts along dimension 0, may hold values from 0.1 to 3
- dissipation_selector: int32 [16, 8, 4], P(('groups', 'gz'), 'gy', 'gx'), parts along dimension 0, may hold values from 0 to 7
- refine_depth: int32 [16, 8, 4], P(('groups', 'gz'), 'gy', 'gx'), parts along dimension 0, may hold values from 1 to 4, as said below
- border_band_width: int32 [16, 4], P(('groups', 'gy'), 'gx'), parts along dimension 0, may hold values from 1 to 16
- microflow_flag: int32 [16], P(('groups', 'gz')), parts along dimension 0, may hold values 0 or 1
Outputs:
- warmth_solution: float32 [16, 512, 512], P(('groups', 'gz'), 'gy', 'gx'), parts along dimension 0
- leftover_misfit: float32 [16, 512, 512], P(('groups', 'gz'), 'gy', 'gx'), parts along dimension 0
The draws below stay inside these ranges and needn't reach their ends.
There are 2 independent parts, one for each index of `groups`. The reference program is written for one: setup_inputs(seed, part) draws one part's arguments, and reference() takes and returns one part's arrays. A program takes and returns all parts, laid end to end along the dimension named above; each array names one. Nothing has to cross between parts.
Inputs may be any that keep to these rules, and one draw needn't show every extreme that they name: `refine_depth`: each tile's level is 1, 2 or 4.
All inputs are finite; a program needn't handle non-finite values. No bound on the sum of `microflow_flag` on one device may be relied on, other than what follows from the above.
Results may differ from the reference program's by a relative error of at most 0.00022.
Values sent between devices are 32-bit elements; how exact they have to be, the bound alone decides.
No kernel may reach another device: no remote copies, remote signals or barrier semaphores. Data moves between devices by JAX's collectives and lax.ppermute only.
A program may use at most 64 MiB of HBM per device.

```python
import math
import jax
import jax.numpy as jnp

CX = 128
TY = 64
NPOW = 8
ITERS = 2
XSPAN = 512
YSPAN = 512
ZLAYERS = 8
NTY = 8
NTX = 4


def draw_refine_depth(key, part):
    scores = jax.random.randint(jax.random.fold_in(key, 17), (ZLAYERS, NTY, NTX), 0, 10)
    return jnp.where(scores < 6, 1, jnp.where(scores < 9, 2, 4)).astype(jnp.int32)


def place_ends(result, own_key, least, largest):
    extent = result.shape
    spot = [jax.random.randint(jax.random.fold_in(own_key, axis), (), 0, extent[axis]) for axis in range(len(extent))]
    result = result.at[tuple(spot)].set(least)
    longest = extent.index(max(extent))
    spot[longest] = (spot[longest] + 1) % extent[longest]
    return result.at[tuple(spot)].set(largest)


def shard_levels(own_key, extent, shards, least, top_value):
    factor_of = 1.0
    for position, shards_of in shards:
        heights = jax.random.uniform(jax.random.fold_in(jax.random.fold_in(own_key, 6), position), (shards_of,), jnp.float32, least / len(shards), top_value / len(shards))
        factor_of = factor_of * jnp.repeat(jnp.exp(heights), extent[position] // shards_of).reshape((-1,) + (1,) * (len(extent) - 1 - position))
    return factor_of


def bell_draw(own_key, shape, width, most, shards=(), kind=jnp.bfloat16):
    values = jax.random.normal(own_key, shape, jnp.float32) * width
    if len(shards) > 0:
        values = shard_levels(own_key, shape, shards, -0.22, 0.18) * values
    return jnp.clip(values, min=-most, max=most).astype(kind)


def setup_inputs(seed: int = 0, part: int = 0) -> dict:
    streams_of = jax.random.split(jax.random.key(seed), 9)
    part_splits = jax.random.split(jax.random.fold_in(streams_of[8], part), 9)
    return {
        "earlier_warmth_field": bell_draw(part_splits[0], (ZLAYERS, YSPAN, XSPAN), 1.0, 6.0, ((0, 2), (1, 2), (2, 4)), jnp.float32),
        "caloric_storage": jnp.clip(jnp.exp(math.log(4.0) - 2.0794415 * jax.random.uniform(part_splits[1], (ZLAYERS, YSPAN, XSPAN), jnp.float32) ** shard_levels(part_splits[1], (ZLAYERS, YSPAN, XSPAN), ((0, 2), (1, 2), (2, 4)), -0.2, 0.2)), 0.5, 4.0),
        "thermal_diffusivity_coefficient": jnp.clip(jnp.exp(math.log(3.0) - 2.3025851 * jax.random.uniform(part_splits[2], (ZLAYERS, YSPAN, XSPAN), jnp.float32) ** shard_levels(part_splits[2], (ZLAYERS, YSPAN, XSPAN), ((0, 2), (1, 2), (2, 4)), -0.2, 0.2)), 0.3, 3.0),
        "dissipation_catalog": jnp.clip(jnp.exp(jax.random.uniform(part_splits[3], (NPOW, TY, CX), jnp.float32, math.log(0.1), math.log(3.0))), 0.1, 3.0),
        "dissipation_selector": place_ends(jax.random.randint(part_splits[4], (ZLAYERS, NTY, NTX), 0, NPOW), jax.random.fold_in(part_splits[4], 1), 0, NPOW - 1).astype(jnp.int32),
        "refine_depth": draw_refine_depth(jax.random.fold_in(jax.random.fold_in(streams_of[8], part), 71), part),
        "border_band_width": place_ends(jax.random.randint(part_splits[6], (NTY, NTX), 1, TY // 4 + 1), jax.random.fold_in(part_splits[6], 1), 1, (TY // 4 + 1) - 1).astype(jnp.int32),
        "microflow_flag": place_ends((jax.random.randint(part_splits[7], (ZLAYERS,), 0, 2) < 1).astype(jnp.int32), jax.random.fold_in(part_splits[7], 1), 0, 1),
    }


interval_increment = 0.5
vertical_ratio = 2.0
coolant_film = 1.5
band_sink = 1.0
damping = 0.8


def harmonic(first, second):
    return 2.0 * first * second / (first + second)


def neighbours(padded):
    return (padded[:-2, 1:-1, 1:-1], padded[2:, 1:-1, 1:-1], padded[1:-1, :-2, 1:-1],
            padded[1:-1, 2:, 1:-1], padded[1:-1, 1:-1, :-2], padded[1:-1, 1:-1, 2:])


def reference(earlier_warmth_field, caloric_storage, thermal_diffusivity_coefficient, dissipation_catalog, dissipation_selector, refine_depth, border_band_width, microflow_flag):
    near = neighbours(jnp.pad(thermal_diffusivity_coefficient, 1))
    faces = [harmonic(thermal_diffusivity_coefficient, other) for other in near]
    faces[0] = vertical_ratio * faces[0]
    faces[1] = vertical_ratio * faces[1]
    edge_cells = jnp.repeat(jnp.repeat(border_band_width, TY, axis=0), CX, axis=1)
    row_tile = (jnp.arange(YSPAN, dtype=jnp.int32) % TY)[:, None]
    band = ((row_tile < edge_cells) | (row_tile >= TY - edge_cells)).astype(jnp.float32)
    sink = coolant_film * microflow_flag.astype(jnp.float32)[:, None, None] + band_sink * band[None]
    diagonal = caloric_storage / interval_increment + sink
    for face in faces:
        diagonal = diagonal + face
    column_patch = jnp.arange(XSPAN, dtype=jnp.int32) % CX
    tile_faces = (faces[2] * (row_tile != 0).astype(jnp.float32), faces[3] * (row_tile != TY - 1).astype(jnp.float32),
                  faces[4] * (column_patch != 0).astype(jnp.float32), faces[5] * (column_patch != CX - 1).astype(jnp.float32))
    level_cells = jnp.repeat(jnp.repeat(refine_depth, TY, axis=1), CX, axis=2)
    tiles = dissipation_catalog[dissipation_selector]
    dissipation_density = jnp.transpose(tiles, (0, 1, 3, 2, 4)).reshape(ZLAYERS, YSPAN, XSPAN)
    linear_source_term = caloric_storage / interval_increment * earlier_warmth_field + dissipation_density

    def linear_map_action(field):
        total = diagonal * field
        for face, other in zip(faces, neighbours(jnp.pad(field, 1))):
            total = total - face * other
        return total

    def smooth(vector):
        state = damping * vector / diagonal
        for sweep in range(1, 4):
            padded = jnp.pad(state, ((0, 0), (1, 1), (1, 1)))
            inner = tile_faces[0] * padded[:, :-2, 1:-1] + tile_faces[1] * padded[:, 2:, 1:-1]
            inner = inner + tile_faces[2] * padded[:, 1:-1, :-2] + tile_faces[3] * padded[:, 1:-1, 2:]
            fresh = (1.0 - damping) * state + damping * (vector + inner) / diagonal
            state = jnp.where(level_cells > sweep, fresh, state)
        return state

    warmth_solution = earlier_warmth_field
    leftover_misfit = linear_source_term - linear_map_action(warmth_solution)
    smoothed = smooth(leftover_misfit)
    applied = linear_map_action(smoothed)
    for turn in range(ITERS):
        gamma_now = jnp.sum(leftover_misfit * smoothed)
        delta_now = jnp.sum(applied * smoothed)
        pre = smooth(applied)
        twice = linear_map_action(pre)
        if turn == 0:
            present_stride_amount = gamma_now / delta_now
            image_dir, smooth_dir, operator_times_direction, conjugate_update_heading = twice, pre, applied, smoothed
        else:
            current_mixing_factor = gamma_now / gamma_prev
            present_stride_amount = gamma_now / (delta_now - current_mixing_factor * gamma_now / alpha_prev)
            image_dir = twice + current_mixing_factor * image_dir
            smooth_dir = pre + current_mixing_factor * smooth_dir
            operator_times_direction = applied + current_mixing_factor * operator_times_direction
            conjugate_update_heading = smoothed + current_mixing_factor * conjugate_update_heading
        warmth_solution = warmth_solution + present_stride_amount * conjugate_update_heading
        leftover_misfit = leftover_misfit - present_stride_amount * operator_times_direction
        smoothed = smoothed - present_stride_amount * smooth_dir
        applied = applied - present_stride_amount * image_dir
        gamma_prev, alpha_prev = gamma_now, present_stride_amount
    return warmth_solution, leftover_misfit
```

```python
import functools
import math

import jax
import jax.numpy as jnp
from jax import lax
from jax.experimental import pallas as pl
from jax.experimental.pallas import tpu as pltpu
from jax.sharding import PartitionSpec as P

interval_increment = 0.5
vertical_ratio = 2.0
coolant_film = 1.5
band_sink = 1.0
damping = 0.8
GRID_AXES = ("gx", "gy", "gz")
VMEM = pl.BlockSpec(memory_space=pltpu.VMEM)
SMEM = pl.BlockSpec(memory_space=pltpu.SMEM)
F32 = jnp.float32


def harmonic(first, second):
    return 2.0 * first * second / (first + second)


def lanes(shape=(8, 128)):
    return lax.broadcasted_iota(jnp.int32, shape, len(shape) - 1)


def rows(shape):
    return lax.broadcasted_iota(jnp.int32, shape, 0)


def odd(axis):
    return lax.rem(lax.axis_index(axis), 2) == 1


def pack_columns(load, count):
    lane = lanes()
    firsts, lasts = [], []
    for start in range(0, count, 128):
        parts = [jnp.zeros((8, 128), F32), jnp.zeros((8, 128), F32)]
        for i in range(min(128, count - start)):
            turned = load(start + i)
            if i:
                turned = pltpu.roll(turned, i, 1)
            here = (lane == i) | (lane == (i + 127) % 128)
            parts[i % 2] = jnp.where(here, turned, parts[i % 2])
        even = lane % 2 == 0
        firsts.append(jnp.where(even, parts[0], parts[1]))
        lasts.append(pltpu.roll(jnp.where(even, parts[1], parts[0]), 1, 1))
    return jnp.concatenate(firsts, 0), jnp.concatenate(lasts, 0)


def stage_columns(pair_ref, slot, first, last):
    for g in range(first.shape[0] // 8):
        f = first[8 * g : 8 * g + 8]
        l = pltpu.roll(last[8 * g : 8 * g + 8], 127, 1)
        even = lanes() % 2 == 0
        pair_ref[slot, 0, g] = jnp.where(even, f, l)
        pair_ref[slot, 1, g] = jnp.where(even, l, f)


def spread_columns(pair_ref, slot, base, count):
    lane = lanes()
    edge = (lane == 0) | (lane == 127)
    out = []
    for j in range(count):
        i = base + j
        group = lax.div(i, 128)
        turned = pltpu.roll(pair_ref[slot, j % 2, group], lax.rem(128 * (group + 1) - i, 128), 1)
        out.append(jnp.where(edge, turned, 0.0))
    return jnp.concatenate(out, 0)


def both_sides(axis, halo_refs, index=()):
    if len(halo_refs) == 1:
        got = halo_refs[0][index] if index else halo_refs[0][...]
        return got, got
    a, b = (ref[index] if index else ref[...] for ref in halo_refs)
    flag = odd(axis)
    return jnp.where(flag, a, b), jnp.where(flag, b, a)


def present(axis):
    here = lax.axis_index(axis)
    low = jnp.where(here > 0, 1.0, 0.0).astype(F32)
    high = jnp.where(here < lax.axis_size(axis) - 1, 1.0, 0.0).astype(F32)
    return low, high


def fill_sends(field_ref, send_refs, slot, columns):
    z, y, _ = field_ref.shape
    sx, sy, sz = send_refs
    put = (slot,) if slot is not None else ()
    for axis, refs in zip(GRID_AXES, (sx, sy, sz)):
        flag = odd(axis)
        for n, ref in enumerate(refs):
            high_first = flag if n else ~flag
            if axis == "gx":
                ref[put + (slice(None), slice(None))] = jnp.where(high_first, columns[1], columns[0])
            elif axis == "gy":
                low = field_ref[:, 0, :]
                high = field_ref[:, y - 1, :]
                ref[put + (slice(None), slice(None))] = jnp.where(high_first, high, low)
            else:
                ref[put + (slice(None), slice(None))] = field_ref[jnp.where(high_first, z - 1, 0)]


def regroup(refs, counts):
    out, at = [], 0
    for c in counts:
        out.append(refs[at : at + c])
        at += c
    return out, refs[at:]


def vreg(ref, i):
    per = ref.shape[1] // 8
    return ref[i // per, 8 * (i % per) : 8 * (i % per) + 8, :]


def first_kernel(rounds, x_ref, k_ref, *refs):
    sends, (own_ref,) = regroup(refs, rounds)
    count = x_ref.shape[0] * x_ref.shape[1] // 8
    for slot, ref in enumerate((x_ref, k_ref)):
        columns = pack_columns(functools.partial(vreg, ref), count)
        own_ref[slot, 0] = columns[0]
        own_ref[slot, 1] = columns[1]
        fill_sends(ref, sends, slot, columns)


def sweep_tile(value, weight, north, south, east, level):
    tall = value.shape[0]
    row = rows(value.shape)
    north = jnp.where(row == 0, 0.0, north)
    south = jnp.where(row == tall - 1, 0.0, south)
    start = weight * value

    def once(_, state):
        inner = north * pltpu.roll(state, 1, 0) + south * pltpu.roll(state, tall - 1, 0)
        inner = inner + east * pltpu.roll(state, 127, 1) + pltpu.roll(east * state, 1, 1)
        return (1.0 - damping) * state + (start + weight * inner)

    return lax.fori_loop(1, jnp.minimum(level, 4), once, start)


def tile_loop(z_count, t_count, body, carry):
    def step(i, carry):
        return body(lax.div(i, t_count), lax.rem(i, t_count), carry)

    return lax.fori_loop(0, z_count * t_count, step, carry)


def second_kernel(rounds, tall, *refs):
    (x_ref, c_ref, k_ref, cat_ref, own_ref, sel_ref, lev_ref, band_ref, flow_ref), refs = refs[:9], refs[9:]
    (hx, hy, hz), refs = regroup(refs, rounds)
    (r_ref, u_ref, cz_ref, cn_ref, ce_ref, diag_ref, wt_ref, cx_ref), refs = refs[:8], refs[8:]
    sends, (kp, xp, pairs) = regroup(refs, rounds)
    z, y, _ = x_ref.shape
    tiles = y // tall
    per = tall // 8

    row8 = rows((8, 128))
    for slot, (src, dst) in enumerate(((x_ref, xp), (k_ref, kp))):
        dst[1 : z + 1, 8 : 8 + y, :] = src[...]
        ylo, yhi = both_sides("gy", hy, (slot,))
        zlo, zhi = both_sides("gz", hz, (slot,))
        if slot:
            has = present("gy")
            ylo, yhi = ylo * has[0], yhi * has[1]
            has = present("gz")
            zlo, zhi = zlo * has[0], zhi * has[1]
        dst[0, 8 : 8 + y, :] = zlo
        dst[z + 1, 8 : 8 + y, :] = zhi
        for i in range(z):
            dst[i + 1, 0:8, :] = jnp.broadcast_to(ylo[i : i + 1], (8, 128))
            dst[i + 1, 8 + y : 16 + y, :] = jnp.broadcast_to(yhi[i : i + 1], (8, 128))
    xlo, xhi = both_sides("gx", hx, (0,))
    klo, khi = both_sides("gx", hx, (1,))
    has = present("gx")
    west = harmonic(own_ref[1, 0], klo * has[0])
    east = harmonic(own_ref[1, 1], khi * has[1])
    cx_ref[0] = west
    cx_ref[1] = east
    stage_columns(pairs, 0, west, east)
    stage_columns(pairs, 1, west * (xlo - own_ref[0, 0]), east * (xhi - own_ref[0, 1]))

    lane = lanes((tall, 128))
    row = rows((tall, 128))

    def faces(i, t, carry):
        at = pl.multiple_of(t * tall, 8)
        here = kp[i + 1, pl.ds(at + 8, tall), :]
        cn_ref[i, pl.ds(at, tall), :] = harmonic(here, kp[i + 1, pl.ds(at + 7, tall), :])
        ce_ref[i, pl.ds(at, tall), :] = jnp.where(lane == 127, 0.0, harmonic(here, pltpu.roll(here, 127, 1)))
        cz_ref[i, pl.ds(at, tall), :] = vertical_ratio * harmonic(here, kp[i, pl.ds(at + 8, tall), :])

        @pl.when(i == z - 1)
        def _():
            cz_ref[z, pl.ds(at, tall), :] = vertical_ratio * harmonic(here, kp[z + 1, pl.ds(at + 8, tall), :])

        return carry

    tile_loop(z, tiles, faces, 0)
    for i in range(z):
        last = kp[i + 1, y + 7 : y + 8, :]
        face = harmonic(last, kp[i + 1, y + 8 : y + 9, :])
        cn_ref[i, y : y + 8, :] = jnp.where(row8 == 0, face, 0.0)

    def body(i, t, carry):
        at = pl.multiple_of(t * tall, 8)
        near = pl.ds(at, tall)
        x = xp[i + 1, pl.ds(at + 8, tall), :]
        width = band_ref[t, 0]
        band = jnp.where((row < width) | (row >= tall - width), band_sink, 0.0)
        sink = coolant_film * flow_ref[i].astype(F32) + band
        cn = cn_ref[i, near, :]
        cs = cn_ref[i, pl.ds(at + 1, tall), :]
        ce = ce_ref[i, near, :]
        cw = pltpu.roll(ce, 1, 1)
        cd = cz_ref[i, near, :]
        cu = cz_ref[i + 1, near, :]
        base = i * (y // 8) + t * per
        diag = c_ref[i, near, :] / interval_increment + sink
        diag = diag + cd + cu + cn + cs + ce + cw + spread_columns(pairs, 0, base, per)
        power = cat_ref[sel_ref[i, t, 0]]
        r = power - sink * x + spread_columns(pairs, 1, base, per)
        r = r + cn * (xp[i + 1, pl.ds(at + 7, tall), :] - x) + cs * (xp[i + 1, pl.ds(at + 9, tall), :] - x)
        r = r + ce * (pltpu.roll(x, 127, 1) - x) + cw * (pltpu.roll(x, 1, 1) - x)
        r = r + cd * (xp[i, pl.ds(at + 8, tall), :] - x) + cu * (xp[i + 2, pl.ds(at + 8, tall), :] - x)
        weight = damping / diag
        diag_ref[i, near, :] = diag
        wt_ref[i, near, :] = weight
        r_ref[i, near, :] = r
        u_ref[i, near, :] = sweep_tile(r, weight, cn, cs, ce, lev_ref[i, t, 0])
        return carry

    tile_loop(z, tiles, body, 0)
    fill_sends(u_ref, sends, None, pack_columns(functools.partial(vreg, u_ref), z * y // 8))


def pad_field(src, dst, pairs, cx_ref, halos):
    z, y, _ = src.shape
    hx, hy, hz = halos
    dst[1 : z + 1, 8 : 8 + y, :] = src[...]
    ylo, yhi = both_sides("gy", hy)
    zlo, zhi = both_sides("gz", hz)
    dst[0, 8 : 8 + y, :] = zlo
    dst[z + 1, 8 : 8 + y, :] = zhi
    for i in range(z):
        dst[i + 1, 0:8, :] = jnp.broadcast_to(ylo[i : i + 1], (8, 128))
        dst[i + 1, 8 + y : 16 + y, :] = jnp.broadcast_to(yhi[i : i + 1], (8, 128))
    xlo, xhi = both_sides("gx", hx)
    stage_columns(pairs, 0, cx_ref[0] * xlo, cx_ref[1] * xhi)


def apply_tile(i, t, tall, y, vp, pairs, cz_ref, cn_ref, ce_ref, diag_ref):
    at = pl.multiple_of(t * tall, 8)
    near = pl.ds(at, tall)
    v = vp[i + 1, pl.ds(at + 8, tall), :]
    cn = cn_ref[i, near, :]
    cs = cn_ref[i, pl.ds(at + 1, tall), :]
    ce = ce_ref[i, near, :]
    total = cn * vp[i + 1, pl.ds(at + 7, tall), :] + cs * vp[i + 1, pl.ds(at + 9, tall), :]
    total = total + ce * pltpu.roll(v, 127, 1) + pltpu.roll(ce * v, 1, 1)
    total = total + cz_ref[i, near, :] * vp[i, pl.ds(at + 8, tall), :]
    total = total + cz_ref[i + 1, near, :] * vp[i + 2, pl.ds(at + 8, tall), :]
    total = total + spread_columns(pairs, 0, i * (y // 8) + t * (tall // 8), tall // 8)
    return near, v, diag_ref[i, near, :] * v - total, cn, cs, ce


def fold(product):
    return jnp.sum(product.reshape(-1, 8, 128), axis=0)


def third_kernel(rounds, tall, *refs):
    (u_ref, r_ref, cz_ref, cn_ref, ce_ref, diag_ref, wt_ref, cx_ref, lev_ref), refs = refs[:9], refs[9:]
    halos, refs = regroup(refs, rounds)
    (w_ref, m_ref, sum_ref), refs = refs[:3], refs[3:]
    sends, (up, pairs) = regroup(refs, rounds)
    z, y, _ = u_ref.shape
    pad_field(u_ref, up, pairs, cx_ref, halos)

    def body(i, t, carry):
        near, u, w, cn, cs, ce = apply_tile(i, t, tall, y, up, pairs, cz_ref, cn_ref, ce_ref, diag_ref)
        m = sweep_tile(w, wt_ref[i, near, :], cn, cs, ce, lev_ref[i, t, 0])
        w_ref[i, near, :] = w
        m_ref[i, near, :] = m
        gamma, delta, cross = carry
        return gamma + fold(r_ref[i, near, :] * u), delta + fold(w * u), cross + fold(w * m)

    zero = jnp.zeros((8, 128), F32)
    sums = tile_loop(z, y // tall, body, (zero, zero, zero))
    for n, value in enumerate(sums):
        sum_ref[n] = value
    fill_sends(m_ref, sends, None, pack_columns(functools.partial(vreg, m_ref), z * y // 8))


def fourth_kernel(rounds, tall, *refs):
    (m_ref, sum_ref, cz_ref, cn_ref, ce_ref, diag_ref, cx_ref), refs = refs[:7], refs[7:]
    halos, refs = regroup(refs, rounds)
    n_ref, out_ref, mp, pairs = refs
    z, y, _ = m_ref.shape
    pad_field(m_ref, mp, pairs, cx_ref, halos)

    def body(i, t, carry):
        near, m, n, _, _, _ = apply_tile(i, t, tall, y, mp, pairs, cz_ref, cn_ref, ce_ref, diag_ref)
        n_ref[i, near, :] = n
        return carry + fold(n * m)

    last = tile_loop(z, y // tall, body, jnp.zeros((8, 128), F32))
    parts = [sum_ref[0], sum_ref[1], sum_ref[2], last]
    parts = jnp.concatenate([jnp.sum(p, axis=0, keepdims=True) for p in parts], 0)
    for d in range(out_ref.shape[0]):
        out_ref[d] = parts


def last_kernel(all_ref, x_ref, r_ref, u_ref, w_ref, m_ref, n_ref, xo_ref, ro_ref):
    sums = jnp.sum(all_ref[...], axis=0)
    gamma, delta, cross, last = (sums[i : i + 1] for i in range(4))

    def total(v):
        return jnp.sum(v, axis=1, keepdims=True)

    gamma0 = total(gamma)
    alpha0 = gamma0 / total(delta)
    gamma1 = total(gamma - 2.0 * alpha0 * delta + alpha0 * alpha0 * cross)
    delta1 = total(delta - 2.0 * alpha0 * cross + alpha0 * alpha0 * last)
    beta = gamma1 / gamma0
    alpha1 = gamma1 / (delta1 - beta * gamma1 / alpha0)
    near = alpha0 + alpha1 * (1.0 + beta)
    far = alpha1 * alpha0
    for i in range(x_ref.shape[0]):
        xo_ref[i] = x_ref[i] + near * u_ref[i] - far * m_ref[i]
        ro_ref[i] = r_ref[i] - near * w_ref[i] + far * n_ref[i]


def swap_pairs(axis, start):
    count = lax.axis_size(axis)
    pairs = []
    for i in range(start, count - 1, 2):
        pairs += [(i, i + 1), (i + 1, i)]
    return pairs


def body(
    earlier_warmth_field,
    caloric_storage,
    thermal_diffusivity_coefficient,
    dissipation_catalog,
    dissipation_selector,
    refine_depth,
    border_band_width,
    microflow_flag,
):
    z, y, x = earlier_warmth_field.shape
    tall = dissipation_catalog.shape[1]
    groups = -(-(z * y // 8) // 128)
    rounds = tuple(2 if lax.axis_size(axis) > 2 else 1 for axis in GRID_AXES)
    shape = lambda *s: jax.ShapeDtypeStruct(s, F32)
    full = shape(z, y, x)

    def call(kernel, outs, ins, name, scratch=()):
        specs = [SMEM if v.dtype == jnp.int32 else VMEM for v in ins]
        return pl.pallas_call(
            kernel, out_shape=outs, in_specs=specs, out_specs=[VMEM] * len(outs), scratch_shapes=list(scratch), name=name
        )(*ins)

    def face_shapes(front):
        out = []
        for axis, n in zip(((8 * groups, x), (z, x), (y, x)), rounds):
            out += [shape(*front, *axis)] * n
        return out

    def swap(faces):
        faces, got = list(faces), []
        for axis, n in zip(GRID_AXES, rounds):
            for start in range(n):
                got.append(lax.ppermute(faces.pop(0), axis, swap_pairs(axis, start)))
        return got

    sends = sum(rounds)
    pairs = pltpu.VMEM((2, 2, groups, 8, 128), F32)
    padded = pltpu.VMEM((z + 2, y + 16, x), F32)
    levels = refine_depth

    outs = call(
        functools.partial(first_kernel, rounds),
        face_shapes((2,)) + [shape(2, 2, 8 * groups, x)],
        [earlier_warmth_field, thermal_diffusivity_coefficient],
        "faces",
    )
    own, halos = outs[sends], swap(outs[:sends])
    outs = call(
        functools.partial(second_kernel, rounds, tall),
        [full, full, shape(z + 1, y, x), shape(z, y + 8, x), full, full, full, shape(2, 8 * groups, x)] + face_shapes(()),
        [
            earlier_warmth_field,
            caloric_storage,
            thermal_diffusivity_coefficient,
            dissipation_catalog,
            own,
            dissipation_selector,
            levels,
            border_band_width,
            microflow_flag,
        ]
        + halos,
        "residual",
        [padded, padded, pairs],
    )
    r, u, cz, cn, ce, diag, weight, cx = outs[:8]
    halos = swap(outs[8:])
    outs = call(
        functools.partial(third_kernel, rounds, tall),
        [full, full, shape(3, 8, 128)] + face_shapes(()),
        [u, r, cz, cn, ce, diag, weight, cx, levels] + halos,
        "applied",
        [padded, pairs],
    )
    w, m, sums = outs[:3]
    halos = swap(outs[3:])
    members = math.prod(lax.axis_size(axis) for axis in GRID_AXES)
    n, parts = call(
        functools.partial(fourth_kernel, rounds, tall),
        [full, shape(members, 4, 128)],
        [m, sums, cz, cn, ce, diag, cx] + halos,
        "twice",
        [padded, pairs],
    )
    every = lax.all_to_all(parts, GRID_AXES, 0, 0, tiled=True)
    return tuple(
        call(last_kernel, [full, full], [every, earlier_warmth_field, r, u, w, m, n], "update")
    )


def solution(mesh):
    cells = P(("groups", "gz"), "gy", "gx")
    return jax.shard_map(
        body,
        mesh=mesh,
        in_specs=(
            cells,
            cells,
            cells,
            P("groups", None, None),
            cells,
            cells,
            P(("groups", "gy"), "gx"),
            P(("groups", "gz")),
        ),
        out_specs=(cells, cells),
        check_vma=False,
    )
```

```python
import functools
import math

import jax
import jax.numpy as jnp
from jax import lax
from jax.experimental import pallas as pl
from jax.experimental.pallas import tpu as pltpu
from jax.sharding import PartitionSpec as P

interval_increment = 0.5
vertical_ratio = 2.0
coolant_film = 1.5
band_sink = 1.0
damping = 0.8
GRID_AXES = ("gx", "gy", "gz")
VMEM = pl.BlockSpec(memory_space=pltpu.VMEM)
SMEM = pl.BlockSpec(memory_space=pltpu.SMEM)
F32 = jnp.float32


def harmonic(first, second):
    return 2.0 * first * second / (first + second)


def lanes(shape=(8, 128)):
    return lax.broadcasted_iota(jnp.int32, shape, len(shape) - 1)


def rows(shape):
    return lax.broadcasted_iota(jnp.int32, shape, 0)


def odd(axis):
    return lax.rem(lax.axis_index(axis), 2) == 1


def pack_columns(load, count):
    lane = lanes()
    firsts, lasts = [], []
    for start in range(0, count, 128):
        parts = [jnp.zeros((8, 128), F32), jnp.zeros((8, 128), F32)]
        for i in range(min(128, count - start)):
            turned = load(start + i)
            if i:
                turned = pltpu.roll(turned, i, 1)
            here = (lane == i) | (lane == (i + 127) % 128)
            parts[i % 2] = jnp.where(here, turned, parts[i % 2])
        even = lane % 2 == 0
        firsts.append(jnp.where(even, parts[0], parts[1]))
        lasts.append(pltpu.roll(jnp.where(even, parts[1], parts[0]), 1, 1))
    return jnp.concatenate(firsts, 0), jnp.concatenate(lasts, 0)


def stage_columns(pair_ref, slot, first, last):
    for g in range(first.shape[0] // 8):
        f = first[8 * g : 8 * g + 8]
        l = pltpu.roll(last[8 * g : 8 * g + 8], 127, 1)
        even = lanes() % 2 == 0
        pair_ref[slot, 0, g] = jnp.where(even, f, l)
        pair_ref[slot, 1, g] = jnp.where(even, l, f)


def spread_columns(pair_ref, slot, base, count):
    lane = lanes()
    edge = (lane == 0) | (lane == 127)
    out = []
    for j in range(count):
        i = base + j
        group = lax.div(i, 128)
        turned = pltpu.roll(pair_ref[slot, j % 2, group], lax.rem(128 * (group + 1) - i, 128), 1)
        out.append(jnp.where(edge, turned, 0.0))
    return jnp.concatenate(out, 0)


def both_sides(axis, halo_refs, index=()):
    if len(halo_refs) == 1:
        got = halo_refs[0][index] if index else halo_refs[0][...]
        return got, got
    a, b = (ref[index] if index else ref[...] for ref in halo_refs)
    flag = odd(axis)
    return jnp.where(flag, a, b), jnp.where(flag, b, a)


def present(axis):
    here = lax.axis_index(axis)
    low = jnp.where(here > 0, 1.0, 0.0).astype(F32)
    high = jnp.where(here < lax.axis_size(axis) - 1, 1.0, 0.0).astype(F32)
    return low, high


def fill_sends(field_ref, send_refs, slot, columns):
    z, y, _ = field_ref.shape
    sx, sy, sz = send_refs
    put = (slot,) if slot is not None else ()
    for axis, refs in zip(GRID_AXES, (sx, sy, sz)):
        flag = odd(axis)
        for n, ref in enumerate(refs):
            high_first = flag if n else ~flag
            if axis == "gx":
                ref[put + (slice(None), slice(None))] = jnp.where(high_first, columns[1], columns[0])
            elif axis == "gy":
                low = field_ref[:, 0, :]
                high = field_ref[:, y - 1, :]
                ref[put + (slice(None), slice(None))] = jnp.where(high_first, high, low)
            else:
                ref[put + (slice(None), slice(None))] = field_ref[jnp.where(high_first, z - 1, 0)]


def regroup(refs, counts):
    out, at = [], 0
    for c in counts:
        out.append(refs[at : at + c])
        at += c
    return out, refs[at:]


def vreg(ref, i):
    per = ref.shape[1] // 8
    return ref[i // per, 8 * (i % per) : 8 * (i % per) + 8, :]


def first_kernel(rounds, *refs):
    sources, fields, refs = refs[:4], refs[4:8], refs[8:]
    sends, (own_ref, sems) = regroup(refs, rounds)
    copies = [pltpu.make_async_copy(a, b, sems.at[n]) for n, (a, b) in enumerate(zip(sources, fields))]
    for copy in copies:
        copy.start()
    z, y, _ = fields[0].shape
    for slot, ref in enumerate(fields[:2]):
        copies[slot].wait()
        columns = pack_columns(functools.partial(vreg, ref), z * y // 8)
        own_ref[slot, 0] = columns[0]
        own_ref[slot, 1] = columns[1]
        fill_sends(ref, sends, slot, columns)
    for copy in copies[2:]:
        copy.wait()


def sweep_tile(value, weight, north, south, east, level):
    tall = value.shape[0]
    row = rows(value.shape)
    north = jnp.where(row == 0, 0.0, north)
    south = jnp.where(row == tall - 1, 0.0, south)
    start = weight * value

    def once(_, state):
        inner = north * pltpu.roll(state, 1, 0) + south * pltpu.roll(state, tall - 1, 0)
        inner = inner + east * pltpu.roll(state, 127, 1) + pltpu.roll(east * state, 1, 1)
        return (1.0 - damping) * state + (start + weight * inner)

    return lax.fori_loop(1, jnp.minimum(level, 4), once, start)


def tile_loop(z_count, t_count, body, carry):
    def step(i, carry):
        return body(lax.div(i, t_count), lax.rem(i, t_count), carry)

    return lax.fori_loop(0, z_count * t_count, step, carry)


def second_kernel(rounds, tall, *refs):
    (x_ref, c_ref, k_ref, cat_ref, own_ref, sel_ref, lev_ref, band_ref, flow_ref), refs = refs[:9], refs[9:]
    (hx, hy, hz), refs = regroup(refs, rounds)
    (r_ref, u_ref, cz_ref, cn_ref, ce_ref, diag_ref, wt_ref, cx_ref), refs = refs[:8], refs[8:]
    sends, (kp, xp, pairs) = regroup(refs, rounds)
    z, y, _ = x_ref.shape
    tiles = y // tall
    per = tall // 8

    row8 = rows((8, 128))
    for slot, (src, dst) in enumerate(((x_ref, xp), (k_ref, kp))):
        dst[1 : z + 1, 8 : 8 + y, :] = src[...]
        ylo, yhi = both_sides("gy", hy, (slot,))
        zlo, zhi = both_sides("gz", hz, (slot,))
        if slot:
            has = present("gy")
            ylo, yhi = ylo * has[0], yhi * has[1]
            has = present("gz")
            zlo, zhi = zlo * has[0], zhi * has[1]
        dst[0, 8 : 8 + y, :] = zlo
        dst[z + 1, 8 : 8 + y, :] = zhi
        for i in range(z):
            dst[i + 1, 0:8, :] = jnp.broadcast_to(ylo[i : i + 1], (8, 128))
            dst[i + 1, 8 + y : 16 + y, :] = jnp.broadcast_to(yhi[i : i + 1], (8, 128))
    xlo, xhi = both_sides("gx", hx, (0,))
    klo, khi = both_sides("gx", hx, (1,))
    has = present("gx")
    west = harmonic(own_ref[1, 0], klo * has[0])
    east = harmonic(own_ref[1, 1], khi * has[1])
    cx_ref[0] = west
    cx_ref[1] = east
    stage_columns(pairs, 0, west, east)
    stage_columns(pairs, 1, west * (xlo - own_ref[0, 0]), east * (xhi - own_ref[0, 1]))

    lane = lanes((tall, 128))
    row = rows((tall, 128))

    def faces(i, t, carry):
        at = pl.multiple_of(t * tall, 8)
        here = kp[i + 1, pl.ds(at + 8, tall), :]
        cn_ref[i, pl.ds(at, tall), :] = harmonic(here, kp[i + 1, pl.ds(at + 7, tall), :])
        ce_ref[i, pl.ds(at, tall), :] = jnp.where(lane == 127, 0.0, harmonic(here, pltpu.roll(here, 127, 1)))
        cz_ref[i, pl.ds(at, tall), :] = vertical_ratio * harmonic(here, kp[i, pl.ds(at + 8, tall), :])

        @pl.when(i == z - 1)
        def _():
            cz_ref[z, pl.ds(at, tall), :] = vertical_ratio * harmonic(here, kp[z + 1, pl.ds(at + 8, tall), :])

        return carry

    tile_loop(z, tiles, faces, 0)
    for i in range(z):
        last = kp[i + 1, y + 7 : y + 8, :]
        face = harmonic(last, kp[i + 1, y + 8 : y + 9, :])
        cn_ref[i, y : y + 8, :] = jnp.where(row8 == 0, face, 0.0)

    def body(i, t, carry):
        at = pl.multiple_of(t * tall, 8)
        near = pl.ds(at, tall)
        x = xp[i + 1, pl.ds(at + 8, tall), :]
        width = band_ref[0, t]
        band = jnp.where((row < width) | (row >= tall - width), band_sink, 0.0)
        sink = coolant_film * flow_ref[i].astype(F32) + band
        cn = cn_ref[i, near, :]
        cs = cn_ref[i, pl.ds(at + 1, tall), :]
        ce = ce_ref[i, near, :]
        cw = pltpu.roll(ce, 1, 1)
        cd = cz_ref[i, near, :]
        cu = cz_ref[i + 1, near, :]
        base = i * (y // 8) + t * per
        diag = c_ref[i, near, :] / interval_increment + sink
        diag = diag + cd + cu + cn + cs + ce + cw + spread_columns(pairs, 0, base, per)
        power = cat_ref[sel_ref[i, 0, t]]
        r = power - sink * x + spread_columns(pairs, 1, base, per)
        r = r + cn * (xp[i + 1, pl.ds(at + 7, tall), :] - x) + cs * (xp[i + 1, pl.ds(at + 9, tall), :] - x)
        r = r + ce * (pltpu.roll(x, 127, 1) - x) + cw * (pltpu.roll(x, 1, 1) - x)
        r = r + cd * (xp[i, pl.ds(at + 8, tall), :] - x) + cu * (xp[i + 2, pl.ds(at + 8, tall), :] - x)
        weight = damping / diag
        diag_ref[i, near, :] = diag
        wt_ref[i, near, :] = weight
        r_ref[i, near, :] = r
        u_ref[i, near, :] = sweep_tile(r, weight, cn, cs, ce, lev_ref[i, 0, t])
        return carry

    tile_loop(z, tiles, body, 0)
    fill_sends(u_ref, sends, None, pack_columns(functools.partial(vreg, u_ref), z * y // 8))


def pad_field(src, dst, pairs, cx_ref, halos):
    z, y, _ = src.shape
    hx, hy, hz = halos
    dst[1 : z + 1, 8 : 8 + y, :] = src[...]
    ylo, yhi = both_sides("gy", hy)
    zlo, zhi = both_sides("gz", hz)
    dst[0, 8 : 8 + y, :] = zlo
    dst[z + 1, 8 : 8 + y, :] = zhi
    for i in range(z):
        dst[i + 1, 0:8, :] = jnp.broadcast_to(ylo[i : i + 1], (8, 128))
        dst[i + 1, 8 + y : 16 + y, :] = jnp.broadcast_to(yhi[i : i + 1], (8, 128))
    xlo, xhi = both_sides("gx", hx)
    stage_columns(pairs, 0, cx_ref[0] * xlo, cx_ref[1] * xhi)


def apply_tile(i, t, tall, y, vp, pairs, cz_ref, cn_ref, ce_ref, diag_ref):
    at = pl.multiple_of(t * tall, 8)
    near = pl.ds(at, tall)
    v = vp[i + 1, pl.ds(at + 8, tall), :]
    cn = cn_ref[i, near, :]
    cs = cn_ref[i, pl.ds(at + 1, tall), :]
    ce = ce_ref[i, near, :]
    total = cn * vp[i + 1, pl.ds(at + 7, tall), :] + cs * vp[i + 1, pl.ds(at + 9, tall), :]
    total = total + ce * pltpu.roll(v, 127, 1) + pltpu.roll(ce * v, 1, 1)
    total = total + cz_ref[i, near, :] * vp[i, pl.ds(at + 8, tall), :]
    total = total + cz_ref[i + 1, near, :] * vp[i + 2, pl.ds(at + 8, tall), :]
    total = total + spread_columns(pairs, 0, i * (y // 8) + t * (tall // 8), tall // 8)
    return near, v, diag_ref[i, near, :] * v - total, cn, cs, ce


def fold(product):
    return jnp.sum(product.reshape(-1, 8, 128), axis=0)


def third_kernel(rounds, tall, *refs):
    (u_ref, r_ref, cz_ref, cn_ref, ce_ref, diag_ref, wt_ref, cx_ref, lev_ref), refs = refs[:9], refs[9:]
    halos, refs = regroup(refs, rounds)
    (w_ref, m_ref, sum_ref), refs = refs[:3], refs[3:]
    sends, (up, pairs) = regroup(refs, rounds)
    z, y, _ = u_ref.shape
    pad_field(u_ref, up, pairs, cx_ref, halos)

    def body(i, t, carry):
        near, u, w, cn, cs, ce = apply_tile(i, t, tall, y, up, pairs, cz_ref, cn_ref, ce_ref, diag_ref)
        m = sweep_tile(w, wt_ref[i, near, :], cn, cs, ce, lev_ref[i, 0, t])
        w_ref[i, near, :] = w
        m_ref[i, near, :] = m
        gamma, delta, cross = carry
        return gamma + fold(r_ref[i, near, :] * u), delta + fold(w * u), cross + fold(w * m)

    zero = jnp.zeros((8, 128), F32)
    sums = tile_loop(z, y // tall, body, (zero, zero, zero))
    for n, value in enumerate(sums):
        sum_ref[n] = value
    fill_sends(m_ref, sends, None, pack_columns(functools.partial(vreg, m_ref), z * y // 8))


def fourth_kernel(rounds, tall, *refs):
    (m_ref, sum_ref, cz_ref, cn_ref, ce_ref, diag_ref, cx_ref), refs = refs[:7], refs[7:]
    halos, refs = regroup(refs, rounds)
    n_ref, out_ref, mp, pairs = refs
    z, y, _ = m_ref.shape
    pad_field(m_ref, mp, pairs, cx_ref, halos)

    def body(i, t, carry):
        near, m, n, _, _, _ = apply_tile(i, t, tall, y, mp, pairs, cz_ref, cn_ref, ce_ref, diag_ref)
        n_ref[i, near, :] = n
        return carry + fold(n * m)

    last = tile_loop(z, y // tall, body, jnp.zeros((8, 128), F32))
    parts = [sum_ref[0], sum_ref[1], sum_ref[2], last]
    parts = jnp.concatenate([jnp.sum(p, axis=0, keepdims=True) for p in parts], 0)
    for d in range(out_ref.shape[0]):
        out_ref[d] = parts


def last_kernel(all_ref, x_ref, r_ref, u_ref, w_ref, m_ref, n_ref, xo_ref, ro_ref):
    sums = jnp.sum(all_ref[...], axis=0)
    gamma, delta, cross, last = (sums[i : i + 1] for i in range(4))

    def total(v):
        return jnp.sum(v, axis=1, keepdims=True)

    gamma0 = total(gamma)
    alpha0 = gamma0 / total(delta)
    gamma1 = total(gamma - 2.0 * alpha0 * delta + alpha0 * alpha0 * cross)
    delta1 = total(delta - 2.0 * alpha0 * cross + alpha0 * alpha0 * last)
    beta = gamma1 / gamma0
    alpha1 = gamma1 / (delta1 - beta * gamma1 / alpha0)
    near = alpha0 + alpha1 * (1.0 + beta)
    far = alpha1 * alpha0
    for i in range(x_ref.shape[0]):
        xo_ref[i] = x_ref[i] + near * u_ref[i] - far * m_ref[i]
        ro_ref[i] = r_ref[i] - near * w_ref[i] + far * n_ref[i]


def swap_pairs(axis, start):
    count = lax.axis_size(axis)
    pairs = []
    for i in range(start, count - 1, 2):
        pairs += [(i, i + 1), (i + 1, i)]
    return pairs


def body(
    earlier_warmth_field,
    caloric_storage,
    thermal_diffusivity_coefficient,
    dissipation_catalog,
    dissipation_selector,
    refine_depth,
    border_band_width,
    microflow_flag,
):
    z, y, x = earlier_warmth_field.shape
    tall = dissipation_catalog.shape[1]
    groups = -(-(z * y // 8) // 128)
    rounds = tuple(2 if lax.axis_size(axis) > 2 else 1 for axis in GRID_AXES)
    shape = lambda *s: pltpu.VMEM(s, F32)
    full = shape(z, y, x)

    def call(kernel, outs, ins, name, scratch=(), specs=None):
        specs = specs or [SMEM if v.dtype == jnp.int32 else VMEM for v in ins]
        return pl.pallas_call(
            kernel, out_shape=outs, in_specs=specs, out_specs=[VMEM] * len(outs), scratch_shapes=list(scratch), name=name,
            compiler_params=pltpu.CompilerParams(vmem_limit_bytes=16 * 2**20),
        )(*ins)

    def face_shapes(front):
        out = []
        for axis, n in zip(((8 * groups, x), (z, x), (y, x)), rounds):
            out += [shape(*front, *axis)] * n
        return out

    def swap(faces):
        faces, got = list(faces), []
        for axis, n in zip(GRID_AXES, rounds):
            for start in range(n):
                got.append(lax.ppermute(faces.pop(0), axis, swap_pairs(axis, start)))
        return got

    sends = sum(rounds)
    pairs = pltpu.VMEM((2, 2, groups, 8, 128), F32)
    padded = pltpu.VMEM((z + 2, y + 16, x), F32)

    outs = call(
        functools.partial(first_kernel, rounds),
        [full, full, full, shape(*dissipation_catalog.shape)] + face_shapes((2,)) + [shape(2, 2, 8 * groups, x)],
        [earlier_warmth_field, thermal_diffusivity_coefficient, caloric_storage, dissipation_catalog],
        "faces",
        [pltpu.SemaphoreType.DMA((4,))],
        [pl.BlockSpec(memory_space=pltpu.HBM)] * 4,
    )
    (field, kappa, storage, catalog), outs = outs[:4], outs[4:]
    own, halos = outs[sends], swap(outs[:sends])
    selector = jnp.swapaxes(dissipation_selector, 1, 2)
    levels = jnp.swapaxes(refine_depth, 1, 2)
    width = jnp.swapaxes(border_band_width, 0, 1)
    outs = call(
        functools.partial(second_kernel, rounds, tall),
        [full, full, shape(z + 1, y, x), shape(z, y + 8, x), full, full, full, shape(2, 8 * groups, x)] + face_shapes(()),
        [field, storage, kappa, catalog, own, selector, levels, width, microflow_flag] + halos,
        "residual",
        [padded, padded, pairs],
    )
    r, u, cz, cn, ce, diag, weight, cx = outs[:8]
    halos = swap(outs[8:])
    outs = call(
        functools.partial(third_kernel, rounds, tall),
        [full, full, shape(3, 8, 128)] + face_shapes(()),
        [u, r, cz, cn, ce, diag, weight, cx, levels] + halos,
        "applied",
        [padded, pairs],
    )
    w, m, sums = outs[:3]
    halos = swap(outs[3:])
    members = math.prod(lax.axis_size(axis) for axis in GRID_AXES)
    n, parts = call(
        functools.partial(fourth_kernel, rounds, tall),
        [full, shape(members, 4, 128)],
        [m, sums, cz, cn, ce, diag, cx] + halos,
        "twice",
        [padded, pairs],
    )
    every = lax.all_to_all(parts, GRID_AXES, 0, 0, tiled=True)
    return tuple(
        call(last_kernel, [jax.ShapeDtypeStruct((z, y, x), F32)] * 2, [every, field, r, u, w, m, n], "update")
    )


def solution(mesh):
    cells = P(("groups", "gz"), "gy", "gx")
    return jax.shard_map(
        body,
        mesh=mesh,
        in_specs=(
            cells,
            cells,
            cells,
            P("groups", None, None),
            cells,
            cells,
            P(("groups", "gy"), "gx"),
            P(("groups", "gz")),
        ),
        out_specs=(cells, cells),
        check_vma=False,
    )
```

```python
import functools
import math

import jax
import jax.numpy as jnp
from jax import lax
from jax.experimental import pallas as pl
from jax.experimental.pallas import tpu as pltpu
from jax.sharding import PartitionSpec as P

interval_increment = 0.5
vertical_ratio = 2.0
coolant_film = 1.5
band_sink = 1.0
damping = 0.8
GRID_AXES = ("gx", "gy", "gz")
VMEM = pl.BlockSpec(memory_space=pltpu.VMEM)
SMEM = pl.BlockSpec(memory_space=pltpu.SMEM)
F32 = jnp.float32


def harmonic(first, second):
    return 2.0 * first * second / (first + second)


def lanes(shape=(8, 128)):
    return lax.broadcasted_iota(jnp.int32, shape, len(shape) - 1)


def rows(shape):
    return lax.broadcasted_iota(jnp.int32, shape, 0)


def low_side(axis, turn):
    odd = lax.rem(lax.axis_index(axis), 2) == 1
    return ~odd if turn else odd


def regroup(refs, counts):
    out, at = [], 0
    for c in counts:
        out.append(refs[at : at + c])
        at += c
    return out, refs[at:]


def pack_columns(load, count):
    lane = lanes()
    firsts, lasts = [], []
    for start in range(0, count, 128):
        parts = [jnp.zeros((8, 128), F32), jnp.zeros((8, 128), F32)]
        for i in range(min(128, count - start)):
            turned = load(start + i)
            if i:
                turned = pltpu.roll(turned, i, 1)
            here = (lane == i) | (lane == (i + 127) % 128)
            parts[i % 2] = jnp.where(here, turned, parts[i % 2])
        even = lane % 2 == 0
        firsts.append(jnp.where(even, parts[0], parts[1]))
        lasts.append(pltpu.roll(jnp.where(even, parts[1], parts[0]), 1, 1))
    return jnp.concatenate(firsts, 0), jnp.concatenate(lasts, 0)


def stage_columns(first, last):
    even = lanes() % 2 == 0
    out = []
    for g in range(first.shape[0] // 8):
        f = first[8 * g : 8 * g + 8]
        l = pltpu.roll(last[8 * g : 8 * g + 8], 127, 1)
        out.append((jnp.where(even, f, l), jnp.where(even, l, f)))
    return out


def spread_columns(staged, edge, i):
    turned = staged[i // 128][i % 2]
    if i % 128:
        turned = pltpu.roll(turned, 128 - i % 128, 1)
    return jnp.where(edge, turned, 0.0)


def edge_lanes():
    lane = lanes()
    return (lane == 0) | (lane == 127)


def column_halos(refs, slot=()):
    low = low_side("gx", 0)
    got = [ref[slot] if slot else ref[...] for ref in refs]
    if len(got) == 1:
        got.append(jnp.zeros_like(got[0]))
    return jnp.where(low, got[0], got[1]), jnp.where(low, got[1], got[0])


def fill_sends(tier, row, send_refs, slot, columns, z, y):
    for axis, refs in zip(GRID_AXES, send_refs):
        for n, ref in enumerate(refs):
            low = low_side(axis, n)
            if axis == "gx":
                value = jnp.where(low, columns[0], columns[1])
            elif axis == "gy":
                value = jnp.where(low, row(0), row(y - 1))
            else:
                value = tier(jnp.where(low, 0, z - 1))
            if slot is None:
                ref[...] = value
            else:
                ref[slot] = value


def padded_access(ref):
    y = ref.shape[1] - 16

    def tier(i):
        return ref[i, pl.ds(8, y), :]

    def row(r):
        return ref[:, 8 + r, :]

    def vreg(i):
        return ref[i // (y // 8), 8 + 8 * (i % (y // 8)) : 16 + 8 * (i % (y // 8)), :]

    return tier, row, vreg


def clear_margins(ref):
    z, y, _ = ref.shape
    for i in range(z):
        ref[i, 0:8, :] = jnp.zeros((8, 128), F32)
        ref[i, y - 8 : y, :] = jnp.zeros((8, 128), F32)


def start_all(sources, targets, sems):
    copies = [pltpu.make_async_copy(a, b, sems.at[n]) for n, (a, b) in enumerate(zip(sources, targets))]
    for copy in copies:
        copy.start()
    return copies


def faces_kernel(rounds, x_in, k_in, sel_in, lev_in, band_in, flow_in, *refs):
    (x_ref, k_ref, sel_ref, lev_ref, band_ref, flow_ref), refs = refs[:6], refs[6:]
    sends, (own_ref, sems) = regroup(refs, rounds)
    z, y, _ = x_in.shape
    inner = pl.ds(8, y)
    copies = start_all(
        (x_in, k_in, sel_in, lev_in, band_in, flow_in),
        (x_ref.at[:, inner, :], k_ref.at[:, inner, :], sel_ref, lev_ref, band_ref, flow_ref),
        sems,
    )
    for slot, ref in enumerate((x_ref, k_ref)):
        clear_margins(ref)
        copies[slot].wait()
        tier, row, vreg = padded_access(ref)
        columns = pack_columns(vreg, z * y // 8)
        own_ref[slot, 0] = columns[0]
        own_ref[slot, 1] = columns[1]
        fill_sends(tier, row, sends, slot, columns, z, y)
    for copy in copies[2:]:
        copy.wait()


def inner_kernel(tall, x_ref, k_ref, c_in, cat_in, sel_ref, band_ref, flow_ref, *refs):
    r_ref, diag_ref, cz_ref, cs_ref, ce_ref, c_ref, cat_ref, sems = refs
    z, y, _ = c_ref.shape
    copies = start_all((c_in, cat_in), (c_ref, cat_ref), sems)
    lane = lanes((tall, 128))
    row = rows((tall, 128))
    for i in range(z):
        cs_ref[i, 0:8, :] = jnp.zeros((8, 128), F32)

    def faces(t, carry):
        at = pl.multiple_of(t * tall, 8)
        last = jnp.where(t == y // tall - 1, tall - 1, tall)
        for i in range(z):
            here = k_ref[i, pl.ds(at + 8, tall), :]
            south = harmonic(here, k_ref[i, pl.ds(at + 9, tall), :])
            cs_ref[i, pl.ds(at + 8, tall), :] = jnp.where(row == last, 0.0, south)
            ce_ref[i, pl.ds(at, tall), :] = jnp.where(lane == 127, 0.0, harmonic(here, pltpu.roll(here, 127, 1)))
            if i + 1 < z:
                above = k_ref[i + 1, pl.ds(at + 8, tall), :]
                cz_ref[i, pl.ds(at, tall), :] = vertical_ratio * harmonic(here, above)
        return carry

    lax.fori_loop(0, y // tall, faces, 0)
    for copy in copies:
        copy.wait()

    def rest(t, carry):
        at = pl.multiple_of(t * tall, 8)
        near = pl.ds(at, tall)
        mid = pl.ds(at + 8, tall)
        width = band_ref[0, t]
        band = jnp.where((row < width) | (row >= tall - width), band_sink, 0.0)
        for i in range(z):
            x = x_ref[i, mid, :]
            sink = coolant_film * flow_ref[i].astype(F32) + band
            cn = cs_ref[i, pl.ds(at + 7, tall), :]
            cs = cs_ref[i, mid, :]
            ce = ce_ref[i, near, :]
            cw = pltpu.roll(ce, 1, 1)
            r = cat_ref[sel_ref[i, 0, t]] - sink * x
            r = r + cn * (x_ref[i, pl.ds(at + 7, tall), :] - x) + cs * (x_ref[i, pl.ds(at + 9, tall), :] - x)
            r = r + ce * (pltpu.roll(x, 127, 1) - x) + cw * (pltpu.roll(x, 1, 1) - x)
            diag = c_ref[i, near, :] * (1.0 / interval_increment) + sink
            diag = diag + ((cn + cs) + (ce + cw))
            if i:
                cd = cz_ref[i - 1, near, :]
                diag = diag + cd
                r = r + cd * (x_ref[i - 1, mid, :] - x)
            if i + 1 < z:
                cu = cz_ref[i, near, :]
                diag = diag + cu
                r = r + cu * (x_ref[i + 1, mid, :] - x)
            diag_ref[i, near, :] = diag
            r_ref[i, near, :] = r
        return carry

    lax.fori_loop(0, y // tall, rest, 0)


def sweeps(field_ref, diag_ref, cs_ref, ce_ref, lev_ref, tall):
    z, y, _ = diag_ref.shape
    tiles = y // tall
    row = rows((tall, 128))

    def tile(i, t):
        level = lev_ref[i, 0, t]

        @pl.when(level > 1)
        def _():
            at = pl.multiple_of(t * tall, 8)
            mid = pl.ds(at + 8, tall)
            start = field_ref[i, mid, :]
            weight = damping / diag_ref[i, pl.ds(at, tall), :]
            north = jnp.where(row == 0, 0.0, cs_ref[i, pl.ds(at + 7, tall), :])
            south = jnp.where(row == tall - 1, 0.0, cs_ref[i, mid, :])
            east = ce_ref[i, pl.ds(at, tall), :]

            def once(_, state):
                inner = north * pltpu.roll(state, 1, 0) + south * pltpu.roll(state, tall - 1, 0)
                inner = inner + east * pltpu.roll(state, 127, 1) + pltpu.roll(east * state, 1, 1)
                return (1.0 - damping) * state + (start + weight * inner)

            field_ref[i, mid, :] = lax.fori_loop(1, jnp.minimum(level, 4), once, start)

    def tier(i, carry):
        def step(t, carry):
            tile(i, t)
            return carry

        return lax.fori_loop(0, tiles, step, carry)

    lax.fori_loop(0, z, tier, 0)


def border_kernel(rounds, tall, *refs):
    (x_ref, k_ref, own_ref, r_in, diag_in, cs_ref, ce_ref, lev_ref), refs = refs[:8], refs[8:]
    (hx, hy, hz), refs = regroup(refs, rounds)
    (r_ref, diag_ref, u_ref, cx_ref, cy_ref, czh_ref), refs = refs[:6], refs[6:]
    sends, _ = regroup(refs, rounds)
    z, y, _ = r_ref.shape
    for n, ref in enumerate(hz):
        p = jnp.where(low_side("gz", n), 0, z - 1)
        face = vertical_ratio * harmonic(k_ref[p, pl.ds(8, y), :], ref[1])
        czh_ref[n] = face
        diag_in[p] = diag_in[p] + face
        r_in[p] = r_in[p] + face * (ref[0] - x_ref[p, pl.ds(8, y), :])
    row8 = rows((8, 128))
    for n, ref in enumerate(hy):
        low = low_side("gy", n)
        at = pl.multiple_of(jnp.where(low, 0, y - 8), 8)
        mask = row8 == jnp.where(low, 0, 7)
        for i in range(z):
            there = pl.ds(at, 8)
            inside = pl.ds(at + 8, 8)
            face = harmonic(k_ref[i, inside, :], ref[1, i : i + 1, :])
            face = jnp.where(mask, face, 0.0)
            cy_ref[n, i] = face
            diag_in[i, there, :] = diag_in[i, there, :] + face
            r_in[i, there, :] = r_in[i, there, :] + face * (ref[0, i : i + 1, :] - x_ref[i, inside, :])
    xlo, xhi = column_halos(hx, (0,))
    klo, khi = column_halos(hx, (1,))
    west = harmonic(own_ref[1, 0], klo)
    east = harmonic(own_ref[1, 1], khi)
    cx_ref[0] = west
    cx_ref[1] = east
    faces = stage_columns(west, east)
    flux = stage_columns(west * (xlo - own_ref[0, 0]), east * (xhi - own_ref[0, 1]))
    edge = edge_lanes()
    clear_margins(u_ref)
    per = y // 8
    for i in range(z * per):
        at = (i // per, slice(8 * (i % per), 8 * (i % per) + 8))
        diag = diag_in[at] + spread_columns(faces, edge, i)
        r = r_in[at] + spread_columns(flux, edge, i)
        diag_ref[at] = diag
        r_ref[at] = r
        u_ref[i // per, 8 + 8 * (i % per) : 16 + 8 * (i % per)] = r * (damping / diag)
    sweeps(u_ref, diag_ref, cs_ref, ce_ref, lev_ref, tall)
    tier, row, vreg = padded_access(u_ref)
    fill_sends(tier, row, sends, None, pack_columns(vreg, z * per), z, y)


def apply_inner(field_ref, diag_ref, cz_ref, cs_ref, ce_ref, i, at, tall):
    z = diag_ref.shape[0]
    near = pl.ds(at, tall)
    mid = pl.ds(at + 8, tall)
    v = field_ref[i, mid, :]
    ce = ce_ref[i, near, :]
    total = cs_ref[i, pl.ds(at + 7, tall), :] * field_ref[i, pl.ds(at + 7, tall), :]
    total = total + cs_ref[i, mid, :] * field_ref[i, pl.ds(at + 9, tall), :]
    total = total + (ce * pltpu.roll(v, 127, 1) + pltpu.roll(ce * v, 1, 1))
    if i:
        total = total + cz_ref[i - 1, near, :] * field_ref[i - 1, mid, :]
    if i + 1 < z:
        total = total + cz_ref[i, near, :] * field_ref[i + 1, mid, :]
    return v, diag_ref[i, near, :] * v - total


def apply_kernel(tall, u_ref, diag_ref, cz_ref, cs_ref, ce_ref, w_ref):
    z, y, _ = diag_ref.shape

    def step(t, carry):
        at = pl.multiple_of(t * tall, 8)
        for i in range(z):
            w_ref[i, pl.ds(at, tall), :] = apply_inner(u_ref, diag_ref, cz_ref, cs_ref, ce_ref, i, at, tall)[1]
        return carry

    lax.fori_loop(0, y // tall, step, 0)


def subtract_halos(w_ref, halos, cy_ref, czh_ref):
    hx, hy, hz = halos
    z, y, _ = w_ref.shape
    for n, ref in enumerate(hz):
        p = jnp.where(low_side("gz", n), 0, z - 1)
        w_ref[p] = w_ref[p] - czh_ref[n] * ref[...]
    for n, ref in enumerate(hy):
        at = pl.ds(pl.multiple_of(jnp.where(low_side("gy", n), 0, y - 8), 8), 8)
        for i in range(z):
            w_ref[i, at, :] = w_ref[i, at, :] - cy_ref[n, i] * ref[i : i + 1, :]


def smooth_kernel(rounds, tall, *refs):
    (w_in, diag_ref, cs_ref, ce_ref, cx_ref, cy_ref, czh_ref, lev_ref), refs = refs[:8], refs[8:]
    halos, refs = regroup(refs, rounds)
    (w_ref, m_ref), refs = refs[:2], refs[2:]
    sends, _ = regroup(refs, rounds)
    z, y, _ = w_ref.shape
    subtract_halos(w_in, halos, cy_ref, czh_ref)
    xlo, xhi = column_halos(halos[0])
    flux = stage_columns(cx_ref[0] * xlo, cx_ref[1] * xhi)
    edge = edge_lanes()
    clear_margins(m_ref)
    per = y // 8
    for i in range(z * per):
        at = (i // per, slice(8 * (i % per), 8 * (i % per) + 8))
        w = w_in[at] - spread_columns(flux, edge, i)
        w_ref[at] = w
        m_ref[i // per, 8 + 8 * (i % per) : 16 + 8 * (i % per)] = w * (damping / diag_ref[at])
    sweeps(m_ref, diag_ref, cs_ref, ce_ref, lev_ref, tall)
    tier, row, vreg = padded_access(m_ref)
    fill_sends(tier, row, sends, None, pack_columns(vreg, z * per), z, y)


def fold(product):
    return jnp.sum(product.reshape(-1, 8, 128), axis=0)


def sums_kernel(tall, m_ref, u_ref, r_ref, w_ref, diag_ref, cz_ref, cs_ref, ce_ref, n_ref, sum_ref):
    z, y, _ = diag_ref.shape

    def step(t, carry):
        gamma, delta, cross = carry
        at = pl.multiple_of(t * tall, 8)
        near = pl.ds(at, tall)
        for i in range(z):
            m, n_ref[i, near, :] = apply_inner(m_ref, diag_ref, cz_ref, cs_ref, ce_ref, i, at, tall)
            u = u_ref[i, pl.ds(at + 8, tall), :]
            w = w_ref[i, near, :]
            gamma = gamma + fold(r_ref[i, near, :] * u)
            delta = delta + fold(w * u)
            cross = cross + fold(w * m)
        return gamma, delta, cross

    zero = jnp.zeros((8, 128), F32)
    for n, value in enumerate(lax.fori_loop(0, y // tall, step, (zero, zero, zero))):
        sum_ref[n] = value


def finish_kernel(rounds, *refs):
    (n_in, m_ref, sum_ref, cx_ref, cy_ref, czh_ref), refs = refs[:6], refs[6:]
    halos, (n_ref, out_ref) = regroup(refs, rounds)
    z, y, _ = n_ref.shape
    subtract_halos(n_in, halos, cy_ref, czh_ref)
    xlo, xhi = column_halos(halos[0])
    flux = stage_columns(cx_ref[0] * xlo, cx_ref[1] * xhi)
    edge = edge_lanes()
    per = y // 8
    parts = [jnp.zeros((8, 128), F32) for _ in range(8)]
    for i in range(z * per):
        at = (i // per, slice(8 * (i % per), 8 * (i % per) + 8))
        n = n_in[at] - spread_columns(flux, edge, i)
        n_ref[at] = n
        parts[i % 8] = parts[i % 8] + n * m_ref[i // per, 8 + 8 * (i % per) : 16 + 8 * (i % per)]
    while len(parts) > 1:
        parts = [a + b for a, b in zip(parts[::2], parts[1::2])]
    parts = [sum_ref[0], sum_ref[1], sum_ref[2], parts[0]]
    parts = jnp.concatenate([jnp.sum(p, axis=0, keepdims=True) for p in parts], 0)
    for d in range(out_ref.shape[0]):
        out_ref[d] = parts


def update_kernel(all_ref, x_ref, r_ref, u_ref, w_ref, m_ref, n_ref, x_out, r_out, xo_ref, ro_ref, sems):
    sums = jnp.sum(all_ref[...], axis=0)
    gamma, delta, cross, last = (sums[i : i + 1] for i in range(4))

    def total(v):
        return jnp.sum(v, axis=1, keepdims=True)

    gamma0 = total(gamma)
    alpha0 = gamma0 / total(delta)
    gamma1 = total(gamma - 2.0 * alpha0 * delta + alpha0 * alpha0 * cross)
    delta1 = total(delta - 2.0 * alpha0 * cross + alpha0 * alpha0 * last)
    beta = gamma1 / gamma0
    alpha1 = gamma1 / (delta1 - beta * gamma1 / alpha0)
    near = alpha0 + alpha1 * (1.0 + beta)
    far = alpha1 * alpha0
    z, y, _ = r_ref.shape
    copies = []
    for i in range(z):
        inner = (i, slice(8, 8 + y))
        xo_ref[i] = x_ref[inner] + near * u_ref[inner] - far * m_ref[inner]
        ro_ref[i] = r_ref[i] - near * w_ref[i] + far * n_ref[i]
        copies += start_all((xo_ref.at[i], ro_ref.at[i]), (x_out.at[i], r_out.at[i]), sems.at[i])
    for copy in copies:
        copy.wait()


def swap_pairs(axis, start):
    count = lax.axis_size(axis)
    pairs = []
    for i in range(start, count - 1, 2):
        pairs += [(i, i + 1), (i + 1, i)]
    return pairs


def body(
    earlier_warmth_field,
    caloric_storage,
    thermal_diffusivity_coefficient,
    dissipation_catalog,
    dissipation_selector,
    refine_depth,
    border_band_width,
    microflow_flag,
):
    z, y, x = earlier_warmth_field.shape
    tall = dissipation_catalog.shape[1]
    groups = -(-(z * y // 8) // 128)
    rounds = tuple(2 if lax.axis_size(axis) > 2 else 1 for axis in GRID_AXES)
    sends = sum(rounds)
    shape = lambda *s: pltpu.VMEM(s, F32)
    full = shape(z, y, x)
    tall_field = shape(z, y + 16, x)

    def outside(v):
        return pltpu.with_memory_space_constraint(v, pltpu.HBM)

    def call(kernel, outs, ins, name, scratch=(), specs=None, out_specs=None, alias=None):
        specs = specs or [SMEM if v.dtype == jnp.int32 else VMEM for v in ins]
        return pl.pallas_call(
            kernel,
            out_shape=outs,
            in_specs=specs,
            out_specs=out_specs or [VMEM] * len(outs),
            scratch_shapes=list(scratch),
            input_output_aliases=alias or {},
            name=name,
            compiler_params=pltpu.CompilerParams(vmem_limit_bytes=16 * 2**20),
        )(*ins)

    def face_shapes(front):
        out = []
        for axis, n in zip(((8 * groups, x), (z, x), (y, x)), rounds):
            out += [shape(*front, *axis)] * n
        return out

    def swap(faces):
        faces, got = list(faces), []
        for axis, n in zip(GRID_AXES, rounds):
            for start in range(n):
                got.append(lax.ppermute(faces.pop(0), axis, swap_pairs(axis, start)))
        return got

    tables = [
        jnp.swapaxes(dissipation_selector, 1, 2),
        jnp.swapaxes(refine_depth, 1, 2),
        jnp.swapaxes(border_band_width, 0, 1),
        microflow_flag,
    ]
    hbm = pl.BlockSpec(memory_space=pltpu.HBM)
    outs = call(
        functools.partial(faces_kernel, rounds),
        [tall_field, tall_field]
        + [pltpu.VMEM(t.shape, t.dtype) for t in tables]
        + face_shapes((2,))
        + [shape(2, 2, 8 * groups, x)],
        [outside(v) for v in (earlier_warmth_field, thermal_diffusivity_coefficient, *tables)],
        "faces",
        [pltpu.SemaphoreType.DMA((6,))],
        [hbm] * 6,
    )
    (field, kappa, selector, levels, width, flow), outs = outs[:6], outs[6:]
    own, halos = outs[sends], swap(outs[:sends])
    r, diag, cz, cs, ce = call(
        functools.partial(inner_kernel, tall),
        [full, full, shape(max(z - 1, 1), y, x), shape(z, y + 8, x), full],
        [field, kappa, outside(caloric_storage), outside(dissipation_catalog), selector, width, flow],
        "inner",
        [full, shape(*dissipation_catalog.shape), pltpu.SemaphoreType.DMA((2,))],
        [VMEM, VMEM, hbm, hbm, SMEM, SMEM, SMEM],
    )
    outs = call(
        functools.partial(border_kernel, rounds, tall),
        [full, full, tall_field, shape(2, 8 * groups, x), shape(rounds[1], z, 8, x), shape(rounds[2], y, x)]
        + face_shapes(()),
        [field, kappa, own, r, diag, cs, ce, levels] + halos,
        "border",
        alias={3: 0, 4: 1},
    )
    r, diag, u, cx, cy, czh = outs[:6]
    halos = swap(outs[6:])
    (w,) = call(functools.partial(apply_kernel, tall), [full], [u, diag, cz, cs, ce], "apply")
    outs = call(
        functools.partial(smooth_kernel, rounds, tall),
        [full, tall_field] + face_shapes(()),
        [w, diag, cs, ce, cx, cy, czh, levels] + halos,
        "smooth",
        alias={0: 0},
    )
    w, m = outs[:2]
    halos = swap(outs[2:])
    n, sums = call(
        functools.partial(sums_kernel, tall), [full, shape(3, 8, 128)], [m, u, r, w, diag, cz, cs, ce], "sums"
    )
    members = math.prod(lax.axis_size(axis) for axis in GRID_AXES)
    n, parts = call(
        functools.partial(finish_kernel, rounds),
        [full, shape(members, 4, 128)],
        [n, m, sums, cx, cy, czh] + halos,
        "finish",
        alias={0: 0},
    )
    every = lax.all_to_all(parts, GRID_AXES, 0, 0, tiled=True)
    return tuple(
        call(
            update_kernel,
            [jax.ShapeDtypeStruct((z, y, x), F32)] * 2,
            [every, field, r, u, w, m, n],
            "update",
            [full, full, pltpu.SemaphoreType.DMA((z, 2))],
            out_specs=[hbm, hbm],
        )
    )


def solution(mesh):
    cells = P(("groups", "gz"), "gy", "gx")
    return jax.shard_map(
        body,
        mesh=mesh,
        in_specs=(
            cells,
            cells,
            cells,
            P("groups", None, None),
            cells,
            cells,
            P(("groups", "gy"), "gx"),
            P(("groups", "gz")),
        ),
        out_specs=(cells, cells),
        check_vma=False,
    )
```

```python
import functools
import math

import jax
import jax.numpy as jnp
from jax import lax
from jax.experimental import pallas as pl
from jax.experimental.pallas import tpu as pltpu
from jax.sharding import PartitionSpec as P

interval_increment = 0.5
vertical_ratio = 2.0
coolant_film = 1.5
band_sink = 1.0
damping = 0.8
GRID_AXES = ("gx", "gy", "gz")
VMEM = pl.BlockSpec(memory_space=pltpu.VMEM)
F32 = jnp.float32


def harmonic(first, second):
    return 2.0 * first * second / (first + second)


def lanes(shape=(8, 128)):
    return lax.broadcasted_iota(jnp.int32, shape, len(shape) - 1)


def rows(shape):
    return lax.broadcasted_iota(jnp.int32, shape, 0)


def low_side(axis, turn):
    odd = lax.rem(lax.axis_index(axis), 2) == 1
    return ~odd if turn else odd


def regroup(refs, counts):
    out, at = [], 0
    for c in counts:
        out.append(refs[at : at + c])
        at += c
    return out, refs[at:]


def pack_columns(load, count):
    lane = lanes()
    firsts, lasts = [], []
    for start in range(0, count, 128):
        parts = [jnp.zeros((8, 128), F32), jnp.zeros((8, 128), F32)]
        for i in range(min(128, count - start)):
            turned = load(start + i)
            if i:
                turned = pltpu.roll(turned, i, 1)
            here = (lane == i) | (lane == (i + 127) % 128)
            parts[i % 2] = jnp.where(here, turned, parts[i % 2])
        even = lane % 2 == 0
        firsts.append(jnp.where(even, parts[0], parts[1]))
        lasts.append(pltpu.roll(jnp.where(even, parts[1], parts[0]), 1, 1))
    return jnp.concatenate(firsts, 0), jnp.concatenate(lasts, 0)


def stage_columns(first, last):
    even = lanes() % 2 == 0
    out = []
    for g in range(first.shape[0] // 8):
        f = first[8 * g : 8 * g + 8]
        l = pltpu.roll(last[8 * g : 8 * g + 8], 127, 1)
        out.append((jnp.where(even, f, l), jnp.where(even, l, f)))
    return out


def spread_columns(staged, edge, i):
    turned = staged[i // 128][i % 2]
    if i % 128:
        turned = pltpu.roll(turned, 128 - i % 128, 1)
    return jnp.where(edge, turned, 0.0)


def edge_lanes():
    lane = lanes()
    return (lane == 0) | (lane == 127)


def column_halos(refs, slot=()):
    low = low_side("gx", 0)
    got = [ref[slot] if slot else ref[...] for ref in refs]
    if len(got) == 1:
        got.append(jnp.zeros_like(got[0]))
    return jnp.where(low, got[0], got[1]), jnp.where(low, got[1], got[0])


def fill_sends(tier, row, send_refs, slot, columns, z, y):
    for axis, refs in zip(GRID_AXES, send_refs):
        for n, ref in enumerate(refs):
            low = low_side(axis, n)
            if axis == "gx":
                value = jnp.where(low, columns[0], columns[1])
            elif axis == "gy":
                value = jnp.where(low, row(0), row(y - 1))
            else:
                value = tier(jnp.where(low, 0, z - 1))
            if slot is None:
                ref[...] = value
            else:
                ref[slot] = value


def padded_access(ref):
    y = ref.shape[1] - 16

    def tier(i):
        return ref[i, pl.ds(8, y), :]

    def row(r):
        return ref[:, 8 + r, :]

    def vreg(i):
        return ref[i // (y // 8), 8 + 8 * (i % (y // 8)) : 16 + 8 * (i % (y // 8)), :]

    return tier, row, vreg


def clear_margins(ref):
    z, y, _ = ref.shape
    for i in range(z):
        ref[i, 0:8, :] = jnp.zeros((8, 128), F32)
        ref[i, y - 8 : y, :] = jnp.zeros((8, 128), F32)


def start_all(sources, targets, sems):
    copies = [pltpu.make_async_copy(a, b, sems.at[n]) for n, (a, b) in enumerate(zip(sources, targets))]
    for copy in copies:
        copy.start()
    return copies


def faces_kernel(rounds, x_in, k_in, x_ref, k_ref, *refs):
    sends, (own_ref, sems) = regroup(refs, rounds)
    z, y, _ = x_in.shape
    per = y // 8
    fields = (x_ref, k_ref)
    copies = [
        start_all([source.at[i] for i in range(z)], [ref.at[i, pl.ds(8, y), :] for i in range(z)], sems.at[n])
        for n, (source, ref) in enumerate(zip((x_in, k_in), fields))
    ]
    for slot, ref in enumerate(fields):
        clear_margins(ref)
        tier, row, vreg = padded_access(ref)

        def load(i):
            if i % per == 0:
                copies[slot][i // per].wait()
            return vreg(i)

        columns = pack_columns(load, z * per)
        own_ref[slot, 0] = columns[0]
        own_ref[slot, 1] = columns[1]
        fill_sends(tier, row, sends, slot, columns, z, y)


def inner_kernel(tall, x_ref, k_ref, c_ref, cat_ref, sel_in, band_in, flow_in, *refs):
    r_ref, diag_ref, cz_ref, cs_ref, ce_ref, sel_ref, band_ref, flow_ref, sems = refs
    z, y, _ = c_ref.shape
    copies = start_all((sel_in, band_in, flow_in), (sel_ref, band_ref, flow_ref), sems)
    lane = lanes((tall, 128))
    row = rows((tall, 128))
    for i in range(z):
        cs_ref[i, 0:8, :] = jnp.zeros((8, 128), F32)

    def faces(t, carry):
        at = pl.multiple_of(t * tall, 8)
        last = jnp.where(t == y // tall - 1, tall - 1, tall)
        for i in range(z):
            here = k_ref[i, pl.ds(at + 8, tall), :]
            south = harmonic(here, k_ref[i, pl.ds(at + 9, tall), :])
            cs_ref[i, pl.ds(at + 8, tall), :] = jnp.where(row == last, 0.0, south)
            ce_ref[i, pl.ds(at, tall), :] = jnp.where(lane == 127, 0.0, harmonic(here, pltpu.roll(here, 127, 1)))
            if i + 1 < z:
                above = k_ref[i + 1, pl.ds(at + 8, tall), :]
                cz_ref[i, pl.ds(at, tall), :] = vertical_ratio * harmonic(here, above)
        return carry

    lax.fori_loop(0, y // tall, faces, 0)
    for copy in copies:
        copy.wait()

    def rest(t, carry):
        at = pl.multiple_of(t * tall, 8)
        near = pl.ds(at, tall)
        mid = pl.ds(at + 8, tall)
        width = band_ref[0, t]
        band = jnp.where((row < width) | (row >= tall - width), band_sink, 0.0)
        for i in range(z):
            x = x_ref[i, mid, :]
            sink = coolant_film * flow_ref[i].astype(F32) + band
            cn = cs_ref[i, pl.ds(at + 7, tall), :]
            cs = cs_ref[i, mid, :]
            ce = ce_ref[i, near, :]
            cw = pltpu.roll(ce, 1, 1)
            r = cat_ref[sel_ref[i, 0, t]] - sink * x
            r = r + cn * (x_ref[i, pl.ds(at + 7, tall), :] - x) + cs * (x_ref[i, pl.ds(at + 9, tall), :] - x)
            r = r + ce * (pltpu.roll(x, 127, 1) - x) + cw * (pltpu.roll(x, 1, 1) - x)
            diag = c_ref[i, near, :] * (1.0 / interval_increment) + sink
            diag = diag + ((cn + cs) + (ce + cw))
            if i:
                cd = cz_ref[i - 1, near, :]
                diag = diag + cd
                r = r + cd * (x_ref[i - 1, mid, :] - x)
            if i + 1 < z:
                cu = cz_ref[i, near, :]
                diag = diag + cu
                r = r + cu * (x_ref[i + 1, mid, :] - x)
            diag_ref[i, near, :] = diag
            r_ref[i, near, :] = r
        return carry

    lax.fori_loop(0, y // tall, rest, 0)


def sweeps(field_ref, diag_ref, cs_ref, ce_ref, lev_ref, tall):
    z, y, _ = diag_ref.shape
    tiles = y // tall
    row = rows((tall, 128))

    def tile(i, t):
        level = lev_ref[i, 0, t]

        @pl.when(level > 1)
        def _():
            at = pl.multiple_of(t * tall, 8)
            mid = pl.ds(at + 8, tall)
            start = field_ref[i, mid, :]
            weight = damping / diag_ref[i, pl.ds(at, tall), :]
            north = jnp.where(row == 0, 0.0, cs_ref[i, pl.ds(at + 7, tall), :])
            south = jnp.where(row == tall - 1, 0.0, cs_ref[i, mid, :])
            east = ce_ref[i, pl.ds(at, tall), :]

            def once(_, state):
                inner = north * pltpu.roll(state, 1, 0) + south * pltpu.roll(state, tall - 1, 0)
                inner = inner + east * pltpu.roll(state, 127, 1) + pltpu.roll(east * state, 1, 1)
                return (1.0 - damping) * state + (start + weight * inner)

            field_ref[i, mid, :] = lax.fori_loop(1, jnp.minimum(level, 4), once, start)

    def tier(i, carry):
        def step(t, carry):
            tile(i, t)
            return carry

        return lax.fori_loop(0, tiles, step, carry)

    lax.fori_loop(0, z, tier, 0)


def border_kernel(rounds, tall, *refs):
    (x_ref, k_ref, own_ref, r_in, diag_in, cs_ref, ce_ref, lev_in), refs = refs[:8], refs[8:]
    (hx, hy, hz), refs = regroup(refs, rounds)
    (r_ref, diag_ref, u_ref, cx_ref, cy_ref, czh_ref), refs = refs[:6], refs[6:]
    sends, (lev_ref, sems) = regroup(refs, rounds)
    z, y, _ = r_ref.shape
    table = start_all((lev_in,), (lev_ref,), sems)
    for n, ref in enumerate(hz):
        p = jnp.where(low_side("gz", n), 0, z - 1)
        face = vertical_ratio * harmonic(k_ref[p, pl.ds(8, y), :], ref[1])
        czh_ref[n] = face
        diag_in[p] = diag_in[p] + face
        r_in[p] = r_in[p] + face * (ref[0] - x_ref[p, pl.ds(8, y), :])
    row8 = rows((8, 128))
    for n, ref in enumerate(hy):
        low = low_side("gy", n)
        at = pl.multiple_of(jnp.where(low, 0, y - 8), 8)
        mask = row8 == jnp.where(low, 0, 7)
        for i in range(z):
            there = pl.ds(at, 8)
            inside = pl.ds(at + 8, 8)
            face = harmonic(k_ref[i, inside, :], ref[1, i : i + 1, :])
            face = jnp.where(mask, face, 0.0)
            cy_ref[n, i] = face
            diag_in[i, there, :] = diag_in[i, there, :] + face
            r_in[i, there, :] = r_in[i, there, :] + face * (ref[0, i : i + 1, :] - x_ref[i, inside, :])
    xlo, xhi = column_halos(hx, (0,))
    klo, khi = column_halos(hx, (1,))
    west = harmonic(own_ref[1, 0], klo)
    east = harmonic(own_ref[1, 1], khi)
    cx_ref[0] = west
    cx_ref[1] = east
    faces = stage_columns(west, east)
    flux = stage_columns(west * (xlo - own_ref[0, 0]), east * (xhi - own_ref[0, 1]))
    edge = edge_lanes()
    clear_margins(u_ref)
    per = y // 8
    for i in range(z * per):
        at = (i // per, slice(8 * (i % per), 8 * (i % per) + 8))
        diag = diag_in[at] + spread_columns(faces, edge, i)
        r = r_in[at] + spread_columns(flux, edge, i)
        diag_ref[at] = diag
        r_ref[at] = r
        u_ref[i // per, 8 + 8 * (i % per) : 16 + 8 * (i % per)] = r * (damping / diag)
    table[0].wait()
    sweeps(u_ref, diag_ref, cs_ref, ce_ref, lev_ref, tall)
    tier, row, vreg = padded_access(u_ref)
    fill_sends(tier, row, sends, None, pack_columns(vreg, z * per), z, y)


def apply_inner(field_ref, diag_ref, cz_ref, cs_ref, ce_ref, i, at, tall):
    z = diag_ref.shape[0]
    near = pl.ds(at, tall)
    mid = pl.ds(at + 8, tall)
    v = field_ref[i, mid, :]
    ce = ce_ref[i, near, :]
    total = cs_ref[i, pl.ds(at + 7, tall), :] * field_ref[i, pl.ds(at + 7, tall), :]
    total = total + cs_ref[i, mid, :] * field_ref[i, pl.ds(at + 9, tall), :]
    total = total + (ce * pltpu.roll(v, 127, 1) + pltpu.roll(ce * v, 1, 1))
    if i:
        total = total + cz_ref[i - 1, near, :] * field_ref[i - 1, mid, :]
    if i + 1 < z:
        total = total + cz_ref[i, near, :] * field_ref[i + 1, mid, :]
    return v, diag_ref[i, near, :] * v - total


def apply_kernel(tall, u_ref, diag_ref, cz_ref, cs_ref, ce_ref, w_ref):
    z, y, _ = diag_ref.shape

    def step(t, carry):
        at = pl.multiple_of(t * tall, 8)
        for i in range(z):
            w_ref[i, pl.ds(at, tall), :] = apply_inner(u_ref, diag_ref, cz_ref, cs_ref, ce_ref, i, at, tall)[1]
        return carry

    lax.fori_loop(0, y // tall, step, 0)


def subtract_halos(w_ref, halos, cy_ref, czh_ref):
    hx, hy, hz = halos
    z, y, _ = w_ref.shape
    for n, ref in enumerate(hz):
        p = jnp.where(low_side("gz", n), 0, z - 1)
        w_ref[p] = w_ref[p] - czh_ref[n] * ref[...]
    for n, ref in enumerate(hy):
        at = pl.ds(pl.multiple_of(jnp.where(low_side("gy", n), 0, y - 8), 8), 8)
        for i in range(z):
            w_ref[i, at, :] = w_ref[i, at, :] - cy_ref[n, i] * ref[i : i + 1, :]


def smooth_kernel(rounds, tall, *refs):
    (w_in, diag_ref, cs_ref, ce_ref, cx_ref, cy_ref, czh_ref, lev_in), refs = refs[:8], refs[8:]
    halos, refs = regroup(refs, rounds)
    (w_ref, m_ref), refs = refs[:2], refs[2:]
    sends, (lev_ref, sems) = regroup(refs, rounds)
    z, y, _ = w_ref.shape
    table = start_all((lev_in,), (lev_ref,), sems)
    subtract_halos(w_in, halos, cy_ref, czh_ref)
    xlo, xhi = column_halos(halos[0])
    flux = stage_columns(cx_ref[0] * xlo, cx_ref[1] * xhi)
    edge = edge_lanes()
    clear_margins(m_ref)
    per = y // 8
    for i in range(z * per):
        at = (i // per, slice(8 * (i % per), 8 * (i % per) + 8))
        w = w_in[at] - spread_columns(flux, edge, i)
        w_ref[at] = w
        m_ref[i // per, 8 + 8 * (i % per) : 16 + 8 * (i % per)] = w * (damping / diag_ref[at])
    table[0].wait()
    sweeps(m_ref, diag_ref, cs_ref, ce_ref, lev_ref, tall)
    tier, row, vreg = padded_access(m_ref)
    fill_sends(tier, row, sends, None, pack_columns(vreg, z * per), z, y)


def fold(product):
    return jnp.sum(product.reshape(-1, 8, 128), axis=0)


def sums_kernel(tall, m_ref, u_ref, r_ref, w_ref, diag_ref, cz_ref, cs_ref, ce_ref, n_ref, sum_ref):
    z, y, _ = diag_ref.shape

    def step(t, carry):
        gamma, delta, cross = carry
        at = pl.multiple_of(t * tall, 8)
        near = pl.ds(at, tall)
        for i in range(z):
            m, n_ref[i, near, :] = apply_inner(m_ref, diag_ref, cz_ref, cs_ref, ce_ref, i, at, tall)
            u = u_ref[i, pl.ds(at + 8, tall), :]
            w = w_ref[i, near, :]
            gamma = gamma + fold(r_ref[i, near, :] * u)
            delta = delta + fold(w * u)
            cross = cross + fold(w * m)
        return gamma, delta, cross

    zero = jnp.zeros((8, 128), F32)
    for n, value in enumerate(lax.fori_loop(0, y // tall, step, (zero, zero, zero))):
        sum_ref[n] = value


def finish_kernel(rounds, *refs):
    (n_in, m_ref, sum_ref, cx_ref, cy_ref, czh_ref), refs = refs[:6], refs[6:]
    halos, (n_ref, out_ref) = regroup(refs, rounds)
    z, y, _ = n_ref.shape
    subtract_halos(n_in, halos, cy_ref, czh_ref)
    xlo, xhi = column_halos(halos[0])
    flux = stage_columns(cx_ref[0] * xlo, cx_ref[1] * xhi)
    edge = edge_lanes()
    per = y // 8
    parts = [jnp.zeros((8, 128), F32) for _ in range(8)]
    for i in range(z * per):
        at = (i // per, slice(8 * (i % per), 8 * (i % per) + 8))
        n = n_in[at] - spread_columns(flux, edge, i)
        n_ref[at] = n
        parts[i % 8] = parts[i % 8] + n * m_ref[i // per, 8 + 8 * (i % per) : 16 + 8 * (i % per)]
    while len(parts) > 1:
        parts = [a + b for a, b in zip(parts[::2], parts[1::2])]
    parts = [sum_ref[0], sum_ref[1], sum_ref[2], parts[0]]
    parts = jnp.concatenate([jnp.sum(p, axis=0, keepdims=True) for p in parts], 0)
    for d in range(out_ref.shape[0]):
        out_ref[d] = parts


def update_kernel(all_ref, x_ref, r_ref, u_ref, w_ref, m_ref, n_ref, x_out, r_out, xo_ref, ro_ref, sems):
    sums = jnp.sum(all_ref[...], axis=0)
    gamma, delta, cross, last = (sums[i : i + 1] for i in range(4))

    def total(v):
        return jnp.sum(v, axis=1, keepdims=True)

    gamma0 = total(gamma)
    alpha0 = gamma0 / total(delta)
    gamma1 = total(gamma - 2.0 * alpha0 * delta + alpha0 * alpha0 * cross)
    delta1 = total(delta - 2.0 * alpha0 * cross + alpha0 * alpha0 * last)
    beta = gamma1 / gamma0
    alpha1 = gamma1 / (delta1 - beta * gamma1 / alpha0)
    near = alpha0 + alpha1 * (1.0 + beta)
    far = alpha1 * alpha0
    z, y, _ = r_ref.shape
    copies = []
    for i in range(z):
        inner = (i, slice(8, 8 + y))
        xo_ref[i] = x_ref[inner] + near * u_ref[inner] - far * m_ref[inner]
        ro_ref[i] = r_ref[i] - near * w_ref[i] + far * n_ref[i]
        copies += start_all((xo_ref.at[i], ro_ref.at[i]), (x_out.at[i], r_out.at[i]), sems.at[i])
    for copy in copies:
        copy.wait()


def swap_pairs(axis, start):
    count = lax.axis_size(axis)
    pairs = []
    for i in range(start, count - 1, 2):
        pairs += [(i, i + 1), (i + 1, i)]
    return pairs


def body(
    earlier_warmth_field,
    caloric_storage,
    thermal_diffusivity_coefficient,
    dissipation_catalog,
    dissipation_selector,
    refine_depth,
    border_band_width,
    microflow_flag,
):
    z, y, x = earlier_warmth_field.shape
    tall = dissipation_catalog.shape[1]
    groups = -(-(z * y // 8) // 128)
    rounds = tuple(2 if lax.axis_size(axis) > 2 else 1 for axis in GRID_AXES)
    sends = sum(rounds)
    shape = lambda *s: pltpu.VMEM(s, F32)
    full = shape(z, y, x)
    tall_field = shape(z, y + 16, x)

    hbm = pl.BlockSpec(memory_space=pltpu.HBM)

    def call(kernel, outs, ins, name, scratch=(), out_specs=None, alias=None, outer=()):
        specs = [hbm if n in outer else VMEM for n in range(len(ins))]
        ins = [pltpu.with_memory_space_constraint(v, pltpu.HBM) if n in outer else v for n, v in enumerate(ins)]
        return pl.pallas_call(
            kernel,
            out_shape=outs,
            in_specs=specs,
            out_specs=out_specs or [VMEM] * len(outs),
            scratch_shapes=list(scratch),
            input_output_aliases=alias or {},
            name=name,
            compiler_params=pltpu.CompilerParams(vmem_limit_bytes=16 * 2**20),
        )(*ins)

    def face_shapes(front):
        out = []
        for axis, n in zip(((8 * groups, x), (z, x), (y, x)), rounds):
            out += [shape(*front, *axis)] * n
        return out

    def swap(faces):
        faces, got = list(faces), []
        for axis, n in zip(GRID_AXES, rounds):
            for start in range(n):
                got.append(lax.ppermute(faces.pop(0), axis, swap_pairs(axis, start)))
        return got

    selector = jnp.swapaxes(dissipation_selector, 1, 2)
    levels = jnp.swapaxes(refine_depth, 1, 2)
    width = jnp.swapaxes(border_band_width, 0, 1)

    def table(v):
        return pltpu.SMEM(v.shape, v.dtype)

    outs = call(
        functools.partial(faces_kernel, rounds),
        [tall_field, tall_field] + face_shapes((2,)) + [shape(2, 2, 8 * groups, x)],
        [earlier_warmth_field, thermal_diffusivity_coefficient],
        "faces",
        [pltpu.SemaphoreType.DMA((2, z))],
        outer=(0, 1),
    )
    (field, kappa), outs = outs[:2], outs[2:]
    own, halos = outs[sends], swap(outs[:sends])
    r, diag, cz, cs, ce = call(
        functools.partial(inner_kernel, tall),
        [full, full, shape(max(z - 1, 1), y, x), shape(z, y + 8, x), full],
        [field, kappa, caloric_storage, dissipation_catalog, selector, width, microflow_flag],
        "inner",
        [table(selector), table(width), table(microflow_flag), pltpu.SemaphoreType.DMA((3,))],
        outer=(4, 5, 6),
    )
    outs = call(
        functools.partial(border_kernel, rounds, tall),
        [full, full, tall_field, shape(2, 8 * groups, x), shape(rounds[1], z, 8, x), shape(rounds[2], y, x)]
        + face_shapes(()),
        [field, kappa, own, r, diag, cs, ce, levels] + halos,
        "border",
        [table(levels), pltpu.SemaphoreType.DMA((1,))],
        alias={3: 0, 4: 1},
        outer=(7,),
    )
    r, diag, u, cx, cy, czh = outs[:6]
    halos = swap(outs[6:])
    (w,) = call(functools.partial(apply_kernel, tall), [full], [u, diag, cz, cs, ce], "apply")
    outs = call(
        functools.partial(smooth_kernel, rounds, tall),
        [full, tall_field] + face_shapes(()),
        [w, diag, cs, ce, cx, cy, czh, levels] + halos,
        "smooth",
        [table(levels), pltpu.SemaphoreType.DMA((1,))],
        alias={0: 0},
        outer=(7,),
    )
    w, m = outs[:2]
    halos = swap(outs[2:])
    n, sums = call(
        functools.partial(sums_kernel, tall), [full, shape(3, 8, 128)], [m, u, r, w, diag, cz, cs, ce], "sums"
    )
    members = math.prod(lax.axis_size(axis) for axis in GRID_AXES)
    n, parts = call(
        functools.partial(finish_kernel, rounds),
        [full, shape(members, 4, 128)],
        [n, m, sums, cx, cy, czh] + halos,
        "finish",
        alias={0: 0},
    )
    every = lax.all_to_all(parts, GRID_AXES, 0, 0, tiled=True)
    return tuple(
        call(
            update_kernel,
            [jax.ShapeDtypeStruct((z, y, x), F32)] * 2,
            [every, field, r, u, w, m, n],
            "update",
            [full, full, pltpu.SemaphoreType.DMA((z, 2))],
            out_specs=[hbm, hbm],
        )
    )


def solution(mesh):
    cells = P(("groups", "gz"), "gy", "gx")
    return jax.shard_map(
        body,
        mesh=mesh,
        in_specs=(
            cells,
            cells,
            cells,
            P("groups", None, None),
            cells,
            cells,
            P(("groups", "gy"), "gx"),
            P(("groups", "gz")),
        ),
        out_specs=(cells, cells),
        check_vma=False,
    )
```

```python
import functools
import math

import jax
import jax.numpy as jnp
from jax import lax
from jax.experimental import pallas as pl
from jax.experimental.pallas import tpu as pltpu
from jax.sharding import PartitionSpec as P

interval_increment = 0.5
vertical_ratio = 2.0
coolant_film = 1.5
band_sink = 1.0
damping = 0.8
GRID_AXES = ("gx", "gy", "gz")
VMEM = pl.BlockSpec(memory_space=pltpu.VMEM)
F32 = jnp.float32


def harmonic(first, second):
    return 2.0 * first * second / (first + second)


def lanes(shape=(8, 128)):
    return lax.broadcasted_iota(jnp.int32, shape, len(shape) - 1)


def rows(shape):
    return lax.broadcasted_iota(jnp.int32, shape, 0)


def low_side(axis, turn):
    odd = lax.rem(lax.axis_index(axis), 2) == 1
    return ~odd if turn else odd


def regroup(refs, counts):
    out, at = [], 0
    for c in counts:
        out.append(refs[at : at + c])
        at += c
    return out, refs[at:]


def pack_columns(load, count):
    lane = lanes()
    firsts, lasts = [], []
    for start in range(0, count, 128):
        parts = [jnp.zeros((8, 128), F32), jnp.zeros((8, 128), F32)]
        for i in range(min(128, count - start)):
            turned = load(start + i)
            if i:
                turned = pltpu.roll(turned, i, 1)
            here = (lane == i) | (lane == (i + 127) % 128)
            parts[i % 2] = jnp.where(here, turned, parts[i % 2])
        even = lane % 2 == 0
        firsts.append(jnp.where(even, parts[0], parts[1]))
        lasts.append(pltpu.roll(jnp.where(even, parts[1], parts[0]), 1, 1))
    return jnp.concatenate(firsts, 0), jnp.concatenate(lasts, 0)


def stage_columns(first, last):
    even = lanes() % 2 == 0
    out = []
    for g in range(first.shape[0] // 8):
        f = first[8 * g : 8 * g + 8]
        l = pltpu.roll(last[8 * g : 8 * g + 8], 127, 1)
        out.append((jnp.where(even, f, l), jnp.where(even, l, f)))
    return out


def spread_columns(staged, edge, i):
    turned = staged[i // 128][i % 2]
    if i % 128:
        turned = pltpu.roll(turned, 128 - i % 128, 1)
    return jnp.where(edge, turned, 0.0)


def edge_lanes():
    lane = lanes()
    return (lane == 0) | (lane == 127)


def column_halos(refs, slot=()):
    low = low_side("gx", 0)
    got = [ref[slot] if slot else ref[...] for ref in refs]
    if len(got) == 1:
        got.append(jnp.zeros_like(got[0]))
    return jnp.where(low, got[0], got[1]), jnp.where(low, got[1], got[0])


def fill_sends(tier, row, send_refs, slot, columns, z, y):
    for axis, refs in zip(GRID_AXES, send_refs):
        for n, ref in enumerate(refs):
            low = low_side(axis, n)
            if axis == "gx":
                value = jnp.where(low, columns[0], columns[1])
            elif axis == "gy":
                value = jnp.where(low, row(0), row(y - 1))
            else:
                value = tier(jnp.where(low, 0, z - 1))
            if slot is None:
                ref[...] = value
            else:
                ref[slot] = value


def padded_access(ref):
    y = ref.shape[1] - 16

    def tier(i):
        return ref[i, pl.ds(8, y), :]

    def row(r):
        return ref[:, 8 + r, :]

    def vreg(i):
        return ref[i // (y // 8), 8 + 8 * (i % (y // 8)) : 16 + 8 * (i % (y // 8)), :]

    return tier, row, vreg


def clear_margins(ref):
    z, y, _ = ref.shape
    for i in range(z):
        ref[i, 0:8, :] = jnp.zeros((8, 128), F32)
        ref[i, y - 8 : y, :] = jnp.zeros((8, 128), F32)


def start_all(sources, targets, sems):
    copies = [pltpu.make_async_copy(a, b, sems.at[n]) for n, (a, b) in enumerate(zip(sources, targets))]
    for copy in copies:
        copy.start()
    return copies


def faces_kernel(rounds, x_in, k_in, x_ref, k_ref, *refs):
    sends, (own_ref, sems) = regroup(refs, rounds)
    z, y, _ = x_in.shape
    per = y // 8
    fields = (x_ref, k_ref)
    copies = [
        start_all([source.at[i] for i in range(z)], [ref.at[i, pl.ds(8, y), :] for i in range(z)], sems.at[n])
        for n, (source, ref) in enumerate(zip((x_in, k_in), fields))
    ]
    for slot, ref in enumerate(fields):
        clear_margins(ref)
        tier, row, vreg = padded_access(ref)

        def load(i):
            if i % per == 0:
                copies[slot][i // per].wait()
            return vreg(i)

        columns = pack_columns(load, z * per)
        own_ref[slot, 0] = columns[0]
        own_ref[slot, 1] = columns[1]
        fill_sends(tier, row, sends, slot, columns, z, y)


def inner_kernel(tall, x_ref, k_ref, c_ref, cat_ref, sel_in, band_in, flow_in, *refs):
    r_ref, diag_ref, cz_ref, cs_ref, ce_ref, sel_ref, band_ref, flow_ref, sems = refs
    z, y, _ = c_ref.shape
    copies = start_all((sel_in, band_in, flow_in), (sel_ref, band_ref, flow_ref), sems)
    lane = lanes((tall, 128))
    row = rows((tall, 128))
    for i in range(z):
        cs_ref[i, 0:8, :] = jnp.zeros((8, 128), F32)

    def faces(t, carry):
        at = pl.multiple_of(t * tall, 8)
        last = jnp.where(t == y // tall - 1, tall - 1, tall)
        for i in range(z):
            here = k_ref[i, pl.ds(at + 8, tall), :]
            south = harmonic(here, k_ref[i, pl.ds(at + 9, tall), :])
            cs_ref[i, pl.ds(at + 8, tall), :] = jnp.where(row == last, 0.0, south)
            ce_ref[i, pl.ds(at, tall), :] = jnp.where(lane == 127, 0.0, harmonic(here, pltpu.roll(here, 127, 1)))
            if i + 1 < z:
                above = k_ref[i + 1, pl.ds(at + 8, tall), :]
                cz_ref[i, pl.ds(at, tall), :] = vertical_ratio * harmonic(here, above)
        return carry

    lax.fori_loop(0, y // tall, faces, 0)
    for copy in copies:
        copy.wait()

    def rest(t, carry):
        at = pl.multiple_of(t * tall, 8)
        near = pl.ds(at, tall)
        mid = pl.ds(at + 8, tall)
        width = band_ref[0, t]
        band = jnp.where((row < width) | (row >= tall - width), band_sink, 0.0)
        for i in range(z):
            x = x_ref[i, mid, :]
            sink = coolant_film * flow_ref[i].astype(F32) + band
            cn = cs_ref[i, pl.ds(at + 7, tall), :]
            cs = cs_ref[i, mid, :]
            ce = ce_ref[i, near, :]
            cw = pltpu.roll(ce, 1, 1)
            r = cat_ref[sel_ref[i, 0, t]] - sink * x
            r = r + cn * (x_ref[i, pl.ds(at + 7, tall), :] - x) + cs * (x_ref[i, pl.ds(at + 9, tall), :] - x)
            r = r + ce * (pltpu.roll(x, 127, 1) - x) + cw * (pltpu.roll(x, 1, 1) - x)
            diag = c_ref[i, near, :] * (1.0 / interval_increment) + sink
            diag = diag + ((cn + cs) + (ce + cw))
            if i:
                cd = cz_ref[i - 1, near, :]
                diag = diag + cd
                r = r + cd * (x_ref[i - 1, mid, :] - x)
            if i + 1 < z:
                cu = cz_ref[i, near, :]
                diag = diag + cu
                r = r + cu * (x_ref[i + 1, mid, :] - x)
            diag_ref[i, near, :] = diag
            r_ref[i, near, :] = r
        return carry

    lax.fori_loop(0, y // tall, rest, 0)


def sweeps(field_ref, diag_ref, cs_ref, ce_ref, lev_ref, tall):
    z, y, _ = diag_ref.shape
    tiles = y // tall
    row = rows((tall, 128))

    def tile(i, t):
        level = lev_ref[i, 0, t]

        @pl.when(level > 1)
        def _():
            at = pl.multiple_of(t * tall, 8)
            mid = pl.ds(at + 8, tall)
            start = field_ref[i, mid, :]
            weight = damping / diag_ref[i, pl.ds(at, tall), :]
            north = jnp.where(row == 0, 0.0, cs_ref[i, pl.ds(at + 7, tall), :])
            south = jnp.where(row == tall - 1, 0.0, cs_ref[i, mid, :])
            east = ce_ref[i, pl.ds(at, tall), :]

            def once(_, state):
                inner = north * pltpu.roll(state, 1, 0) + south * pltpu.roll(state, tall - 1, 0)
                inner = inner + east * pltpu.roll(state, 127, 1) + pltpu.roll(east * state, 1, 1)
                return (1.0 - damping) * state + (start + weight * inner)

            field_ref[i, mid, :] = lax.fori_loop(1, jnp.minimum(level, 4), once, start)

    def tier(i, carry):
        def step(t, carry):
            tile(i, t)
            return carry

        return lax.fori_loop(0, tiles, step, carry)

    lax.fori_loop(0, z, tier, 0)


def border_kernel(rounds, tall, *refs):
    (x_ref, k_ref, own_ref, r_in, diag_in, cs_ref, ce_ref, lev_in), refs = refs[:8], refs[8:]
    (hx, hy, hz), refs = regroup(refs, rounds)
    (r_ref, diag_ref, u_ref, cx_ref, cy_ref, czh_ref), refs = refs[:6], refs[6:]
    sends, (lev_ref, sems) = regroup(refs, rounds)
    z, y, _ = r_ref.shape
    table = start_all((lev_in,), (lev_ref,), sems)
    for n, ref in enumerate(hz):
        p = jnp.where(low_side("gz", n), 0, z - 1)
        face = vertical_ratio * harmonic(k_ref[p, pl.ds(8, y), :], ref[1])
        czh_ref[n] = face
        diag_in[p] = diag_in[p] + face
        r_in[p] = r_in[p] + face * (ref[0] - x_ref[p, pl.ds(8, y), :])
    row8 = rows((8, 128))
    for n, ref in enumerate(hy):
        low = low_side("gy", n)
        at = pl.multiple_of(jnp.where(low, 0, y - 8), 8)
        mask = row8 == jnp.where(low, 0, 7)
        for i in range(z):
            there = pl.ds(at, 8)
            inside = pl.ds(at + 8, 8)
            face = harmonic(k_ref[i, inside, :], ref[1, i : i + 1, :])
            face = jnp.where(mask, face, 0.0)
            cy_ref[n, i : i + 1, :] = jnp.sum(face, axis=0, keepdims=True)
            diag_in[i, there, :] = diag_in[i, there, :] + face
            r_in[i, there, :] = r_in[i, there, :] + face * (ref[0, i : i + 1, :] - x_ref[i, inside, :])
    xlo, xhi = column_halos(hx, (0,))
    klo, khi = column_halos(hx, (1,))
    west = harmonic(own_ref[1, 0], klo)
    east = harmonic(own_ref[1, 1], khi)
    cx_ref[0] = west
    cx_ref[1] = east
    faces = stage_columns(west, east)
    flux = stage_columns(west * (xlo - own_ref[0, 0]), east * (xhi - own_ref[0, 1]))
    edge = edge_lanes()
    clear_margins(u_ref)
    per = y // 8
    for i in range(z * per):
        at = (i // per, slice(8 * (i % per), 8 * (i % per) + 8))
        diag = diag_in[at] + spread_columns(faces, edge, i)
        r = r_in[at] + spread_columns(flux, edge, i)
        diag_ref[at] = diag
        r_ref[at] = r
        u_ref[i // per, 8 + 8 * (i % per) : 16 + 8 * (i % per)] = r * (damping / diag)
    table[0].wait()
    sweeps(u_ref, diag_ref, cs_ref, ce_ref, lev_ref, tall)
    tier, row, vreg = padded_access(u_ref)
    fill_sends(tier, row, sends, None, pack_columns(vreg, z * per), z, y)


def apply_inner(field_ref, diag_ref, cz_ref, cs_ref, ce_ref, i, at, tall):
    z = diag_ref.shape[0]
    near = pl.ds(at, tall)
    mid = pl.ds(at + 8, tall)
    v = field_ref[i, mid, :]
    ce = ce_ref[i, near, :]
    total = cs_ref[i, pl.ds(at + 7, tall), :] * field_ref[i, pl.ds(at + 7, tall), :]
    total = total + cs_ref[i, mid, :] * field_ref[i, pl.ds(at + 9, tall), :]
    total = total + (ce * pltpu.roll(v, 127, 1) + pltpu.roll(ce * v, 1, 1))
    if i:
        total = total + cz_ref[i - 1, near, :] * field_ref[i - 1, mid, :]
    if i + 1 < z:
        total = total + cz_ref[i, near, :] * field_ref[i + 1, mid, :]
    return v, diag_ref[i, near, :] * v - total


def apply_kernel(tall, u_ref, diag_ref, cz_ref, cs_ref, ce_ref, w_ref):
    z, y, _ = diag_ref.shape

    def step(t, carry):
        at = pl.multiple_of(t * tall, 8)
        for i in range(z):
            w_ref[i, pl.ds(at, tall), :] = apply_inner(u_ref, diag_ref, cz_ref, cs_ref, ce_ref, i, at, tall)[1]
        return carry

    lax.fori_loop(0, y // tall, step, 0)


def subtract_tiers(w_ref, halos, czh_ref):
    for n, ref in enumerate(halos):
        p = jnp.where(low_side("gz", n), 0, w_ref.shape[0] - 1)
        w_ref[p] = w_ref[p] - czh_ref[n] * ref[...]


def border_rows(n, y):
    low = low_side("gy", n)
    at = pl.ds(pl.multiple_of(jnp.where(low, 0, y - 8), 8), 8)
    return at, rows((8, 128)) == jnp.where(low, 0, 7)


def smooth_kernel(rounds, tall, *refs):
    (w_in, diag_ref, cs_ref, ce_ref, cx_ref, cy_ref, czh_ref, lev_in), refs = refs[:8], refs[8:]
    halos, refs = regroup(refs, rounds)
    w_ref, m_ref, face_ref, *send_refs, lev_ref, sems = refs
    z, y, _ = w_ref.shape
    table = start_all((lev_in,), (lev_ref,), sems)
    subtract_tiers(w_in, halos[2], czh_ref)
    for n, ref in enumerate(halos[1]):
        at, mask = border_rows(n, y)
        for i in range(z):
            w_in[i, at, :] = w_in[i, at, :] - jnp.where(mask, cy_ref[n, i : i + 1, :] * ref[i : i + 1, :], 0.0)
    xlo, xhi = column_halos(halos[0])
    flux = stage_columns(cx_ref[0] * xlo, cx_ref[1] * xhi)
    edge = edge_lanes()
    clear_margins(m_ref)
    per = y // 8
    for i in range(z * per):
        at = (i // per, slice(8 * (i % per), 8 * (i % per) + 8))
        w = w_in[at] - spread_columns(flux, edge, i)
        w_ref[at] = w
        m_ref[i // per, 8 + 8 * (i % per) : 16 + 8 * (i % per)] = w * (damping / diag_ref[at])
    table[0].wait()
    sweeps(m_ref, diag_ref, cs_ref, ce_ref, lev_ref, tall)
    tier, row, vreg = padded_access(m_ref)
    for n, ref in enumerate(send_refs):
        ref[...] = tier(jnp.where(low_side("gz", n), 0, z - 1))
    first, last = pack_columns(vreg, z * per)
    plan, _ = face_plan(z, first.shape[0], rounds)
    low = low_side("gy", 0)
    if rounds[1] == 1:
        face_ref[plan["y_low"]] = jnp.where(low, cy_ref[0] * row(0), row(y - 1))
    else:
        face_ref[plan["y_low"]] = jnp.where(low, cy_ref[0], cy_ref[1]) * row(0)
        face_ref[plan["y_high"]] = row(y - 1)
    face_ref[plan["x_low"]] = cx_ref[0] * first
    face_ref[plan["x_high"]] = last
    face_ref[plan["sums"]] = jnp.zeros((4, 128), F32)


def face_plan(z, packed, rounds):
    plan, at = {}, 0
    parts = (("sums", 4), ("y_low", z), ("x_low", packed), ("x_high", packed), ("y_high", z))
    for name, count in parts[: 4 if rounds[1] == 1 else 5]:
        plan[name] = slice(at, at + count)
        at += count
    return plan, at


def fold(product):
    return jnp.sum(product.reshape(-1, 8, 128), axis=0)


def sums_kernel(tall, m_ref, u_ref, r_ref, w_ref, diag_ref, cz_ref, cs_ref, ce_ref, n_ref, sum_ref):
    z, y, _ = diag_ref.shape

    def step(t, carry):
        gamma, delta, cross, last = carry
        at = pl.multiple_of(t * tall, 8)
        near = pl.ds(at, tall)
        for i in range(z):
            m, n = apply_inner(m_ref, diag_ref, cz_ref, cs_ref, ce_ref, i, at, tall)
            n_ref[i, near, :] = n
            u = u_ref[i, pl.ds(at + 8, tall), :]
            w = w_ref[i, near, :]
            gamma = gamma + fold(r_ref[i, near, :] * u)
            delta = delta + fold(w * u)
            cross = cross + fold(w * m)
            last = last + fold(n * m)
        return gamma, delta, cross, last

    zero = jnp.zeros((8, 128), F32)
    for n, value in enumerate(lax.fori_loop(0, y // tall, step, (zero,) * 4)):
        sum_ref[n] = value


def finish_kernel(rounds, *refs):
    (n_in, m_ref, sum_ref, czh_ref, face_ref), refs = refs[:5], refs[5:]
    (halos,), (n_ref, out_ref) = regroup(refs, rounds[2:])
    z, y, _ = n_ref.shape
    last = sum_ref[3]
    for n, ref in enumerate(halos):
        p = jnp.where(low_side("gz", n), 0, z - 1)
        flux = czh_ref[n] * ref[...]
        n_ref[p] = n_in[p] - flux
        last = last - fold(flux * m_ref[p, pl.ds(8, y), :])
    parts = [sum_ref[0], sum_ref[1], sum_ref[2], last]
    parts = [jnp.sum(p, axis=0, keepdims=True) for p in parts]
    height = face_ref.shape[0]
    everything = jnp.concatenate(parts + [face_ref[4:height]], 0)
    for d in range(out_ref.shape[0]):
        out_ref[d] = everything


def update_kernel(rounds, sizes, *refs):
    all_ref, x_ref, r_ref, u_ref, w_ref, m_ref, n_ref, cx_ref, cy_ref, x_out, r_out, xo_ref, ro_ref, sems = refs
    z, y, _ = r_ref.shape
    packed = cx_ref.shape[1]
    plan, _ = face_plan(z, packed, rounds)
    nx, ny, nz = sizes
    members = nx * ny * nz
    y_high = plan["y_low" if rounds[1] == 1 else "y_high"]

    def tree(values):
        while len(values) > 1:
            values = [a + b for a, b in zip(values[::2], values[1::2])] + values[len(values) // 2 * 2 :]
        return values[0]

    sums = tree([all_ref[d, plan["sums"], :] for d in range(members)])
    gamma, delta, cross, last = (sums[i : i + 1] for i in range(4))
    links = []
    for d in range(members - ny * nz):
        links.append(all_ref[d, plan["x_high"], :] * all_ref[d + ny * nz, plan["x_low"], :])
    if links:
        last = last - 2.0 * jnp.sum(tree(links), axis=0, keepdims=True)
    links = []
    for d in range(members - nz):
        if d // nz % ny + 1 < ny:
            links.append(all_ref[d, y_high, :] * all_ref[d + nz, plan["y_low"], :])
    if links:
        last = last - 2.0 * jnp.sum(tree(links), axis=0, keepdims=True)

    def total(v):
        return jnp.sum(v, axis=1, keepdims=True)

    gamma0 = total(gamma)
    alpha0 = gamma0 / total(delta)
    gamma1 = total(gamma - 2.0 * alpha0 * delta + alpha0 * alpha0 * cross)
    delta1 = total(delta - 2.0 * alpha0 * cross + alpha0 * alpha0 * last)
    beta = gamma1 / gamma0
    alpha1 = gamma1 / (delta1 - beta * gamma1 / alpha0)
    near = alpha0 + alpha1 * (1.0 + beta)
    far = alpha1 * alpha0

    gx, gy, gz = (lax.axis_index(axis) for axis in GRID_AXES)
    me = (gx * ny + gy) * nz + gz
    left = jnp.maximum(me - ny * nz, 0)
    right = jnp.minimum(me + ny * nz, members - 1)
    has_right = gx < nx - 1
    west = far * (cx_ref[0] * all_ref[left, plan["x_high"], :])
    east = far * jnp.where(has_right, all_ref[right, plan["x_low"], :], 0.0)
    flux = stage_columns(west, east)
    below = jnp.maximum(me - nz, 0)
    above = jnp.minimum(me + nz, members - 1)
    row_flux = []
    for n in range(rounds[1]):
        low = low_side("gy", n)
        from_below = cy_ref[n] * all_ref[below, y_high, :]
        from_above = jnp.where(gy < ny - 1, all_ref[above, plan["y_low"], :], 0.0)
        row_flux.append(far * jnp.where(low, from_below, from_above))
    edge = edge_lanes()
    per = y // 8
    copies = []
    for i in range(z):
        inner = (i, slice(8, 8 + y))
        for j in range(per):
            at = (i, slice(8 * j, 8 * j + 8))
            ro_ref[at] = r_ref[at] - near * w_ref[at] + (far * n_ref[at] - spread_columns(flux, edge, i * per + j))
        for n in range(rounds[1]):
            at, mask = border_rows(n, y)
            ro_ref[i, at, :] = ro_ref[i, at, :] - jnp.where(mask, row_flux[n][i : i + 1], 0.0)
        copies += start_all((ro_ref.at[i],), (r_out.at[i],), sems.at[0, i : i + 1])
        xo_ref[i] = x_ref[inner] + near * u_ref[inner] - far * m_ref[inner]
        copies += start_all((xo_ref.at[i],), (x_out.at[i],), sems.at[1, i : i + 1])
    for copy in copies:
        copy.wait()


def swap_pairs(axis, start):
    count = lax.axis_size(axis)
    pairs = []
    for i in range(start, count - 1, 2):
        pairs += [(i, i + 1), (i + 1, i)]
    return pairs


def body(
    earlier_warmth_field,
    caloric_storage,
    thermal_diffusivity_coefficient,
    dissipation_catalog,
    dissipation_selector,
    refine_depth,
    border_band_width,
    microflow_flag,
):
    z, y, x = earlier_warmth_field.shape
    tall = dissipation_catalog.shape[1]
    groups = -(-(z * y // 8) // 128)
    rounds = tuple(2 if lax.axis_size(axis) > 2 else 1 for axis in GRID_AXES)
    sends = sum(rounds)
    shape = lambda *s: pltpu.VMEM(s, F32)
    full = shape(z, y, x)
    tall_field = shape(z, y + 16, x)
    _, height = face_plan(z, 8 * groups, rounds)

    hbm = pl.BlockSpec(memory_space=pltpu.HBM)

    def call(kernel, outs, ins, name, scratch=(), out_specs=None, alias=None, outer=()):
        specs = [hbm if n in outer else VMEM for n in range(len(ins))]
        ins = [pltpu.with_memory_space_constraint(v, pltpu.HBM) if n in outer else v for n, v in enumerate(ins)]
        return pl.pallas_call(
            kernel,
            out_shape=outs,
            in_specs=specs,
            out_specs=out_specs or [VMEM] * len(outs),
            scratch_shapes=list(scratch),
            input_output_aliases=alias or {},
            name=name,
            compiler_params=pltpu.CompilerParams(vmem_limit_bytes=16 * 2**20),
        )(*ins)

    def face_shapes(front):
        out = []
        for axis, n in zip(((8 * groups, x), (z, x), (y, x)), rounds):
            out += [shape(*front, *axis)] * n
        return out

    def swap(faces, axes=GRID_AXES):
        faces, got = list(faces), []
        for axis in axes:
            for start in range(rounds[GRID_AXES.index(axis)]):
                got.append(lax.ppermute(faces.pop(0), axis, swap_pairs(axis, start)))
        return got

    selector = jnp.swapaxes(dissipation_selector, 1, 2)
    levels = jnp.swapaxes(refine_depth, 1, 2)
    width = jnp.swapaxes(border_band_width, 0, 1)

    def table(v):
        return pltpu.SMEM(v.shape, v.dtype)

    outs = call(
        functools.partial(faces_kernel, rounds),
        [tall_field, tall_field] + face_shapes((2,)) + [shape(2, 2, 8 * groups, x)],
        [earlier_warmth_field, thermal_diffusivity_coefficient],
        "faces",
        [pltpu.SemaphoreType.DMA((2, z))],
        outer=(0, 1),
    )
    (field, kappa), outs = outs[:2], outs[2:]
    own, halos = outs[sends], swap(outs[:sends])
    r, diag, cz, cs, ce = call(
        functools.partial(inner_kernel, tall),
        [full, full, shape(max(z - 1, 1), y, x), shape(z, y + 8, x), full],
        [field, kappa, caloric_storage, dissipation_catalog, selector, width, microflow_flag],
        "inner",
        [table(selector), table(width), table(microflow_flag), pltpu.SemaphoreType.DMA((3,))],
        outer=(4, 5, 6),
    )
    outs = call(
        functools.partial(border_kernel, rounds, tall),
        [full, full, tall_field, shape(2, 8 * groups, x), shape(rounds[1], z, x), shape(rounds[2], y, x)]
        + face_shapes(()),
        [field, kappa, own, r, diag, cs, ce, levels] + halos,
        "border",
        [table(levels), pltpu.SemaphoreType.DMA((1,))],
        alias={3: 0, 4: 1},
        outer=(7,),
    )
    r, diag, u, cx, cy, czh = outs[:6]
    halos = swap(outs[6:])
    (w,) = call(functools.partial(apply_kernel, tall), [full], [u, diag, cz, cs, ce], "apply")
    outs = call(
        functools.partial(smooth_kernel, rounds, tall),
        [full, tall_field, shape(height, x)] + [shape(y, x)] * rounds[2],
        [w, diag, cs, ce, cx, cy, czh, levels] + halos,
        "smooth",
        [table(levels), pltpu.SemaphoreType.DMA((1,))],
        alias={0: 0},
        outer=(7,),
    )
    w, m, faces = outs[:3]
    halos = swap(outs[3:], GRID_AXES[2:])
    n, sums = call(
        functools.partial(sums_kernel, tall), [full, shape(4, 8, 128)], [m, u, r, w, diag, cz, cs, ce], "sums"
    )
    sizes = tuple(lax.axis_size(axis) for axis in GRID_AXES)
    n, parts = call(
        functools.partial(finish_kernel, rounds),
        [full, shape(math.prod(sizes), height, x)],
        [n, m, sums, czh, faces] + halos,
        "finish",
        alias={0: 0},
    )
    every = lax.all_to_all(parts, GRID_AXES, 0, 0, tiled=True)
    return tuple(
        call(
            functools.partial(update_kernel, rounds, sizes),
            [jax.ShapeDtypeStruct((z, y, x), F32)] * 2,
            [every, field, r, u, w, m, n, cx, cy],
            "update",
            [full, full, pltpu.SemaphoreType.DMA((2, z))],
            out_specs=[hbm, hbm],
        )
    )


def solution(mesh):
    cells = P(("groups", "gz"), "gy", "gx")
    return jax.shard_map(
        body,
        mesh=mesh,
        in_specs=(
            cells,
            cells,
            cells,
            P("groups", None, None),
            cells,
            cells,
            P(("groups", "gy"), "gx"),
            P(("groups", "gz")),
        ),
        out_specs=(cells, cells),
        check_vma=False,
    )
```

```python
import functools
import math

import jax
import jax.numpy as jnp
from jax import lax
from jax.experimental import pallas as pl
from jax.experimental.pallas import tpu as pltpu
from jax.sharding import PartitionSpec as P

interval_increment = 0.5
vertical_ratio = 2.0
coolant_film = 1.5
band_sink = 1.0
damping = 0.8
GRID_AXES = ("gx", "gy", "gz")
VMEM = pl.BlockSpec(memory_space=pltpu.VMEM)
F32 = jnp.float32


def harmonic(first, second):
    return 2.0 * first * second / (first + second)


def lanes(shape=(8, 128)):
    return lax.broadcasted_iota(jnp.int32, shape, len(shape) - 1)


def rows(shape):
    return lax.broadcasted_iota(jnp.int32, shape, 0)


def low_side(axis, turn):
    odd = lax.rem(lax.axis_index(axis), 2) == 1
    return ~odd if turn else odd


def regroup(refs, counts):
    out, at = [], 0
    for c in counts:
        out.append(refs[at : at + c])
        at += c
    return out, refs[at:]


def pack_columns(load, count):
    lane = lanes()
    firsts, lasts = [], []
    for start in range(0, count, 128):
        parts = [[], []]
        for chunk in range(start, min(start + 128, count), 16):
            sums = [None, None]
            for i in range(chunk, min(chunk + 16, count)):
                j = i - start
                turned = load(i)
                if j:
                    turned = pltpu.roll(turned, j, 1)
                turned = jnp.where((lane == j) | (lane == (j + 127) % 128), turned, 0.0)
                sums[j % 2] = turned if sums[j % 2] is None else sums[j % 2] + turned
            for kept, new in zip(parts, sums):
                if new is not None:
                    kept.append(new)
        odd = tree(parts[1]) if parts[1] else jnp.zeros((8, 128), F32)
        even = tree(parts[0])
        here = lane % 2 == 0
        firsts.append(jnp.where(here, even, odd))
        lasts.append(pltpu.roll(jnp.where(here, odd, even), 1, 1))
    return jnp.concatenate(firsts, 0), jnp.concatenate(lasts, 0)


def tree(values):
    while len(values) > 1:
        values = [a + b for a, b in zip(values[::2], values[1::2])] + values[len(values) // 2 * 2 :]
    return values[0]


def vreg_groups(z, per, size=8):
    places = []
    for i in range(z * per):
        tier, at = i // per, 8 * (i % per)
        places.append((i, (tier, slice(at, at + 8)), (tier, slice(at + 8, at + 16))))
    return [places[k : k + size] for k in range(0, len(places), size)]


def stage_columns(first, last):
    even = lanes() % 2 == 0
    out = []
    for g in range(first.shape[0] // 8):
        f = first[8 * g : 8 * g + 8]
        l = pltpu.roll(last[8 * g : 8 * g + 8], 127, 1)
        out.append((jnp.where(even, f, l), jnp.where(even, l, f)))
    return out


def spread_columns(staged, edge, i):
    turned = staged[i // 128][i % 2]
    if i % 128:
        turned = pltpu.roll(turned, 128 - i % 128, 1)
    return jnp.where(edge, turned, 0.0)


def edge_lanes():
    lane = lanes()
    return (lane == 0) | (lane == 127)


def column_halos(refs, slot=()):
    low = low_side("gx", 0)
    got = [ref[slot] if slot else ref[...] for ref in refs]
    if len(got) == 1:
        got.append(jnp.zeros_like(got[0]))
    return jnp.where(low, got[0], got[1]), jnp.where(low, got[1], got[0])


def fill_sends(tier, row, send_refs, slot, columns, z, y):
    for axis, refs in zip(GRID_AXES, send_refs):
        for n, ref in enumerate(refs):
            low = low_side(axis, n)
            if axis == "gx":
                value = jnp.where(low, columns[0], columns[1])
            elif axis == "gy":
                value = jnp.where(low, row(0), row(y - 1))
            else:
                value = tier(jnp.where(low, 0, z - 1))
            if slot is None:
                ref[...] = value
            else:
                ref[slot] = value


def padded_access(ref):
    y = ref.shape[1] - 16

    def tier(i):
        return ref[i, pl.ds(8, y), :]

    def row(r):
        return ref[:, 8 + r, :]

    def vreg(i):
        return ref[i // (y // 8), 8 + 8 * (i % (y // 8)) : 16 + 8 * (i % (y // 8)), :]

    return tier, row, vreg


def clear_margins(ref):
    z, y, _ = ref.shape
    for i in range(z):
        ref[i, 0:8, :] = jnp.zeros((8, 128), F32)
        ref[i, y - 8 : y, :] = jnp.zeros((8, 128), F32)


def start_all(sources, targets, sems):
    copies = [pltpu.make_async_copy(a, b, sems.at[n]) for n, (a, b) in enumerate(zip(sources, targets))]
    for copy in copies:
        copy.start()
    return copies


def faces_kernel(rounds, x_in, k_in, x_ref, k_ref, *refs):
    sends, (own_ref, sems) = regroup(refs, rounds)
    z, y, _ = x_in.shape
    per = y // 8
    fields = (x_ref, k_ref)
    copies = [
        start_all([source.at[i] for i in range(z)], [ref.at[i, pl.ds(8, y), :] for i in range(z)], sems.at[n])
        for n, (source, ref) in enumerate(zip((x_in, k_in), fields))
    ]
    for slot, ref in enumerate(fields):
        clear_margins(ref)
        tier, row, vreg = padded_access(ref)

        def load(i):
            if i % per == 0:
                copies[slot][i // per].wait()
            return vreg(i)

        columns = pack_columns(load, z * per)
        own_ref[slot, 0] = columns[0]
        own_ref[slot, 1] = columns[1]
        fill_sends(tier, row, sends, slot, columns, z, y)


def inner_kernel(tall, x_ref, k_ref, c_in, cat_in, sel_in, band_in, flow_in, *refs):
    r_ref, diag_ref, cz_ref, cs_ref, ce_ref, c_ref, cat_ref, sel_ref, band_ref, flow_ref, sems = refs
    z, y, _ = c_ref.shape
    copies = start_all(
        (c_in, cat_in, sel_in, band_in, flow_in), (c_ref, cat_ref, sel_ref, band_ref, flow_ref), sems
    )
    lane = lanes((tall, 128))
    row = rows((tall, 128))
    for i in range(z):
        cs_ref[i, 0:8, :] = jnp.zeros((8, 128), F32)

    def faces(t, carry):
        at = pl.multiple_of(t * tall, 8)
        last = jnp.where(t == y // tall - 1, tall - 1, tall)
        for i in range(z):
            here = k_ref[i, pl.ds(at + 8, tall), :]
            south = harmonic(here, k_ref[i, pl.ds(at + 9, tall), :])
            cs_ref[i, pl.ds(at + 8, tall), :] = jnp.where(row == last, 0.0, south)
            ce_ref[i, pl.ds(at, tall), :] = jnp.where(lane == 127, 0.0, harmonic(here, pltpu.roll(here, 127, 1)))
            if i + 1 < z:
                above = k_ref[i + 1, pl.ds(at + 8, tall), :]
                cz_ref[i, pl.ds(at, tall), :] = vertical_ratio * harmonic(here, above)
        return carry

    lax.fori_loop(0, y // tall, faces, 0)
    for copy in copies:
        copy.wait()

    def rest(t, carry):
        at = pl.multiple_of(t * tall, 8)
        near = pl.ds(at, tall)
        mid = pl.ds(at + 8, tall)
        width = band_ref[0, t]
        band = jnp.where((row < width) | (row >= tall - width), band_sink, 0.0)
        for i in range(z):
            x = x_ref[i, mid, :]
            sink = coolant_film * flow_ref[i].astype(F32) + band
            cn = cs_ref[i, pl.ds(at + 7, tall), :]
            cs = cs_ref[i, mid, :]
            ce = ce_ref[i, near, :]
            cw = pltpu.roll(ce, 1, 1)
            r = cat_ref[sel_ref[i, 0, t]] - sink * x
            r = r + cn * (x_ref[i, pl.ds(at + 7, tall), :] - x) + cs * (x_ref[i, pl.ds(at + 9, tall), :] - x)
            r = r + ce * (pltpu.roll(x, 127, 1) - x) + cw * (pltpu.roll(x, 1, 1) - x)
            diag = c_ref[i, near, :] * (1.0 / interval_increment) + sink
            diag = diag + ((cn + cs) + (ce + cw))
            if i:
                cd = cz_ref[i - 1, near, :]
                diag = diag + cd
                r = r + cd * (x_ref[i - 1, mid, :] - x)
            if i + 1 < z:
                cu = cz_ref[i, near, :]
                diag = diag + cu
                r = r + cu * (x_ref[i + 1, mid, :] - x)
            diag_ref[i, near, :] = diag
            r_ref[i, near, :] = r
        return carry

    lax.fori_loop(0, y // tall, rest, 0)


def sweeps(field_ref, diag_ref, cs_ref, ce_ref, lev_ref, tall):
    z, y, _ = diag_ref.shape
    row = rows((tall, 128))

    def tile(i, t):
        level = lev_ref[i, 0, t]
        at = t * tall
        mid = pl.ds(at + 8, tall)

        def run(count):
            start = field_ref[i, mid, :]
            weight = damping / diag_ref[i, pl.ds(at, tall), :]
            north = jnp.where(row == 0, 0.0, cs_ref[i, pl.ds(at + 7, tall), :])
            south = jnp.where(row == tall - 1, 0.0, cs_ref[i, mid, :])
            east = ce_ref[i, pl.ds(at, tall), :]
            state = start
            for sweep in range(1, count + 1):
                inner = north * pltpu.roll(state, 1, 0) + south * pltpu.roll(state, tall - 1, 0)
                inner = inner + (east * pltpu.roll(state, 127, 1) + pltpu.roll(east * state, 1, 1))
                fresh = ((1.0 - damping) * state + start) + weight * inner
                state = fresh if sweep < 3 else jnp.where(level > sweep, fresh, state)
            field_ref[i, mid, :] = state

        pl.when(level == 2)(functools.partial(run, 1))
        pl.when(level > 2)(functools.partial(run, 3))

    def tier(i, carry):
        for t in range(y // tall):
            tile(i, t)
        return carry

    lax.fori_loop(0, z, tier, 0)


def border_kernel(rounds, tall, *refs):
    (x_ref, k_ref, own_ref, r_in, diag_in, cs_ref, ce_ref, lev_in), refs = refs[:8], refs[8:]
    (hx, hy, hz), refs = regroup(refs, rounds)
    (r_ref, diag_ref, u_ref, cx_ref, cy_ref, czh_ref), refs = refs[:6], refs[6:]
    sends, (lev_ref, sems) = regroup(refs, rounds)
    z, y, _ = r_ref.shape
    table = start_all((lev_in,), (lev_ref,), sems)
    for n, ref in enumerate(hz):
        p = jnp.where(low_side("gz", n), 0, z - 1)
        for at in range(0, y, tall):
            near, inside = slice(at, at + tall), slice(at + 8, at + 8 + tall)
            face = vertical_ratio * harmonic(k_ref[p, inside, :], ref[1, near, :])
            diag = diag_in[p, near, :] + face
            r = r_in[p, near, :] + face * (ref[0, near, :] - x_ref[p, inside, :])
            czh_ref[n, near, :] = face
            diag_in[p, near, :] = diag
            r_in[p, near, :] = r
    row8 = rows((8, 128))
    for n, ref in enumerate(hy):
        low = low_side("gy", n)
        at = pl.multiple_of(jnp.where(low, 0, y - 8), 8)
        mask = row8 == jnp.where(low, 0, 7)
        for i in range(z):
            there = pl.ds(at, 8)
            inside = pl.ds(at + 8, 8)
            face = harmonic(k_ref[i, inside, :], ref[1, i : i + 1, :])
            face = jnp.where(mask, face, 0.0)
            cy_ref[n, i : i + 1, :] = jnp.sum(face, axis=0, keepdims=True)
            diag_in[i, there, :] = diag_in[i, there, :] + face
            r_in[i, there, :] = r_in[i, there, :] + face * (ref[0, i : i + 1, :] - x_ref[i, inside, :])
    xlo, xhi = column_halos(hx, (0,))
    klo, khi = column_halos(hx, (1,))
    west = harmonic(own_ref[1, 0], klo)
    east = harmonic(own_ref[1, 1], khi)
    cx_ref[0] = west
    cx_ref[1] = east
    faces = stage_columns(west, east)
    flux = stage_columns(west * (xlo - own_ref[0, 0]), east * (xhi - own_ref[0, 1]))
    edge = edge_lanes()
    clear_margins(u_ref)
    per = y // 8
    for group in vreg_groups(z, per):
        diags = [diag_in[at] + spread_columns(faces, edge, i) for i, at, _ in group]
        values = [r_in[at] + spread_columns(flux, edge, i) for i, at, _ in group]
        for (_, at, inside), diag, r in zip(group, diags, values):
            diag_ref[at] = diag
            r_ref[at] = r
            u_ref[inside] = r * (damping / diag)
    table[0].wait()
    sweeps(u_ref, diag_ref, cs_ref, ce_ref, lev_ref, tall)
    tier, row, vreg = padded_access(u_ref)
    fill_sends(tier, row, sends, None, pack_columns(vreg, z * per), z, y)


def apply_inner(field_ref, diag_ref, cz_ref, cs_ref, ce_ref, i, at, tall):
    z = diag_ref.shape[0]
    near = pl.ds(at, tall)
    mid = pl.ds(at + 8, tall)
    v = field_ref[i, mid, :]
    ce = ce_ref[i, near, :]
    total = cs_ref[i, pl.ds(at + 7, tall), :] * field_ref[i, pl.ds(at + 7, tall), :]
    total = total + cs_ref[i, mid, :] * field_ref[i, pl.ds(at + 9, tall), :]
    total = total + (ce * pltpu.roll(v, 127, 1) + pltpu.roll(ce * v, 1, 1))
    if i:
        total = total + cz_ref[i - 1, near, :] * field_ref[i - 1, mid, :]
    if i + 1 < z:
        total = total + cz_ref[i, near, :] * field_ref[i + 1, mid, :]
    return v, diag_ref[i, near, :] * v - total


def apply_kernel(tall, u_ref, diag_ref, cz_ref, cs_ref, ce_ref, w_ref):
    z, y, _ = diag_ref.shape

    def step(t, carry):
        at = pl.multiple_of(t * tall, 8)
        for i in range(z):
            w_ref[i, pl.ds(at, tall), :] = apply_inner(u_ref, diag_ref, cz_ref, cs_ref, ce_ref, i, at, tall)[1]
        return carry

    lax.fori_loop(0, y // tall, step, 0)


def subtract_tiers(w_ref, halos, czh_ref):
    for n, ref in enumerate(halos):
        p = jnp.where(low_side("gz", n), 0, w_ref.shape[0] - 1)
        w_ref[p] = w_ref[p] - czh_ref[n] * ref[...]


def border_rows(n, y):
    low = low_side("gy", n)
    at = pl.ds(pl.multiple_of(jnp.where(low, 0, y - 8), 8), 8)
    return at, rows((8, 128)) == jnp.where(low, 0, 7)


def smooth_kernel(rounds, tall, *refs):
    (w_in, diag_ref, cs_ref, ce_ref, cx_ref, cy_ref, czh_ref, lev_in), refs = refs[:8], refs[8:]
    halos, refs = regroup(refs, rounds)
    w_ref, m_ref, face_ref, *send_refs, lev_ref, sems = refs
    z, y, _ = w_ref.shape
    table = start_all((lev_in,), (lev_ref,), sems)
    subtract_tiers(w_in, halos[2], czh_ref)
    for n, ref in enumerate(halos[1]):
        at, mask = border_rows(n, y)
        for i in range(z):
            w_in[i, at, :] = w_in[i, at, :] - jnp.where(mask, cy_ref[n, i : i + 1, :] * ref[i : i + 1, :], 0.0)
    xlo, xhi = column_halos(halos[0])
    flux = stage_columns(cx_ref[0] * xlo, cx_ref[1] * xhi)
    edge = edge_lanes()
    clear_margins(m_ref)
    per = y // 8
    for group in vreg_groups(z, per):
        values = [w_in[at] - spread_columns(flux, edge, i) for i, at, _ in group]
        weights = [damping / diag_ref[at] for _, at, _ in group]
        for (_, at, inside), w, weight in zip(group, values, weights):
            w_ref[at] = w
            m_ref[inside] = w * weight
    table[0].wait()
    sweeps(m_ref, diag_ref, cs_ref, ce_ref, lev_ref, tall)
    tier, row, vreg = padded_access(m_ref)
    for n, ref in enumerate(send_refs):
        ref[...] = tier(jnp.where(low_side("gz", n), 0, z - 1))
    first, last = pack_columns(vreg, z * per)
    plan, _ = face_plan(z, first.shape[0], rounds)
    low = low_side("gy", 0)
    if rounds[1] == 1:
        face_ref[plan["y_low"]] = jnp.where(low, cy_ref[0] * row(0), row(y - 1))
    else:
        face_ref[plan["y_low"]] = jnp.where(low, cy_ref[0], cy_ref[1]) * row(0)
        face_ref[plan["y_high"]] = row(y - 1)
    face_ref[plan["x_low"]] = cx_ref[0] * first
    face_ref[plan["x_high"]] = last
    face_ref[plan["sums"]] = jnp.zeros((4, 128), F32)


def face_plan(z, packed, rounds):
    plan, at = {}, 0
    parts = (("sums", 4), ("y_low", z), ("x_low", packed), ("x_high", packed), ("y_high", z))
    for name, count in parts[: 4 if rounds[1] == 1 else 5]:
        plan[name] = slice(at, at + count)
        at += count
    return plan, at


def fold(product):
    return jnp.sum(product.reshape(-1, 8, 128), axis=0)


def sums_kernel(tall, m_ref, u_ref, r_ref, w_ref, diag_ref, cz_ref, cs_ref, ce_ref, n_ref, sum_ref):
    z, y, _ = diag_ref.shape

    def step(t, carry):
        gamma, delta, cross, last = carry
        at = pl.multiple_of(t * tall, 8)
        near = pl.ds(at, tall)
        for i in range(z):
            m, n = apply_inner(m_ref, diag_ref, cz_ref, cs_ref, ce_ref, i, at, tall)
            n_ref[i, near, :] = n
            u = u_ref[i, pl.ds(at + 8, tall), :]
            w = w_ref[i, near, :]
            gamma = gamma + fold(r_ref[i, near, :] * u)
            delta = delta + fold(w * u)
            cross = cross + fold(w * m)
            last = last + fold(n * m)
        return gamma, delta, cross, last

    zero = jnp.zeros((8, 128), F32)
    for n, value in enumerate(lax.fori_loop(0, y // tall, step, (zero,) * 4)):
        sum_ref[n] = value


def finish_kernel(rounds, *refs):
    (n_in, m_ref, sum_ref, czh_ref, face_ref), refs = refs[:5], refs[5:]
    (halos,), (n_ref, out_ref) = regroup(refs, rounds[2:])
    z, y, _ = n_ref.shape
    last = sum_ref[3]
    for n, ref in enumerate(halos):
        p = jnp.where(low_side("gz", n), 0, z - 1)
        flux = czh_ref[n] * ref[...]
        n_ref[p] = n_in[p] - flux
        last = last - fold(flux * m_ref[p, pl.ds(8, y), :])
    parts = [sum_ref[0], sum_ref[1], sum_ref[2], last]
    parts = [jnp.sum(p, axis=0, keepdims=True) for p in parts]
    height = face_ref.shape[0]
    everything = jnp.concatenate(parts + [face_ref[4:height]], 0)
    for d in range(out_ref.shape[0]):
        out_ref[d] = everything


def update_kernel(rounds, sizes, *refs):
    all_ref, x_ref, r_ref, u_ref, w_ref, m_ref, n_ref, cx_ref, cy_ref, x_out, r_out, xo_ref, ro_ref, sems = refs
    z, y, _ = r_ref.shape
    packed = cx_ref.shape[1]
    plan, _ = face_plan(z, packed, rounds)
    nx, ny, nz = sizes
    members = nx * ny * nz
    y_high = plan["y_low" if rounds[1] == 1 else "y_high"]

    sums = tree([all_ref[d, plan["sums"], :] for d in range(members)])
    gamma, delta, cross, last = (sums[i : i + 1] for i in range(4))
    links = []
    for d in range(members - ny * nz):
        links.append(all_ref[d, plan["x_high"], :] * all_ref[d + ny * nz, plan["x_low"], :])
    if links:
        last = last - 2.0 * jnp.sum(tree(links), axis=0, keepdims=True)
    links = []
    for d in range(members - nz):
        if d // nz % ny + 1 < ny:
            links.append(all_ref[d, y_high, :] * all_ref[d + nz, plan["y_low"], :])
    if links:
        last = last - 2.0 * jnp.sum(tree(links), axis=0, keepdims=True)

    def total(v):
        return jnp.sum(v, axis=1, keepdims=True)

    gamma0 = total(gamma)
    alpha0 = gamma0 / total(delta)
    gamma1 = total(gamma - 2.0 * alpha0 * delta + alpha0 * alpha0 * cross)
    delta1 = total(delta - 2.0 * alpha0 * cross + alpha0 * alpha0 * last)
    beta = gamma1 / gamma0
    alpha1 = gamma1 / (delta1 - beta * gamma1 / alpha0)
    near = alpha0 + alpha1 * (1.0 + beta)
    far = alpha1 * alpha0

    gx, gy, gz = (lax.axis_index(axis) for axis in GRID_AXES)
    me = (gx * ny + gy) * nz + gz
    left = jnp.maximum(me - ny * nz, 0)
    right = jnp.minimum(me + ny * nz, members - 1)
    has_right = gx < nx - 1
    west = far * (cx_ref[0] * all_ref[left, plan["x_high"], :])
    east = far * jnp.where(has_right, all_ref[right, plan["x_low"], :], 0.0)
    flux = stage_columns(west, east)
    below = jnp.maximum(me - nz, 0)
    above = jnp.minimum(me + nz, members - 1)
    row_flux = []
    for n in range(rounds[1]):
        low = low_side("gy", n)
        from_below = cy_ref[n] * all_ref[below, y_high, :]
        from_above = jnp.where(gy < ny - 1, all_ref[above, plan["y_low"], :], 0.0)
        row_flux.append(far * jnp.where(low, from_below, from_above))
    edge = edge_lanes()
    near, far = (jnp.broadcast_to(v, (8, 128)) for v in (near, far))
    per = y // 8
    copies = []
    batches = vreg_groups(z, per)
    for i in range(z):
        for group in batches[i * len(batches) // z : (i + 1) * len(batches) // z]:
            values = [
                r_ref[at] - near * w_ref[at] + (far * n_ref[at] - spread_columns(flux, edge, j)) for j, at, _ in group
            ]
            fields = [x_ref[inside] + near * u_ref[inside] - far * m_ref[inside] for _, _, inside in group]
            for (_, at, _), value, field in zip(group, values, fields):
                ro_ref[at] = value
                xo_ref[at] = field
        for n in range(rounds[1]):
            at, mask = border_rows(n, y)
            ro_ref[i, at, :] = ro_ref[i, at, :] - jnp.where(mask, row_flux[n][i : i + 1], 0.0)
        copies += start_all((ro_ref.at[i], xo_ref.at[i]), (r_out.at[i], x_out.at[i]), sems.at[i])
    for copy in copies:
        copy.wait()


def swap_pairs(axis, start):
    count = lax.axis_size(axis)
    pairs = []
    for i in range(start, count - 1, 2):
        pairs += [(i, i + 1), (i + 1, i)]
    return pairs


def body(
    earlier_warmth_field,
    caloric_storage,
    thermal_diffusivity_coefficient,
    dissipation_catalog,
    dissipation_selector,
    refine_depth,
    border_band_width,
    microflow_flag,
):
    z, y, x = earlier_warmth_field.shape
    tall = dissipation_catalog.shape[1]
    groups = -(-(z * y // 8) // 128)
    rounds = tuple(2 if lax.axis_size(axis) > 2 else 1 for axis in GRID_AXES)
    sends = sum(rounds)
    shape = lambda *s: pltpu.VMEM(s, F32)
    full = shape(z, y, x)
    tall_field = shape(z, y + 16, x)
    _, height = face_plan(z, 8 * groups, rounds)

    hbm = pl.BlockSpec(memory_space=pltpu.HBM)

    def call(kernel, outs, ins, name, scratch=(), out_specs=None, alias=None, outer=()):
        specs = [hbm if n in outer else VMEM for n in range(len(ins))]
        ins = [pltpu.with_memory_space_constraint(v, pltpu.HBM) if n in outer else v for n, v in enumerate(ins)]
        return pl.pallas_call(
            kernel,
            out_shape=outs,
            in_specs=specs,
            out_specs=out_specs or [VMEM] * len(outs),
            scratch_shapes=list(scratch),
            input_output_aliases=alias or {},
            name=name,
            compiler_params=pltpu.CompilerParams(vmem_limit_bytes=16 * 2**20),
        )(*ins)

    def face_shapes(front):
        out = []
        for axis, n in zip(((8 * groups, x), (z, x), (y, x)), rounds):
            out += [shape(*front, *axis)] * n
        return out

    def swap(faces, axes=GRID_AXES):
        faces, got = list(faces), []
        for axis in axes:
            for start in range(rounds[GRID_AXES.index(axis)]):
                got.append(lax.ppermute(faces.pop(0), axis, swap_pairs(axis, start)))
        return got

    selector = jnp.swapaxes(dissipation_selector, 1, 2)
    levels = jnp.swapaxes(refine_depth, 1, 2)
    width = jnp.swapaxes(border_band_width, 0, 1)

    def table(v):
        return pltpu.SMEM(v.shape, v.dtype)

    outs = call(
        functools.partial(faces_kernel, rounds),
        [tall_field, tall_field] + face_shapes((2,)) + [shape(2, 2, 8 * groups, x)],
        [earlier_warmth_field, thermal_diffusivity_coefficient],
        "faces",
        [pltpu.SemaphoreType.DMA((2, z))],
        outer=(0, 1),
    )
    (field, kappa), outs = outs[:2], outs[2:]
    own, halos = outs[sends], swap(outs[:sends])
    r, diag, cz, cs, ce = call(
        functools.partial(inner_kernel, tall),
        [full, full, shape(max(z - 1, 1), y, x), shape(z, y + 8, x), full],
        [field, kappa, caloric_storage, dissipation_catalog, selector, width, microflow_flag],
        "inner",
        [
            full,
            shape(*dissipation_catalog.shape),
            table(selector),
            table(width),
            table(microflow_flag),
            pltpu.SemaphoreType.DMA((5,)),
        ],
        outer=(2, 3, 4, 5, 6),
    )
    outs = call(
        functools.partial(border_kernel, rounds, tall),
        [full, full, tall_field, shape(2, 8 * groups, x), shape(rounds[1], z, x), shape(rounds[2], y, x)]
        + face_shapes(()),
        [field, kappa, own, r, diag, cs, ce, levels] + halos,
        "border",
        [table(levels), pltpu.SemaphoreType.DMA((1,))],
        alias={3: 0, 4: 1},
        outer=(7,),
    )
    r, diag, u, cx, cy, czh = outs[:6]
    halos = swap(outs[6:])
    (w,) = call(functools.partial(apply_kernel, tall), [full], [u, diag, cz, cs, ce], "apply")
    outs = call(
        functools.partial(smooth_kernel, rounds, tall),
        [full, tall_field, shape(height, x)] + [shape(y, x)] * rounds[2],
        [w, diag, cs, ce, cx, cy, czh, levels] + halos,
        "smooth",
        [table(levels), pltpu.SemaphoreType.DMA((1,))],
        alias={0: 0},
        outer=(7,),
    )
    w, m, faces = outs[:3]
    halos = swap(outs[3:], GRID_AXES[2:])
    n, sums = call(
        functools.partial(sums_kernel, tall), [full, shape(4, 8, 128)], [m, u, r, w, diag, cz, cs, ce], "sums"
    )
    sizes = tuple(lax.axis_size(axis) for axis in GRID_AXES)
    n, parts = call(
        functools.partial(finish_kernel, rounds),
        [full, shape(math.prod(sizes), height, x)],
        [n, m, sums, czh, faces] + halos,
        "finish",
        alias={0: 0},
    )
    every = lax.all_to_all(parts, GRID_AXES, 0, 0, tiled=True)
    return tuple(
        call(
            functools.partial(update_kernel, rounds, sizes),
            [jax.ShapeDtypeStruct((z, y, x), F32)] * 2,
            [every, field, r, u, w, m, n, cx, cy],
            "update",
            [full, full, pltpu.SemaphoreType.DMA((z, 2))],
            out_specs=[hbm, hbm],
        )
    )


def solution(mesh):
    cells = P(("groups", "gz"), "gy", "gx")
    return jax.shard_map(
        body,
        mesh=mesh,
        in_specs=(
            cells,
            cells,
            cells,
            P("groups", None, None),
            cells,
            cells,
            P(("groups", "gy"), "gx"),
            P(("groups", "gz")),
        ),
        out_specs=(cells, cells),
        check_vma=False,
    )
```

```python
import functools
import math

import jax
import jax.numpy as jnp
from jax import lax
from jax.experimental import pallas as pl
from jax.experimental.pallas import tpu as pltpu
from jax.sharding import PartitionSpec as P

interval_increment = 0.5
vertical_ratio = 2.0
coolant_film = 1.5
band_sink = 1.0
damping = 0.8
GRID_AXES = ("gx", "gy", "gz")
VMEM = pl.BlockSpec(memory_space=pltpu.VMEM)
F32 = jnp.float32


def harmonic(first, second):
    return 2.0 * first * second / (first + second)


def lanes(shape=(8, 128)):
    return lax.broadcasted_iota(jnp.int32, shape, len(shape) - 1)


def rows(shape):
    return lax.broadcasted_iota(jnp.int32, shape, 0)


def low_side(axis, turn):
    odd = lax.rem(lax.axis_index(axis), 2) == 1
    return ~odd if turn else odd


def regroup(refs, counts):
    out, at = [], 0
    for c in counts:
        out.append(refs[at : at + c])
        at += c
    return out, refs[at:]


def pack_columns(load, count):
    lane = lanes()
    firsts, lasts = [], []
    for start in range(0, count, 128):
        parts = [[], []]
        for chunk in range(start, min(start + 128, count), 16):
            sums = [None, None]
            for i in range(chunk, min(chunk + 16, count)):
                j = i - start
                turned = load(i)
                if j:
                    turned = pltpu.roll(turned, j, 1)
                turned = jnp.where((lane == j) | (lane == (j + 127) % 128), turned, 0.0)
                sums[j % 2] = turned if sums[j % 2] is None else sums[j % 2] + turned
            for kept, new in zip(parts, sums):
                if new is not None:
                    kept.append(new)
        odd = tree(parts[1]) if parts[1] else jnp.zeros((8, 128), F32)
        even = tree(parts[0])
        here = lane % 2 == 0
        firsts.append(jnp.where(here, even, odd))
        lasts.append(pltpu.roll(jnp.where(here, odd, even), 1, 1))
    return jnp.concatenate(firsts, 0), jnp.concatenate(lasts, 0)


def tree(values):
    while len(values) > 1:
        values = [a + b for a, b in zip(values[::2], values[1::2])] + values[len(values) // 2 * 2 :]
    return values[0]


def vreg_groups(z, per, size=8):
    places = []
    for i in range(z * per):
        tier, at = i // per, 8 * (i % per)
        places.append((i, (tier, slice(at, at + 8)), (tier, slice(at + 8, at + 16))))
    return [places[k : k + size] for k in range(0, len(places), size)]


def stage_columns(first, last):
    even = lanes() % 2 == 0
    out = []
    for g in range(first.shape[0] // 8):
        f = first[8 * g : 8 * g + 8]
        l = pltpu.roll(last[8 * g : 8 * g + 8], 127, 1)
        out.append((jnp.where(even, f, l), jnp.where(even, l, f)))
    return out


def spread_columns(staged, edge, i):
    turned = staged[i // 128][i % 2]
    if i % 128:
        turned = pltpu.roll(turned, 128 - i % 128, 1)
    return jnp.where(edge, turned, 0.0)


def edge_lanes():
    lane = lanes()
    return (lane == 0) | (lane == 127)


def column_halos(refs, slot=()):
    low = low_side("gx", 0)
    got = [ref[slot] if slot else ref[...] for ref in refs]
    if len(got) == 1:
        got.append(jnp.zeros_like(got[0]))
    return jnp.where(low, got[0], got[1]), jnp.where(low, got[1], got[0])


def fill_sends(tier, row, send_refs, slot, columns, z, y):
    for axis, refs in zip(GRID_AXES, send_refs):
        for n, ref in enumerate(refs):
            low = low_side(axis, n)
            if axis == "gx":
                value = jnp.where(low, columns[0], columns[1])
            elif axis == "gy":
                value = jnp.where(low, row(0), row(y - 1))
            else:
                value = tier(jnp.where(low, 0, z - 1))
            if slot is None:
                ref[...] = value
            else:
                ref[slot] = value


def padded_access(ref):
    y = ref.shape[1] - 16

    def tier(i):
        return ref[i, pl.ds(8, y), :]

    def row(r):
        return ref[:, 8 + r, :]

    def vreg(i):
        return ref[i // (y // 8), 8 + 8 * (i % (y // 8)) : 16 + 8 * (i % (y // 8)), :]

    return tier, row, vreg


def clear_margins(ref):
    z, y, _ = ref.shape
    for i in range(z):
        ref[i, 0:8, :] = jnp.zeros((8, 128), F32)
        ref[i, y - 8 : y, :] = jnp.zeros((8, 128), F32)


def start_all(sources, targets, sems):
    copies = [pltpu.make_async_copy(a, b, sems.at[n]) for n, (a, b) in enumerate(zip(sources, targets))]
    for copy in copies:
        copy.start()
    return copies


def faces_kernel(rounds, x_in, k_in, x_ref, k_ref, *refs):
    sends, (own_ref, sems) = regroup(refs, rounds)
    z, y, _ = x_in.shape
    per = y // 8
    fields = (x_ref, k_ref)
    copies = [
        start_all([source.at[i] for i in range(z)], [ref.at[i, pl.ds(8, y), :] for i in range(z)], sems.at[n])
        for n, (source, ref) in enumerate(zip((x_in, k_in), fields))
    ]
    for slot, ref in enumerate(fields):
        clear_margins(ref)
        tier, row, vreg = padded_access(ref)

        def load(i):
            if i % per == 0:
                copies[slot][i // per].wait()
            return vreg(i)

        columns = pack_columns(load, z * per)
        own_ref[slot, 0] = columns[0]
        own_ref[slot, 1] = columns[1]
        fill_sends(tier, row, sends, slot, columns, z, y)


def inner_kernel(tall, x_ref, k_ref, c_in, cat_in, sel_in, band_in, flow_in, lev_in, *refs):
    r_ref, diag_ref, cz_ref, cs_ref, ce_ref, mask_ref, c_ref, cat_ref, *tables, sems = refs
    sel_ref, band_ref, flow_ref, lev_ref = tables
    z, y, _ = c_ref.shape
    copies = start_all(
        (c_in, cat_in, sel_in, band_in, flow_in, lev_in),
        (c_ref, cat_ref, *tables),
        sems,
    )
    lane = lanes((tall, 128))
    row = rows((tall, 128))
    for i in range(z):
        cs_ref[i, 0:8, :] = jnp.zeros((8, 128), F32)

    def faces(t, carry):
        at = pl.multiple_of(t * tall, 8)
        last = jnp.where(t == y // tall - 1, tall - 1, tall)
        for i in range(z):
            here = k_ref[i, pl.ds(at + 8, tall), :]
            south = harmonic(here, k_ref[i, pl.ds(at + 9, tall), :])
            cs_ref[i, pl.ds(at + 8, tall), :] = jnp.where(row == last, 0.0, south)
            ce_ref[i, pl.ds(at, tall), :] = jnp.where(lane == 127, 0.0, harmonic(here, pltpu.roll(here, 127, 1)))
            if i + 1 < z:
                above = k_ref[i + 1, pl.ds(at + 8, tall), :]
                cz_ref[i, pl.ds(at, tall), :] = vertical_ratio * harmonic(here, above)
        return carry

    lax.fori_loop(0, y // tall, faces, 0)
    for copy in copies:
        copy.wait()

    tiles = y // tall
    for word in range(mask_ref.shape[1]):
        few, many = jnp.int32(0), jnp.int32(0)
        for number in range(16 * word, min(16 * word + 16, z * tiles)):
            level = lev_ref[number // tiles, 0, number % tiles]
            few = few + jnp.where(level == 2, 1 << (number - 16 * word), 0)
            many = many + jnp.where(level > 2, 1 << (number - 16 * word), 0)
        mask_ref[0, word] = jnp.full((8, 128), few.astype(F32))
        mask_ref[1, word] = jnp.full((8, 128), many.astype(F32))

    def rest(t, carry):
        at = pl.multiple_of(t * tall, 8)
        near = pl.ds(at, tall)
        mid = pl.ds(at + 8, tall)
        width = band_ref[0, t]
        band = jnp.where((row < width) | (row >= tall - width), band_sink, 0.0)
        for i in range(z):
            x = x_ref[i, mid, :]
            sink = coolant_film * flow_ref[i].astype(F32) + band
            cn = cs_ref[i, pl.ds(at + 7, tall), :]
            cs = cs_ref[i, mid, :]
            ce = ce_ref[i, near, :]
            cw = pltpu.roll(ce, 1, 1)
            r = cat_ref[sel_ref[i, 0, t]] - sink * x
            r = r + cn * (x_ref[i, pl.ds(at + 7, tall), :] - x) + cs * (x_ref[i, pl.ds(at + 9, tall), :] - x)
            r = r + ce * (pltpu.roll(x, 127, 1) - x) + cw * (pltpu.roll(x, 1, 1) - x)
            diag = c_ref[i, near, :] * (1.0 / interval_increment) + sink
            diag = diag + ((cn + cs) + (ce + cw))
            if i:
                cd = cz_ref[i - 1, near, :]
                diag = diag + cd
                r = r + cd * (x_ref[i - 1, mid, :] - x)
            if i + 1 < z:
                cu = cz_ref[i, near, :]
                diag = diag + cu
                r = r + cu * (x_ref[i + 1, mid, :] - x)
            diag_ref[i, near, :] = diag
            r_ref[i, near, :] = r
        return carry

    lax.fori_loop(0, y // tall, rest, 0)


def list_tiles(mask_ref, todo_ref, tiles):
    counts = []
    for kind in range(2):
        count = jnp.int32(0)
        for word in range(mask_ref.shape[1]):
            mask = jnp.max(mask_ref[kind, word]).astype(jnp.int32)
            for bit in range(min(16, tiles - 16 * word)):
                todo_ref[kind, count] = 16 * word + bit
                count = count + ((mask >> bit) & 1)
        counts.append(count)
    return counts


def sweeps(field_ref, diag_ref, cs_ref, ce_ref, todo_ref, counts, tall):
    z, y, _ = diag_ref.shape
    tiles = y // tall

    def run(count):
        def tile(n, carry):
            number = todo_ref[min(count, 2) - 1, n]
            i, t = lax.div(number, tiles), lax.rem(number, tiles)
            at = pl.multiple_of(t * tall, 8)
            mid = pl.ds(at + 8, tall)
            start = field_ref[i, mid, :]
            weight = damping / diag_ref[i, pl.ds(at, tall), :]
            first = rows((8, 128)) == 0
            final = rows((8, 128)) == 7
            north = cs_ref[i, pl.ds(at + 7, tall), :]
            north = jnp.concatenate([jnp.where(first, 0.0, north[:8]), north[8:]], 0)
            south = cs_ref[i, mid, :]
            south = jnp.concatenate([south[:-8], jnp.where(final, 0.0, south[-8:])], 0)
            east = ce_ref[i, pl.ds(at, tall), :]
            state = start
            for sweep in range(1, count + 1):
                if sweep == 1:
                    above, below = field_ref[i, pl.ds(at + 7, tall), :], field_ref[i, pl.ds(at + 9, tall), :]
                else:
                    above, below = pltpu.roll(state, 1, 0), pltpu.roll(state, tall - 1, 0)
                inner = (north * above + south * below) + (
                    east * pltpu.roll(state, 127, 1) + pltpu.roll(east * state, 1, 1)
                )
                state = ((1.0 - damping) * state + start) + weight * inner
            field_ref[i, mid, :] = state
            return carry

        lax.fori_loop(0, counts[min(count, 2) - 1], tile, 0)

    run(1)
    run(3)


def border_kernel(rounds, tall, *refs):
    (x_ref, k_ref, own_ref, r_in, diag_in, cs_ref, ce_ref, mask_ref), refs = refs[:8], refs[8:]
    (hx, hy, hz), refs = regroup(refs, rounds)
    (r_ref, diag_ref, u_ref, cx_ref, cy_ref, czh_ref), refs = refs[:6], refs[6:]
    sends, (todo_ref,) = regroup(refs, rounds)
    z, y, _ = r_ref.shape
    counts = list_tiles(mask_ref, todo_ref, z * (y // tall))
    for n, ref in enumerate(hz):
        p = jnp.where(low_side("gz", n), 0, z - 1)
        for at in range(0, y, tall):
            near, inside = slice(at, at + tall), slice(at + 8, at + 8 + tall)
            face = vertical_ratio * harmonic(k_ref[p, inside, :], ref[1, near, :])
            diag = diag_in[p, near, :] + face
            r = r_in[p, near, :] + face * (ref[0, near, :] - x_ref[p, inside, :])
            czh_ref[n, near, :] = face
            diag_in[p, near, :] = diag
            r_in[p, near, :] = r
    row8 = rows((8, 128))
    for n, ref in enumerate(hy):
        low = low_side("gy", n)
        at = pl.multiple_of(jnp.where(low, 0, y - 8), 8)
        mask = row8 == jnp.where(low, 0, 7)
        for i in range(z):
            there = pl.ds(at, 8)
            inside = pl.ds(at + 8, 8)
            face = harmonic(k_ref[i, inside, :], ref[1, i : i + 1, :])
            face = jnp.where(mask, face, 0.0)
            cy_ref[n, i : i + 1, :] = jnp.sum(face, axis=0, keepdims=True)
            diag_in[i, there, :] = diag_in[i, there, :] + face
            r_in[i, there, :] = r_in[i, there, :] + face * (ref[0, i : i + 1, :] - x_ref[i, inside, :])
    xlo, xhi = column_halos(hx, (0,))
    klo, khi = column_halos(hx, (1,))
    west = harmonic(own_ref[1, 0], klo)
    east = harmonic(own_ref[1, 1], khi)
    cx_ref[0] = west
    cx_ref[1] = east
    faces = stage_columns(west, east)
    flux = stage_columns(west * (xlo - own_ref[0, 0]), east * (xhi - own_ref[0, 1]))
    edge = edge_lanes()
    clear_margins(u_ref)
    per = y // 8
    for group in vreg_groups(z, per):
        diags = [diag_in[at] + spread_columns(faces, edge, i) for i, at, _ in group]
        values = [r_in[at] + spread_columns(flux, edge, i) for i, at, _ in group]
        for (_, at, inside), diag, r in zip(group, diags, values):
            diag_ref[at] = diag
            r_ref[at] = r
            u_ref[inside] = r * (damping / diag)
    sweeps(u_ref, diag_ref, cs_ref, ce_ref, todo_ref, counts, tall)
    tier, row, vreg = padded_access(u_ref)
    fill_sends(tier, row, sends, None, pack_columns(vreg, z * per), z, y)


def apply_inner(field_ref, diag_ref, cz_ref, cs_ref, ce_ref, i, at, tall):
    z = diag_ref.shape[0]
    near = pl.ds(at, tall)
    mid = pl.ds(at + 8, tall)
    v = field_ref[i, mid, :]
    ce = ce_ref[i, near, :]
    total = cs_ref[i, pl.ds(at + 7, tall), :] * field_ref[i, pl.ds(at + 7, tall), :]
    total = total + cs_ref[i, mid, :] * field_ref[i, pl.ds(at + 9, tall), :]
    total = total + (ce * pltpu.roll(v, 127, 1) + pltpu.roll(ce * v, 1, 1))
    if i:
        total = total + cz_ref[i - 1, near, :] * field_ref[i - 1, mid, :]
    if i + 1 < z:
        total = total + cz_ref[i, near, :] * field_ref[i + 1, mid, :]
    return v, diag_ref[i, near, :] * v - total


def apply_kernel(tall, u_ref, diag_ref, cz_ref, cs_ref, ce_ref, w_ref):
    z, y, _ = diag_ref.shape

    def step(t, carry):
        at = pl.multiple_of(t * tall, 8)
        for i in range(z):
            w_ref[i, pl.ds(at, tall), :] = apply_inner(u_ref, diag_ref, cz_ref, cs_ref, ce_ref, i, at, tall)[1]
        return carry

    lax.fori_loop(0, y // tall, step, 0)


def subtract_tiers(w_ref, halos, czh_ref):
    for n, ref in enumerate(halos):
        p = jnp.where(low_side("gz", n), 0, w_ref.shape[0] - 1)
        w_ref[p] = w_ref[p] - czh_ref[n] * ref[...]


def border_rows(n, y):
    low = low_side("gy", n)
    at = pl.ds(pl.multiple_of(jnp.where(low, 0, y - 8), 8), 8)
    return at, rows((8, 128)) == jnp.where(low, 0, 7)


def smooth_kernel(rounds, tall, *refs):
    (w_in, diag_ref, cs_ref, ce_ref, cx_ref, cy_ref, czh_ref, mask_ref), refs = refs[:8], refs[8:]
    halos, refs = regroup(refs, rounds)
    w_ref, m_ref, face_ref, *send_refs, todo_ref = refs
    z, y, _ = w_ref.shape
    counts = list_tiles(mask_ref, todo_ref, z * (y // tall))
    subtract_tiers(w_in, halos[2], czh_ref)
    for n, ref in enumerate(halos[1]):
        at, mask = border_rows(n, y)
        for i in range(z):
            w_in[i, at, :] = w_in[i, at, :] - jnp.where(mask, cy_ref[n, i : i + 1, :] * ref[i : i + 1, :], 0.0)
    xlo, xhi = column_halos(halos[0])
    flux = stage_columns(cx_ref[0] * xlo, cx_ref[1] * xhi)
    edge = edge_lanes()
    clear_margins(m_ref)
    per = y // 8
    for group in vreg_groups(z, per):
        values = [w_in[at] - spread_columns(flux, edge, i) for i, at, _ in group]
        weights = [damping / diag_ref[at] for _, at, _ in group]
        for (_, at, inside), w, weight in zip(group, values, weights):
            w_ref[at] = w
            m_ref[inside] = w * weight
    sweeps(m_ref, diag_ref, cs_ref, ce_ref, todo_ref, counts, tall)
    tier, row, vreg = padded_access(m_ref)
    for n, ref in enumerate(send_refs):
        ref[...] = tier(jnp.where(low_side("gz", n), 0, z - 1))
    first, last = pack_columns(vreg, z * per)
    plan, _ = face_plan(z, first.shape[0], rounds)
    low = low_side("gy", 0)
    if rounds[1] == 1:
        face_ref[plan["y_low"]] = jnp.where(low, cy_ref[0] * row(0), row(y - 1))
    else:
        face_ref[plan["y_low"]] = jnp.where(low, cy_ref[0], cy_ref[1]) * row(0)
        face_ref[plan["y_high"]] = row(y - 1)
    face_ref[plan["x_low"]] = cx_ref[0] * first
    face_ref[plan["x_high"]] = last
    face_ref[plan["sums"]] = jnp.zeros((4, 128), F32)


def face_plan(z, packed, rounds):
    plan, at = {}, 0
    parts = (("sums", 4), ("y_low", z), ("x_low", packed), ("x_high", packed), ("y_high", z))
    for name, count in parts[: 4 if rounds[1] == 1 else 5]:
        plan[name] = slice(at, at + count)
        at += count
    return plan, at


def fold(product):
    return jnp.sum(product.reshape(-1, 8, 128), axis=0)


def sums_kernel(tall, m_ref, u_ref, r_ref, w_ref, diag_ref, cz_ref, cs_ref, ce_ref, n_ref, sum_ref):
    z, y, _ = diag_ref.shape

    def step(t, carry):
        gamma, delta, cross, last = carry
        at = pl.multiple_of(t * tall, 8)
        near = pl.ds(at, tall)
        for i in range(z):
            m, n = apply_inner(m_ref, diag_ref, cz_ref, cs_ref, ce_ref, i, at, tall)
            n_ref[i, near, :] = n
            u = u_ref[i, pl.ds(at + 8, tall), :]
            w = w_ref[i, near, :]
            gamma = gamma + fold(r_ref[i, near, :] * u)
            delta = delta + fold(w * u)
            cross = cross + fold(w * m)
            last = last + fold(n * m)
        return gamma, delta, cross, last

    zero = jnp.zeros((8, 128), F32)
    for n, value in enumerate(lax.fori_loop(0, y // tall, step, (zero,) * 4)):
        sum_ref[n] = value


def finish_kernel(rounds, *refs):
    (n_in, m_ref, sum_ref, czh_ref, face_ref), refs = refs[:5], refs[5:]
    (halos,), (n_ref, out_ref) = regroup(refs, rounds[2:])
    z, y, _ = n_ref.shape
    last = sum_ref[3]
    for n, ref in enumerate(halos):
        p = jnp.where(low_side("gz", n), 0, z - 1)
        flux = czh_ref[n] * ref[...]
        n_ref[p] = n_in[p] - flux
        last = last - fold(flux * m_ref[p, pl.ds(8, y), :])
    parts = [sum_ref[0], sum_ref[1], sum_ref[2], last]
    parts = [jnp.sum(p, axis=0, keepdims=True) for p in parts]
    height = face_ref.shape[0]
    everything = jnp.concatenate(parts + [face_ref[4:height]], 0)
    for d in range(out_ref.shape[0]):
        out_ref[d] = everything


def update_kernel(rounds, sizes, *refs):
    all_ref, x_ref, r_ref, u_ref, w_ref, m_ref, n_ref, cx_ref, cy_ref, x_out, r_out, xo_ref, ro_ref, sems = refs
    z, y, _ = r_ref.shape
    packed = cx_ref.shape[1]
    plan, _ = face_plan(z, packed, rounds)
    nx, ny, nz = sizes
    members = nx * ny * nz
    y_high = plan["y_low" if rounds[1] == 1 else "y_high"]

    sums = tree([all_ref[d, plan["sums"], :] for d in range(members)])
    gamma, delta, cross, last = (sums[i : i + 1] for i in range(4))
    links = []
    for d in range(members - ny * nz):
        links.append(all_ref[d, plan["x_high"], :] * all_ref[d + ny * nz, plan["x_low"], :])
    if links:
        last = last - 2.0 * jnp.sum(tree(links), axis=0, keepdims=True)
    links = []
    for d in range(members - nz):
        if d // nz % ny + 1 < ny:
            links.append(all_ref[d, y_high, :] * all_ref[d + nz, plan["y_low"], :])
    if links:
        last = last - 2.0 * jnp.sum(tree(links), axis=0, keepdims=True)

    def total(v):
        return jnp.sum(v, axis=1, keepdims=True)

    gamma0 = total(gamma)
    alpha0 = gamma0 / total(delta)
    gamma1 = total(gamma - 2.0 * alpha0 * delta + alpha0 * alpha0 * cross)
    delta1 = total(delta - 2.0 * alpha0 * cross + alpha0 * alpha0 * last)
    beta = gamma1 / gamma0
    alpha1 = gamma1 / (delta1 - beta * gamma1 / alpha0)
    near = alpha0 + alpha1 * (1.0 + beta)
    far = alpha1 * alpha0

    gx, gy, gz = (lax.axis_index(axis) for axis in GRID_AXES)
    me = (gx * ny + gy) * nz + gz
    left = jnp.maximum(me - ny * nz, 0)
    right = jnp.minimum(me + ny * nz, members - 1)
    has_right = gx < nx - 1
    west = far * (cx_ref[0] * all_ref[left, plan["x_high"], :])
    east = far * jnp.where(has_right, all_ref[right, plan["x_low"], :], 0.0)
    flux = stage_columns(west, east)
    below = jnp.maximum(me - nz, 0)
    above = jnp.minimum(me + nz, members - 1)
    row_flux = []
    for n in range(rounds[1]):
        low = low_side("gy", n)
        from_below = cy_ref[n] * all_ref[below, y_high, :]
        from_above = jnp.where(gy < ny - 1, all_ref[above, plan["y_low"], :], 0.0)
        row_flux.append(far * jnp.where(low, from_below, from_above))
    edge = edge_lanes()
    near, far = (jnp.broadcast_to(v, (8, 128)) for v in (near, far))
    per = y // 8
    copies = []
    batches = vreg_groups(z, per)
    for i in range(z):
        for group in batches[i * len(batches) // z : (i + 1) * len(batches) // z]:
            values = [
                r_ref[at] - near * w_ref[at] + (far * n_ref[at] - spread_columns(flux, edge, j)) for j, at, _ in group
            ]
            fields = [x_ref[inside] + near * u_ref[inside] - far * m_ref[inside] for _, _, inside in group]
            for (_, at, _), value, field in zip(group, values, fields):
                ro_ref[at] = value
                xo_ref[at] = field
        for n in range(rounds[1]):
            at, mask = border_rows(n, y)
            ro_ref[i, at, :] = ro_ref[i, at, :] - jnp.where(mask, row_flux[n][i : i + 1], 0.0)
        copies += start_all((ro_ref.at[i], xo_ref.at[i]), (r_out.at[i], x_out.at[i]), sems.at[i])
    for copy in copies:
        copy.wait()


def swap_pairs(axis, start):
    count = lax.axis_size(axis)
    pairs = []
    for i in range(start, count - 1, 2):
        pairs += [(i, i + 1), (i + 1, i)]
    return pairs


def body(
    earlier_warmth_field,
    caloric_storage,
    thermal_diffusivity_coefficient,
    dissipation_catalog,
    dissipation_selector,
    refine_depth,
    border_band_width,
    microflow_flag,
):
    z, y, x = earlier_warmth_field.shape
    tall = dissipation_catalog.shape[1]
    groups = -(-(z * y // 8) // 128)
    rounds = tuple(2 if lax.axis_size(axis) > 2 else 1 for axis in GRID_AXES)
    sends = sum(rounds)
    shape = lambda *s: pltpu.VMEM(s, F32)
    full = shape(z, y, x)
    tall_field = shape(z, y + 16, x)
    _, height = face_plan(z, 8 * groups, rounds)

    hbm = pl.BlockSpec(memory_space=pltpu.HBM)

    def call(kernel, outs, ins, name, scratch=(), out_specs=None, alias=None, outer=()):
        specs = [hbm if n in outer else VMEM for n in range(len(ins))]
        ins = [pltpu.with_memory_space_constraint(v, pltpu.HBM) if n in outer else v for n, v in enumerate(ins)]
        return pl.pallas_call(
            kernel,
            out_shape=outs,
            in_specs=specs,
            out_specs=out_specs or [VMEM] * len(outs),
            scratch_shapes=list(scratch),
            input_output_aliases=alias or {},
            name=name,
            compiler_params=pltpu.CompilerParams(vmem_limit_bytes=16 * 2**20),
        )(*ins)

    def face_shapes(front):
        out = []
        for axis, n in zip(((8 * groups, x), (z, x), (y, x)), rounds):
            out += [shape(*front, *axis)] * n
        return out

    def swap(faces, axes=GRID_AXES):
        faces, got = list(faces), []
        for axis in axes:
            for start in range(rounds[GRID_AXES.index(axis)]):
                got.append(lax.ppermute(faces.pop(0), axis, swap_pairs(axis, start)))
        return got

    selector = jnp.swapaxes(dissipation_selector, 1, 2)
    levels = jnp.swapaxes(refine_depth, 1, 2)
    width = jnp.swapaxes(border_band_width, 0, 1)

    todo = pltpu.SMEM((2, z * (y // tall) + 1), jnp.int32)

    def table(v):
        return pltpu.SMEM(v.shape, v.dtype)

    outs = call(
        functools.partial(faces_kernel, rounds),
        [tall_field, tall_field] + face_shapes((2,)) + [shape(2, 2, 8 * groups, x)],
        [earlier_warmth_field, thermal_diffusivity_coefficient],
        "faces",
        [pltpu.SemaphoreType.DMA((2, z))],
        outer=(0, 1),
    )
    (field, kappa), outs = outs[:2], outs[2:]
    own, halos = outs[sends], swap(outs[:sends])
    r, diag, cz, cs, ce, masks = call(
        functools.partial(inner_kernel, tall),
        [full, full, shape(max(z - 1, 1), y, x), shape(z, y + 8, x), full, shape(2, -(-z * (y // tall) // 16), 8, 128)],
        [field, kappa, caloric_storage, dissipation_catalog, selector, width, microflow_flag, levels],
        "inner",
        [
            full,
            shape(*dissipation_catalog.shape),
            table(selector),
            table(width),
            table(microflow_flag),
            table(levels),
            pltpu.SemaphoreType.DMA((6,)),
        ],
        outer=(2, 3, 4, 5, 6, 7),
    )
    outs = call(
        functools.partial(border_kernel, rounds, tall),
        [full, full, tall_field, shape(2, 8 * groups, x), shape(rounds[1], z, x), shape(rounds[2], y, x)]
        + face_shapes(()),
        [field, kappa, own, r, diag, cs, ce, masks] + halos,
        "border",
        [todo],
        alias={3: 0, 4: 1},
    )
    r, diag, u, cx, cy, czh = outs[:6]
    halos = swap(outs[6:])
    (w,) = call(functools.partial(apply_kernel, tall), [full], [u, diag, cz, cs, ce], "apply")
    outs = call(
        functools.partial(smooth_kernel, rounds, tall),
        [full, tall_field, shape(height, x)] + [shape(y, x)] * rounds[2],
        [w, diag, cs, ce, cx, cy, czh, masks] + halos,
        "smooth",
        [todo],
        alias={0: 0},
    )
    w, m, faces = outs[:3]
    halos = swap(outs[3:], GRID_AXES[2:])
    n, sums = call(
        functools.partial(sums_kernel, tall), [full, shape(4, 8, 128)], [m, u, r, w, diag, cz, cs, ce], "sums"
    )
    sizes = tuple(lax.axis_size(axis) for axis in GRID_AXES)
    n, parts = call(
        functools.partial(finish_kernel, rounds),
        [full, shape(math.prod(sizes), height, x)],
        [n, m, sums, czh, faces] + halos,
        "finish",
        alias={0: 0},
    )
    every = lax.all_to_all(parts, GRID_AXES, 0, 0, tiled=True)
    return tuple(
        call(
            functools.partial(update_kernel, rounds, sizes),
            [jax.ShapeDtypeStruct((z, y, x), F32)] * 2,
            [every, field, r, u, w, m, n, cx, cy],
            "update",
            [full, full, pltpu.SemaphoreType.DMA((z, 2))],
            out_specs=[hbm, hbm],
        )
    )


def solution(mesh):
    cells = P(("groups", "gz"), "gy", "gx")
    return jax.shard_map(
        body,
        mesh=mesh,
        in_specs=(
            cells,
            cells,
            cells,
            P("groups", None, None),
            cells,
            cells,
            P(("groups", "gy"), "gx"),
            P(("groups", "gz")),
        ),
        out_specs=(cells, cells),
        check_vma=False,
    )
```

```python
import functools
import math

import jax
import jax.numpy as jnp
from jax import lax
from jax.experimental import pallas as pl
from jax.experimental.pallas import tpu as pltpu
from jax.sharding import PartitionSpec as P

interval_increment = 0.5
vertical_ratio = 2.0
coolant_film = 1.5
band_sink = 1.0
damping = 0.8
GRID_AXES = ("gx", "gy", "gz")
VMEM = pl.BlockSpec(memory_space=pltpu.VMEM)
F32 = jnp.float32


def harmonic(first, second):
    return 2.0 * first * second / (first + second)


def lanes(shape=(8, 128)):
    return lax.broadcasted_iota(jnp.int32, shape, len(shape) - 1)


def rows(shape):
    return lax.broadcasted_iota(jnp.int32, shape, 0)


def low_side(axis, turn):
    odd = lax.rem(lax.axis_index(axis), 2) == 1
    return ~odd if turn else odd


def regroup(refs, counts):
    out, at = [], 0
    for c in counts:
        out.append(refs[at : at + c])
        at += c
    return out, refs[at:]


def pack_columns(load, count):
    lane = lanes()
    firsts, lasts = [], []
    for start in range(0, count, 128):
        parts = [[], []]
        for chunk in range(start, min(start + 128, count), 16):
            sums = [None, None]
            for i in range(chunk, min(chunk + 16, count)):
                j = i - start
                turned = load(i)
                if j:
                    turned = pltpu.roll(turned, j, 1)
                turned = jnp.where((lane == j) | (lane == (j + 127) % 128), turned, 0.0)
                sums[j % 2] = turned if sums[j % 2] is None else sums[j % 2] + turned
            for kept, new in zip(parts, sums):
                if new is not None:
                    kept.append(new)
        odd = tree(parts[1]) if parts[1] else jnp.zeros((8, 128), F32)
        even = tree(parts[0])
        here = lane % 2 == 0
        firsts.append(jnp.where(here, even, odd))
        lasts.append(pltpu.roll(jnp.where(here, odd, even), 1, 1))
    return jnp.concatenate(firsts, 0), jnp.concatenate(lasts, 0)


def tree(values):
    while len(values) > 1:
        values = [a + b for a, b in zip(values[::2], values[1::2])] + values[len(values) // 2 * 2 :]
    return values[0]


def vreg_groups(z, per, size=8):
    places = []
    for i in range(z * per):
        tier, at = i // per, 8 * (i % per)
        places.append((i, (tier, slice(at, at + 8)), (tier, slice(at + 8, at + 16))))
    return [places[k : k + size] for k in range(0, len(places), size)]


def stage_columns(first, last):
    even = lanes() % 2 == 0
    out = []
    for g in range(first.shape[0] // 8):
        f = first[8 * g : 8 * g + 8]
        l = pltpu.roll(last[8 * g : 8 * g + 8], 127, 1)
        out.append((jnp.where(even, f, l), jnp.where(even, l, f)))
    return out


def spread_columns(staged, edge, i):
    turned = staged[i // 128][i % 2]
    if i % 128:
        turned = pltpu.roll(turned, 128 - i % 128, 1)
    return jnp.where(edge, turned, 0.0)


def edge_lanes():
    lane = lanes()
    return (lane == 0) | (lane == 127)


def column_halos(refs, slot=()):
    low = low_side("gx", 0)
    got = [ref[slot] if slot else ref[...] for ref in refs]
    if len(got) == 1:
        got.append(jnp.zeros_like(got[0]))
    return jnp.where(low, got[0], got[1]), jnp.where(low, got[1], got[0])


def fill_sends(tier, row, send_refs, slot, columns, z, y):
    for axis, refs in zip(GRID_AXES, send_refs):
        for n, ref in enumerate(refs):
            low = low_side(axis, n)
            if axis == "gx":
                value = jnp.where(low, columns[0], columns[1])
            elif axis == "gy":
                value = jnp.where(low, row(0), row(y - 1))
            else:
                value = tier(jnp.where(low, 0, z - 1))
            if slot is None:
                ref[...] = value
            else:
                ref[slot] = value


def padded_access(ref):
    y = ref.shape[1] - 16

    def tier(i):
        return ref[i, pl.ds(8, y), :]

    def row(r):
        return ref[:, 8 + r, :]

    def vreg(i):
        return ref[i // (y // 8), 8 + 8 * (i % (y // 8)) : 16 + 8 * (i % (y // 8)), :]

    return tier, row, vreg


def clear_margins(ref):
    z, y, _ = ref.shape
    for i in range(z):
        ref[i, 0:8, :] = jnp.zeros((8, 128), F32)
        ref[i, y - 8 : y, :] = jnp.zeros((8, 128), F32)


def start_all(sources, targets, sems):
    copies = [pltpu.make_async_copy(a, b, sems.at[n]) for n, (a, b) in enumerate(zip(sources, targets))]
    for copy in copies:
        copy.start()
    return copies


def faces_kernel(rounds, x_in, k_in, x_ref, k_ref, *refs):
    sends, (own_ref, sems) = regroup(refs, rounds)
    z, y, _ = x_in.shape
    per = y // 8
    fields = (x_ref, k_ref)
    copies = [
        start_all([source], [ref.at[:, pl.ds(8, y), :]], sems.at[n])
        for n, (source, ref) in enumerate(zip((x_in, k_in), fields))
    ]
    for slot, ref in enumerate(fields):
        clear_margins(ref)
        tier, row, vreg = padded_access(ref)

        def load(i):
            if i == 0:
                copies[slot][0].wait()
            return vreg(i)

        columns = pack_columns(load, z * per)
        own_ref[slot, 0] = columns[0]
        own_ref[slot, 1] = columns[1]
        fill_sends(tier, row, sends, slot, columns, z, y)


def inner_kernel(tall, x_ref, k_ref, c_ref, cat_ref, sel_in, band_in, flow_in, lev_in, *refs):
    r_ref, diag_ref, cz_ref, cs_ref, ce_ref, mask_ref, *tables, sems = refs
    sel_ref, band_ref, flow_ref, lev_ref = tables
    z, y, _ = c_ref.shape
    copies = start_all(
        (sel_in, band_in, flow_in, lev_in),
        tables,
        sems,
    )
    lane = lanes((tall, 128))
    row = rows((tall, 128))
    for i in range(z):
        cs_ref[i, 0:8, :] = jnp.zeros((8, 128), F32)

    def faces(t, carry):
        at = pl.multiple_of(t * tall, 8)
        last = jnp.where(t == y // tall - 1, tall - 1, tall)
        for i in range(z):
            here = k_ref[i, pl.ds(at + 8, tall), :]
            south = harmonic(here, k_ref[i, pl.ds(at + 9, tall), :])
            cs_ref[i, pl.ds(at + 8, tall), :] = jnp.where(row == last, 0.0, south)
            ce_ref[i, pl.ds(at, tall), :] = jnp.where(lane == 127, 0.0, harmonic(here, pltpu.roll(here, 127, 1)))
            if i + 1 < z:
                above = k_ref[i + 1, pl.ds(at + 8, tall), :]
                cz_ref[i, pl.ds(at, tall), :] = vertical_ratio * harmonic(here, above)
        return carry

    lax.fori_loop(0, y // tall, faces, 0)
    for copy in copies:
        copy.wait()

    tiles = y // tall
    for word in range(mask_ref.shape[1]):
        few, many = jnp.int32(0), jnp.int32(0)
        for number in range(16 * word, min(16 * word + 16, z * tiles)):
            level = lev_ref[number // tiles, 0, number % tiles]
            few = few + jnp.where(level == 2, 1 << (number - 16 * word), 0)
            many = many + jnp.where(level > 2, 1 << (number - 16 * word), 0)
        mask_ref[0, word] = jnp.full((8, 128), few.astype(F32))
        mask_ref[1, word] = jnp.full((8, 128), many.astype(F32))

    def rest(t, carry):
        at = pl.multiple_of(t * tall, 8)
        near = pl.ds(at, tall)
        mid = pl.ds(at + 8, tall)
        width = band_ref[0, t]
        band = jnp.where((row < width) | (row >= tall - width), band_sink, 0.0)
        for i in range(z):
            x = x_ref[i, mid, :]
            sink = coolant_film * flow_ref[i].astype(F32) + band
            cn = cs_ref[i, pl.ds(at + 7, tall), :]
            cs = cs_ref[i, mid, :]
            ce = ce_ref[i, near, :]
            cw = pltpu.roll(ce, 1, 1)
            r = cat_ref[sel_ref[i, 0, t]] - sink * x
            r = r + cn * (x_ref[i, pl.ds(at + 7, tall), :] - x) + cs * (x_ref[i, pl.ds(at + 9, tall), :] - x)
            r = r + ce * (pltpu.roll(x, 127, 1) - x) + cw * (pltpu.roll(x, 1, 1) - x)
            diag = c_ref[i, near, :] * (1.0 / interval_increment) + sink
            diag = diag + ((cn + cs) + (ce + cw))
            if i:
                cd = cz_ref[i - 1, near, :]
                diag = diag + cd
                r = r + cd * (x_ref[i - 1, mid, :] - x)
            if i + 1 < z:
                cu = cz_ref[i, near, :]
                diag = diag + cu
                r = r + cu * (x_ref[i + 1, mid, :] - x)
            diag_ref[i, near, :] = diag
            r_ref[i, near, :] = r
        return carry

    lax.fori_loop(0, y // tall, rest, 0)


def list_tiles(mask_ref, todo_ref, tiles):
    counts = []
    for kind in range(2):
        count = jnp.int32(0)
        for word in range(mask_ref.shape[1]):
            mask = jnp.max(mask_ref[kind, word]).astype(jnp.int32)
            for bit in range(min(16, tiles - 16 * word)):
                todo_ref[kind, count] = 16 * word + bit
                count = count + ((mask >> bit) & 1)
        counts.append(count)
    return counts


def sweeps(field_ref, diag_ref, cs_ref, ce_ref, todo_ref, counts, tall):
    z, y, _ = diag_ref.shape
    tiles = y // tall

    def run(count):
        def tile(n, carry):
            number = todo_ref[min(count, 2) - 1, n]
            i, t = lax.div(number, tiles), lax.rem(number, tiles)
            at = pl.multiple_of(t * tall, 8)
            mid = pl.ds(at + 8, tall)
            start = field_ref[i, mid, :]
            weight = damping / diag_ref[i, pl.ds(at, tall), :]
            first = rows((8, 128)) == 0
            final = rows((8, 128)) == 7
            north = cs_ref[i, pl.ds(at + 7, tall), :]
            north = jnp.concatenate([jnp.where(first, 0.0, north[:8]), north[8:]], 0)
            south = cs_ref[i, mid, :]
            south = jnp.concatenate([south[:-8], jnp.where(final, 0.0, south[-8:])], 0)
            east = ce_ref[i, pl.ds(at, tall), :]
            state = start
            for sweep in range(1, count + 1):
                if sweep == 1:
                    above, below = field_ref[i, pl.ds(at + 7, tall), :], field_ref[i, pl.ds(at + 9, tall), :]
                else:
                    above, below = pltpu.roll(state, 1, 0), pltpu.roll(state, tall - 1, 0)
                inner = (north * above + south * below) + (
                    east * pltpu.roll(state, 127, 1) + pltpu.roll(east * state, 1, 1)
                )
                state = ((1.0 - damping) * state + start) + weight * inner
            field_ref[i, mid, :] = state
            return carry

        lax.fori_loop(0, counts[min(count, 2) - 1], tile, 0)

    run(1)
    run(3)


def border_kernel(rounds, tall, *refs):
    (x_ref, k_ref, own_ref, r_in, diag_in, cs_ref, ce_ref, mask_ref), refs = refs[:8], refs[8:]
    (hx, hy, hz), refs = regroup(refs, rounds)
    (r_ref, diag_ref, u_ref, cx_ref, cy_ref, czh_ref), refs = refs[:6], refs[6:]
    sends, (todo_ref,) = regroup(refs, rounds)
    z, y, _ = r_ref.shape
    counts = list_tiles(mask_ref, todo_ref, z * (y // tall))
    for n, ref in enumerate(hz):
        p = jnp.where(low_side("gz", n), 0, z - 1)
        for at in range(0, y, tall):
            near, inside = slice(at, at + tall), slice(at + 8, at + 8 + tall)
            face = vertical_ratio * harmonic(k_ref[p, inside, :], ref[1, near, :])
            diag = diag_in[p, near, :] + face
            r = r_in[p, near, :] + face * (ref[0, near, :] - x_ref[p, inside, :])
            czh_ref[n, near, :] = face
            diag_in[p, near, :] = diag
            r_in[p, near, :] = r
    row8 = rows((8, 128))
    for n, ref in enumerate(hy):
        low = low_side("gy", n)
        at = pl.multiple_of(jnp.where(low, 0, y - 8), 8)
        mask = row8 == jnp.where(low, 0, 7)
        for i in range(z):
            there = pl.ds(at, 8)
            inside = pl.ds(at + 8, 8)
            face = harmonic(k_ref[i, inside, :], ref[1, i : i + 1, :])
            face = jnp.where(mask, face, 0.0)
            cy_ref[n, i : i + 1, :] = jnp.sum(face, axis=0, keepdims=True)
            diag_in[i, there, :] = diag_in[i, there, :] + face
            r_in[i, there, :] = r_in[i, there, :] + face * (ref[0, i : i + 1, :] - x_ref[i, inside, :])
    xlo, xhi = column_halos(hx, (0,))
    klo, khi = column_halos(hx, (1,))
    west = harmonic(own_ref[1, 0], klo)
    east = harmonic(own_ref[1, 1], khi)
    cx_ref[0] = west
    cx_ref[1] = east
    faces = stage_columns(west, east)
    flux = stage_columns(west * (xlo - own_ref[0, 0]), east * (xhi - own_ref[0, 1]))
    edge = edge_lanes()
    clear_margins(u_ref)
    per = y // 8
    for group in vreg_groups(z, per):
        diags = [diag_in[at] + spread_columns(faces, edge, i) for i, at, _ in group]
        values = [r_in[at] + spread_columns(flux, edge, i) for i, at, _ in group]
        for (_, at, inside), diag, r in zip(group, diags, values):
            diag_ref[at] = diag
            r_ref[at] = r
            u_ref[inside] = r * (damping / diag)
    sweeps(u_ref, diag_ref, cs_ref, ce_ref, todo_ref, counts, tall)
    tier, row, vreg = padded_access(u_ref)
    fill_sends(tier, row, sends, None, pack_columns(vreg, z * per), z, y)


def apply_inner(field_ref, diag_ref, cz_ref, cs_ref, ce_ref, i, at, tall):
    z = diag_ref.shape[0]
    near = pl.ds(at, tall)
    mid = pl.ds(at + 8, tall)
    v = field_ref[i, mid, :]
    ce = ce_ref[i, near, :]
    total = cs_ref[i, pl.ds(at + 7, tall), :] * field_ref[i, pl.ds(at + 7, tall), :]
    total = total + cs_ref[i, mid, :] * field_ref[i, pl.ds(at + 9, tall), :]
    total = total + (ce * pltpu.roll(v, 127, 1) + pltpu.roll(ce * v, 1, 1))
    if i:
        total = total + cz_ref[i - 1, near, :] * field_ref[i - 1, mid, :]
    if i + 1 < z:
        total = total + cz_ref[i, near, :] * field_ref[i + 1, mid, :]
    return v, diag_ref[i, near, :] * v - total


def apply_kernel(tall, u_ref, diag_ref, cz_ref, cs_ref, ce_ref, w_ref):
    z, y, _ = diag_ref.shape

    def step(t, carry):
        at = pl.multiple_of(t * tall, 8)
        for i in range(z):
            w_ref[i, pl.ds(at, tall), :] = apply_inner(u_ref, diag_ref, cz_ref, cs_ref, ce_ref, i, at, tall)[1]
        return carry

    lax.fori_loop(0, y // tall, step, 0)


def subtract_tiers(w_ref, halos, czh_ref):
    for n, ref in enumerate(halos):
        p = jnp.where(low_side("gz", n), 0, w_ref.shape[0] - 1)
        w_ref[p] = w_ref[p] - czh_ref[n] * ref[...]


def border_rows(n, y):
    low = low_side("gy", n)
    at = pl.ds(pl.multiple_of(jnp.where(low, 0, y - 8), 8), 8)
    return at, rows((8, 128)) == jnp.where(low, 0, 7)


def smooth_kernel(rounds, tall, *refs):
    (w_in, diag_ref, cs_ref, ce_ref, cx_ref, cy_ref, czh_ref, mask_ref), refs = refs[:8], refs[8:]
    halos, refs = regroup(refs, rounds)
    w_ref, m_ref, face_ref, *send_refs, todo_ref = refs
    z, y, _ = w_ref.shape
    counts = list_tiles(mask_ref, todo_ref, z * (y // tall))
    subtract_tiers(w_in, halos[2], czh_ref)
    for n, ref in enumerate(halos[1]):
        at, mask = border_rows(n, y)
        for i in range(z):
            w_in[i, at, :] = w_in[i, at, :] - jnp.where(mask, cy_ref[n, i : i + 1, :] * ref[i : i + 1, :], 0.0)
    xlo, xhi = column_halos(halos[0])
    flux = stage_columns(cx_ref[0] * xlo, cx_ref[1] * xhi)
    edge = edge_lanes()
    clear_margins(m_ref)
    per = y // 8
    for group in vreg_groups(z, per):
        values = [w_in[at] - spread_columns(flux, edge, i) for i, at, _ in group]
        weights = [damping / diag_ref[at] for _, at, _ in group]
        for (_, at, inside), w, weight in zip(group, values, weights):
            w_ref[at] = w
            m_ref[inside] = w * weight
    sweeps(m_ref, diag_ref, cs_ref, ce_ref, todo_ref, counts, tall)
    tier, row, vreg = padded_access(m_ref)
    for n, ref in enumerate(send_refs):
        ref[...] = tier(jnp.where(low_side("gz", n), 0, z - 1))
    first, last = pack_columns(vreg, z * per)
    plan, _ = face_plan(z, first.shape[0], rounds)
    low = low_side("gy", 0)
    if rounds[1] == 1:
        face_ref[plan["y_low"]] = jnp.where(low, cy_ref[0] * row(0), row(y - 1))
    else:
        face_ref[plan["y_low"]] = jnp.where(low, cy_ref[0], cy_ref[1]) * row(0)
        face_ref[plan["y_high"]] = row(y - 1)
    face_ref[plan["x_low"]] = cx_ref[0] * first
    face_ref[plan["x_high"]] = last
    face_ref[plan["sums"]] = jnp.zeros((4, 128), F32)


def face_plan(z, packed, rounds):
    plan, at = {}, 0
    parts = (("sums", 4), ("y_low", z), ("x_low", packed), ("x_high", packed), ("y_high", z))
    for name, count in parts[: 4 if rounds[1] == 1 else 5]:
        plan[name] = slice(at, at + count)
        at += count
    return plan, at


def fold(product):
    return jnp.sum(product.reshape(-1, 8, 128), axis=0)


def sums_kernel(tall, m_ref, u_ref, r_ref, w_ref, diag_ref, cz_ref, cs_ref, ce_ref, n_ref, sum_ref):
    z, y, _ = diag_ref.shape

    def step(t, carry):
        gamma, delta, cross, last = carry
        at = pl.multiple_of(t * tall, 8)
        near = pl.ds(at, tall)
        for i in range(z):
            m, n = apply_inner(m_ref, diag_ref, cz_ref, cs_ref, ce_ref, i, at, tall)
            n_ref[i, near, :] = n
            u = u_ref[i, pl.ds(at + 8, tall), :]
            w = w_ref[i, near, :]
            gamma = gamma + fold(r_ref[i, near, :] * u)
            delta = delta + fold(w * u)
            cross = cross + fold(w * m)
            last = last + fold(n * m)
        return gamma, delta, cross, last

    zero = jnp.zeros((8, 128), F32)
    for n, value in enumerate(lax.fori_loop(0, y // tall, step, (zero,) * 4)):
        sum_ref[n] = value


def finish_kernel(rounds, *refs):
    (n_in, m_ref, sum_ref, czh_ref, face_ref), refs = refs[:5], refs[5:]
    (halos,), (n_ref, out_ref) = regroup(refs, rounds[2:])
    z, y, _ = n_ref.shape
    last = sum_ref[3]
    for n, ref in enumerate(halos):
        p = jnp.where(low_side("gz", n), 0, z - 1)
        flux = czh_ref[n] * ref[...]
        n_ref[p] = n_in[p] - flux
        last = last - fold(flux * m_ref[p, pl.ds(8, y), :])
    parts = [sum_ref[0], sum_ref[1], sum_ref[2], last]
    parts = [jnp.sum(p, axis=0, keepdims=True) for p in parts]
    height = face_ref.shape[0]
    everything = jnp.concatenate(parts + [face_ref[4:height]], 0)
    for d in range(out_ref.shape[0]):
        out_ref[d] = everything


def update_kernel(rounds, sizes, *refs):
    all_ref, x_ref, r_ref, u_ref, w_ref, m_ref, n_ref, cx_ref, cy_ref, x_out, r_out, xo_ref, ro_ref, sems = refs
    z, y, _ = r_ref.shape
    packed = cx_ref.shape[1]
    plan, _ = face_plan(z, packed, rounds)
    nx, ny, nz = sizes
    members = nx * ny * nz
    y_high = plan["y_low" if rounds[1] == 1 else "y_high"]

    sums = tree([all_ref[d, plan["sums"], :] for d in range(members)])
    gamma, delta, cross, last = (sums[i : i + 1] for i in range(4))
    links = []
    for d in range(members - ny * nz):
        links.append(all_ref[d, plan["x_high"], :] * all_ref[d + ny * nz, plan["x_low"], :])
    if links:
        last = last - 2.0 * jnp.sum(tree(links), axis=0, keepdims=True)
    links = []
    for d in range(members - nz):
        if d // nz % ny + 1 < ny:
            links.append(all_ref[d, y_high, :] * all_ref[d + nz, plan["y_low"], :])
    if links:
        last = last - 2.0 * jnp.sum(tree(links), axis=0, keepdims=True)

    def total(v):
        return jnp.sum(v, axis=1, keepdims=True)

    gamma0 = total(gamma)
    alpha0 = gamma0 / total(delta)
    gamma1 = total(gamma - 2.0 * alpha0 * delta + alpha0 * alpha0 * cross)
    delta1 = total(delta - 2.0 * alpha0 * cross + alpha0 * alpha0 * last)
    beta = gamma1 / gamma0
    alpha1 = gamma1 / (delta1 - beta * gamma1 / alpha0)
    near = alpha0 + alpha1 * (1.0 + beta)
    far = alpha1 * alpha0

    gx, gy, gz = (lax.axis_index(axis) for axis in GRID_AXES)
    me = (gx * ny + gy) * nz + gz
    left = jnp.maximum(me - ny * nz, 0)
    right = jnp.minimum(me + ny * nz, members - 1)
    has_right = gx < nx - 1
    west = far * (cx_ref[0] * all_ref[left, plan["x_high"], :])
    east = far * jnp.where(has_right, all_ref[right, plan["x_low"], :], 0.0)
    flux = stage_columns(west, east)
    below = jnp.maximum(me - nz, 0)
    above = jnp.minimum(me + nz, members - 1)
    row_flux = []
    for n in range(rounds[1]):
        low = low_side("gy", n)
        from_below = cy_ref[n] * all_ref[below, y_high, :]
        from_above = jnp.where(gy < ny - 1, all_ref[above, plan["y_low"], :], 0.0)
        row_flux.append(far * jnp.where(low, from_below, from_above))
    edge = edge_lanes()
    near, far = (jnp.broadcast_to(v, (8, 128)) for v in (near, far))
    per = y // 8
    copies = []
    batches = vreg_groups(z, per)
    for i in range(z):
        for group in batches[i * len(batches) // z : (i + 1) * len(batches) // z]:
            values = [
                r_ref[at] - near * w_ref[at] + (far * n_ref[at] - spread_columns(flux, edge, j)) for j, at, _ in group
            ]
            fields = [x_ref[inside] + near * u_ref[inside] - far * m_ref[inside] for _, _, inside in group]
            for (_, at, _), value, field in zip(group, values, fields):
                ro_ref[at] = value
                xo_ref[at] = field
        for n in range(rounds[1]):
            at, mask = border_rows(n, y)
            ro_ref[i, at, :] = ro_ref[i, at, :] - jnp.where(mask, row_flux[n][i : i + 1], 0.0)
        copies += start_all((ro_ref.at[i], xo_ref.at[i]), (r_out.at[i], x_out.at[i]), sems.at[i])
    for copy in copies:
        copy.wait()


def swap_pairs(axis, start):
    count = lax.axis_size(axis)
    pairs = []
    for i in range(start, count - 1, 2):
        pairs += [(i, i + 1), (i + 1, i)]
    return pairs


def body(
    earlier_warmth_field,
    caloric_storage,
    thermal_diffusivity_coefficient,
    dissipation_catalog,
    dissipation_selector,
    refine_depth,
    border_band_width,
    microflow_flag,
):
    z, y, x = earlier_warmth_field.shape
    tall = dissipation_catalog.shape[1]
    groups = -(-(z * y // 8) // 128)
    rounds = tuple(2 if lax.axis_size(axis) > 2 else 1 for axis in GRID_AXES)
    sends = sum(rounds)
    shape = lambda *s: pltpu.VMEM(s, F32)
    full = shape(z, y, x)
    tall_field = shape(z, y + 16, x)
    _, height = face_plan(z, 8 * groups, rounds)

    hbm = pl.BlockSpec(memory_space=pltpu.HBM)

    def call(kernel, outs, ins, name, scratch=(), out_specs=None, alias=None, outer=()):
        specs = [hbm if n in outer else VMEM for n in range(len(ins))]
        ins = [pltpu.with_memory_space_constraint(v, pltpu.HBM) if n in outer else v for n, v in enumerate(ins)]
        return pl.pallas_call(
            kernel,
            out_shape=outs,
            in_specs=specs,
            out_specs=out_specs or [VMEM] * len(outs),
            scratch_shapes=list(scratch),
            input_output_aliases=alias or {},
            name=name,
            compiler_params=pltpu.CompilerParams(vmem_limit_bytes=16 * 2**20),
        )(*ins)

    def face_shapes(front):
        out = []
        for axis, n in zip(((8 * groups, x), (z, x), (y, x)), rounds):
            out += [shape(*front, *axis)] * n
        return out

    def swap(faces, axes=GRID_AXES):
        faces, got = list(faces), []
        for axis in axes:
            for start in range(rounds[GRID_AXES.index(axis)]):
                got.append(lax.ppermute(faces.pop(0), axis, swap_pairs(axis, start)))
        return got

    selector = jnp.swapaxes(dissipation_selector, 1, 2)
    levels = jnp.swapaxes(refine_depth, 1, 2)
    width = jnp.swapaxes(border_band_width, 0, 1)

    todo = pltpu.SMEM((2, z * (y // tall) + 1), jnp.int32)

    def table(v):
        return pltpu.SMEM(v.shape, v.dtype)

    outs = call(
        functools.partial(faces_kernel, rounds),
        [tall_field, tall_field] + face_shapes((2,)) + [shape(2, 2, 8 * groups, x)],
        [earlier_warmth_field, thermal_diffusivity_coefficient],
        "faces",
        [pltpu.SemaphoreType.DMA((2, z))],
        outer=(0, 1),
    )
    (field, kappa), outs = outs[:2], outs[2:]
    own, halos = outs[sends], swap(outs[:sends])
    r, diag, cz, cs, ce, masks = call(
        functools.partial(inner_kernel, tall),
        [full, full, shape(max(z - 1, 1), y, x), shape(z, y + 8, x), full, shape(2, -(-z * (y // tall) // 16), 8, 128)],
        [field, kappa, caloric_storage, dissipation_catalog, selector, width, microflow_flag, levels],
        "inner",
        [
            table(selector),
            table(width),
            table(microflow_flag),
            table(levels),
            pltpu.SemaphoreType.DMA((4,)),
        ],
        outer=(4, 5, 6, 7),
    )
    outs = call(
        functools.partial(border_kernel, rounds, tall),
        [full, full, tall_field, shape(2, 8 * groups, x), shape(rounds[1], z, x), shape(rounds[2], y, x)]
        + face_shapes(()),
        [field, kappa, own, r, diag, cs, ce, masks] + halos,
        "border",
        [todo],
        alias={3: 0, 4: 1},
    )
    r, diag, u, cx, cy, czh = outs[:6]
    halos = swap(outs[6:])
    (w,) = call(functools.partial(apply_kernel, tall), [full], [u, diag, cz, cs, ce], "apply")
    outs = call(
        functools.partial(smooth_kernel, rounds, tall),
        [full, tall_field, shape(height, x)] + [shape(y, x)] * rounds[2],
        [w, diag, cs, ce, cx, cy, czh, masks] + halos,
        "smooth",
        [todo],
        alias={0: 0},
    )
    w, m, faces = outs[:3]
    halos = swap(outs[3:], GRID_AXES[2:])
    n, sums = call(
        functools.partial(sums_kernel, tall), [full, shape(4, 8, 128)], [m, u, r, w, diag, cz, cs, ce], "sums"
    )
    sizes = tuple(lax.axis_size(axis) for axis in GRID_AXES)
    n, parts = call(
        functools.partial(finish_kernel, rounds),
        [full, shape(math.prod(sizes), height, x)],
        [n, m, sums, czh, faces] + halos,
        "finish",
        alias={0: 0},
    )
    every = lax.all_to_all(parts, GRID_AXES, 0, 0, tiled=True)
    return tuple(
        call(
            functools.partial(update_kernel, rounds, sizes),
            [jax.ShapeDtypeStruct((z, y, x), F32)] * 2,
            [every, field, r, u, w, m, n, cx, cy],
            "update",
            [full, full, pltpu.SemaphoreType.DMA((z, 2))],
            out_specs=[hbm, hbm],
        )
    )


def solution(mesh):
    cells = P(("groups", "gz"), "gy", "gx")
    return jax.shard_map(
        body,
        mesh=mesh,
        in_specs=(
            cells,
            cells,
            cells,
            P("groups", None, None),
            cells,
            cells,
            P(("groups", "gy"), "gx"),
            P(("groups", "gz")),
        ),
        out_specs=(cells, cells),
        check_vma=False,
    )
```
